32 devices in a mesh: tile: 16 (over z, y, core), samp: 2 (over x).
Axes of the slice: x: 2, y: 2, z: 4, core: 2. Of those that a mesh axis runs over, the one named last changes fastest.
Arguments:
- bathymetry: float32 [6, 512, 512], P(None, 'tile'), may hold values from 0.5 to 2
- initial_state: float32 [16, 6, 512, 512], P(None, None, 'tile'), may hold values from -6 to 6
- patterns: bfloat16 [4, 6, 512, 512], P(None, None, 'tile'), may hold values from -6 to 6
- pattern_index: int32 [2, 16], P('samp'), may hold values from 0 to 3
- coupling: float32 [16, 16], replicated, may hold values from -1.5 to 1.5
- final_weights: float32 [2, 16, 6, 512, 512], P('samp', None, None, 'tile'), may hold values from -6 to 6
Outputs:
- gradient: float32 [6, 512, 512], P(None, 'tile')
The draws below stay inside these ranges and needn't reach their ends.
All inputs are finite; a program needn't handle non-finite values.
Results may differ from the reference program's by a relative error of at most 0.0003.
Values sent between devices are 32-bit elements; how exact they have to be, the bound alone decides.
No kernel may reach another device: no remote copies, remote signals or barrier semaphores. Data moves between devices by JAX's collectives and lax.ppermute only.
A program may use at most 128 MiB of HBM per device.

```python
import math
import jax
import jax.numpy as jnp
from jax import lax

N = 512
LAYERS = 16
PATTERNS = 4
SAMPLES = 2


def set_ends(values, key, least, largest):
    place = [jax.random.randint(jax.random.fold_in(key, axis), (), 0, length) for axis, length in enumerate(values.shape)]
    main_axis = values.shape.index(max(values.shape))
    beside = place[:main_axis] + [(place[main_axis] + 1) % values.shape[main_axis]] + place[main_axis + 1:]
    return values.at[tuple(place)].set(least).at[tuple(beside)].set(largest)


def levels(stream_key, dims, cuts, low, top_value):
    level, own = 1.0, jax.random.fold_in(stream_key, 6)
    for axis_at, parts in cuts:
        heights = jnp.exp(jax.random.uniform(jax.random.fold_in(own, axis_at), (parts,), jnp.float32, low / len(cuts), top_value / len(cuts)))
        level = level * jnp.repeat(heights, dims[axis_at] // parts).reshape([-1 if axis == axis_at else 1 for axis in range(len(dims))])
    return level


def normal_values(own_key, shape, width, reach, shards=(), kind=jnp.bfloat16):
    entries = width * jax.random.normal(own_key, shape, jnp.float32)
    if shards:
        entries = entries * levels(own_key, shape, shards, -0.22, 0.18)
    return jnp.clip(entries, -reach, reach).astype(kind)


def setup_inputs(seed: int = 0) -> dict:
    key_of = jax.random.split(jax.random.key(seed), 7)
    bathymetry = jnp.clip(jnp.exp(math.log(2.0) - 1.3862944 * jax.random.uniform(key_of[0], (6, N, N), jnp.float32) ** levels(key_of[0], (6, N, N), ((1, 16),), -0.2, 0.2)), 0.5, 2.0)
    initial_state = normal_values(key_of[1], (LAYERS, 6, N, N), 1.0, 6.0, ((2, 16),), jnp.float32)
    patterns = normal_values(key_of[2], (PATTERNS, 6, N, N), 1.0, 6.0, ((2, 16),))
    pattern_index = set_ends(jax.random.randint(key_of[3], (SAMPLES, LAYERS), 0, PATTERNS), jax.random.fold_in(key_of[3], 1), 0, PATTERNS - 1).astype(jnp.int32)
    coupling = normal_values(key_of[4], (LAYERS, LAYERS), LAYERS ** -0.5, 1.5, (), jnp.float32)
    final_weights = normal_values(key_of[5], (SAMPLES, LAYERS, 6, N, N), 1.0, 6.0, ((0, 2), (3, 16)), jnp.float32)
    return dict(bathymetry=bathymetry, initial_state=initial_state, patterns=patterns, pattern_index=pattern_index, coupling=coupling, final_weights=final_weights)


STEP_FACTOR = 0.1

def pad_cube(field):
    cells = field.shape[-1]
    last = cells - 1
    padded = jnp.zeros(field.shape[:-3] + (6, cells + 2, cells + 2), field.dtype)
    padded = padded.at[..., 1:-1, 1:-1].set(field)
    western = jnp.stack([field[..., 3, last, :], field[..., 0, last, :], field[..., 1, last, :], field[..., 2, last, :], field[..., 3, ::-1, last], field[..., 3, :, 0]], axis=-2)
    eastern = jnp.stack([field[..., 1, 0, :], field[..., 2, 0, :], field[..., 3, 0, :], field[..., 0, 0, :], field[..., 1, :, last], field[..., 1, ::-1, 0]], axis=-2)
    southern = jnp.stack([field[..., 5, :, last], field[..., 5, last, ::-1], field[..., 5, ::-1, 0], field[..., 5, 0, :], field[..., 0, :, last], field[..., 2, ::-1, 0]], axis=-2)
    northern = jnp.stack([field[..., 4, :, 0], field[..., 4, last, :], field[..., 4, ::-1, last], field[..., 4, 0, ::-1], field[..., 2, ::-1, last], field[..., 0, :, 0]], axis=-2)
    padded = padded.at[..., :, 0, 1:-1].set(western)
    padded = padded.at[..., :, -1, 1:-1].set(eastern)
    padded = padded.at[..., :, 1:-1, 0].set(southern)
    padded = padded.at[..., :, 1:-1, -1].set(northern)
    return padded

def stencil(padded, depth_pad):
    rows_i = padded.shape[-2] - 2
    rows_j = padded.shape[-1] - 2
    centre = padded[..., 1:1 + rows_i, 1:1 + rows_j]
    depth_here = depth_pad[..., 1:1 + rows_i, 1:1 + rows_j]
    summed = jnp.zeros_like(centre)
    for shift_i, shift_j in ((1, 0), (-1, 0), (0, 1), (0, -1)):
        beside_value = padded[..., 1 + shift_i:1 + shift_i + rows_i, 1 + shift_j:1 + shift_j + rows_j]
        depth_near = depth_pad[..., 1 + shift_i:1 + shift_i + rows_i, 1 + shift_j:1 + shift_j + rows_j]
        summed = summed + 0.5 * (depth_here + depth_near) * (beside_value - centre)
    return summed

def mix_layers(matrix, state):
    return jnp.einsum('km,mpij->kpij', matrix, state, precision=lax.Precision.HIGHEST)

def reference(bathymetry, initial_state, patterns, pattern_index, coupling, final_weights):
    mixing = jnp.eye(LAYERS, dtype=coupling.dtype) + coupling

    def sample_loss(bathy, forcing, cotangent):
        depth_pad = pad_cube(bathy)
        mixed_zero = mix_layers(mixing, initial_state)
        state_one = initial_state + STEP_FACTOR * (stencil(pad_cube(mixed_zero), depth_pad) + forcing)
        mixed_one = mix_layers(mixing, state_one)
        state_two = 2.0 * state_one - initial_state + STEP_FACTOR * (stencil(pad_cube(mixed_one), depth_pad) + forcing)
        return jnp.sum(cotangent * state_two)

    def one_sample(summed, sample):
        forcing = patterns[pattern_index[sample]].astype(initial_state.dtype)
        gradient = jax.grad(sample_loss)(bathymetry, forcing, final_weights[sample])
        return (summed + gradient, None)
    summed, _ = lax.scan(one_sample, jnp.zeros_like(bathymetry), jnp.arange(SAMPLES, dtype=jnp.int32))
    return summed / SAMPLES
```

```python
import functools

import jax
import jax.numpy as jnp
from jax import lax
from jax.experimental import pallas as pl
from jax.experimental.pallas import tpu as pltpu
from jax.sharding import PartitionSpec as P

STEP_FACTOR = 0.1
LANES = 128
CH = 40
F32 = jnp.float32


def lane_iota(shape):
    return lax.broadcasted_iota(jnp.int32, shape, len(shape) - 1)


def lane_gather(x, idx):
    return jnp.take_along_axis(x, idx, axis=1, mode="promise_in_bounds")


def mix(cat, x):
    hi = x.astype(jnp.bfloat16)
    lo = (x - hi.astype(F32)).astype(jnp.bfloat16)
    return jnp.dot(cat, jnp.concatenate([hi, hi, lo], axis=0), preferred_element_type=F32)


STRIDED = True


def layer_rows(ref, r):
    size, rows = ref.shape[0], ref.shape[2]
    if not STRIDED:
        return ref[:, 0, r, :]
    return ref.reshape(size * rows, LANES)[pl.ds(r, size, stride=rows), :]


def pack_kernel(tiles, s_ref, w_ref, pat_ref, b_ref, em_ref, lo_ref, hi_ref, mm_ref, aa_ref, aux):
    layers, rows = s_ref.shape[0], s_ref.shape[2]
    p, block, blocks = pl.program_id(0), pl.program_id(1), pl.num_programs(1)
    place = lax.axis_index("tile")
    first, final = place == 0, place == tiles - 1
    npat = pat_ref.shape[0]
    aux[...] = jnp.zeros(aux.shape, F32)
    aux[0:npat, 0] = pat_ref[:, 0].astype(F32)
    aux[npat, 0] = b_ref[0]
    groups = ((0, layers, s_ref), (layers, layers, w_ref), (2 * layers, 8, aux))

    for at, size, ref in groups:
        for c in range(2):
            lo_ref[0, c, at : at + size, :] = layer_rows(ref, c)
            hi_ref[0, c, at : at + size, :] = layer_rows(ref, rows - 2 + c)

    lane = lane_iota((CH, LANES))
    side = lane % 4

    @pl.when((p == 0) & (block == 0))
    def _():
        aa_ref[...] = jnp.zeros(aa_ref.shape, F32)

    @pl.when(block == 0)
    def _():
        em_ref[...] = jnp.zeros(em_ref.shape, F32)

    for mine, at_block in (((0, 1), blocks - 1), ((2, 3), 0)):
        @pl.when(block == at_block)
        def _(mine=mine):
            for at, size, ref in groups:
                ln = lane_iota((size, LANES))
                keep = (ln % 4 == mine[0]) | (ln % 4 == mine[1])
                out = jnp.zeros((size, LANES), F32)
                for r in range(rows):
                    turned = pltpu.roll(layer_rows(ref, r), (4 * r - 126) % LANES, 1)
                    out = jnp.where(ln // 4 == r, turned, out)
                em_ref[0, at : at + size, :] = jnp.where(keep, out, em_ref[0, at : at + size, :])

    @pl.when(block == blocks - 1)
    def _():
        @pl.when(p == 1)
        def _():
            aa_ref[tiles - 1, 0:CH, :] = em_ref[0]
            mm_ref[2] = em_ref[0]

        @pl.when(p == 2)
        def _():
            mm_ref[0] = em_ref[0]

        @pl.when(p == 3)
        def _():
            aa_ref[0, 0:CH, :] = em_ref[0]

        @pl.when((p == 3) & jnp.logical_not(first))
        def _():
            mm_ref[2] = em_ref[0]

        @pl.when(p == 4)
        def _():
            mm_ref[1] = em_ref[0]

        @pl.when(p == 5)
        def _():
            mm_ref[1] = jnp.where(side < 2, mm_ref[1], em_ref[0])

    per = LANES // rows

    def pole(ref, near, far, backward, is_five):
        x, y = ref[0, near], ref[0, far]
        turned = jnp.concatenate([x, jnp.zeros((LANES - CH, LANES), F32)], axis=0).T
        for q in range(per):
            if backward:
                t = (blocks - 1 - block) * per + q
                idx = LANES - 1 - q * rows - lane // 4
            else:
                t = block * per + q
                idx = q * rows + lane // 4
            idx = jnp.clip(idx, 0, LANES - 1)
            a, b = lane_gather(x, idx), lane_gather(y, idx)
            if is_five:
                aa_ref[t, 0:CH, :] = jnp.where(side == 1, a, jnp.where(side == 0, b, aa_ref[t, 0:CH, :]))
            else:
                aa_ref[t, 0:CH, :] = jnp.where(side == 2, a, b)
            low, high = q * rows, (q + 1) * rows - 1
            if backward:
                before, at_before = tiles - block * per - q, low
                after, at_after = tiles - 1 - block * per - (q + 1), high
            else:
                before, at_before = block * per + q + 1, high
                after, at_after = block * per + q - 1, low
            m = 0 if is_five else 1

            @pl.when(before < tiles)
            def _(before=before, at=at_before):
                aa_ref[before, CH + m : CH + m + 1, :] = turned[at : at + 1, :]

            @pl.when(after >= 0)
            def _(after=after, at=at_after):
                aa_ref[after, CH + m + 2 : CH + m + 3, :] = turned[at : at + 1, :]

    for panel in (4, 5):
        @pl.when((p == panel) & first)
        def _(panel=panel):
            pole(lo_ref, 0, 1, panel == 4, panel == 5)

        @pl.when((p == panel) & final)
        def _(panel=panel):
            pole(hi_ref, 1, 0, panel == 5, panel == 5)


def pack(tiles, s, w, pat, b):
    layers, panels, rows, n = s.shape
    npat = pat.shape[0]
    full = lambda *shape: pl.BlockSpec(shape, lambda p, c: (0,) * len(shape))
    part = lambda size: pl.BlockSpec((size, 1, rows, LANES), lambda p, c: (0, p, 0, c))
    line = pl.BlockSpec((1, 2, CH, LANES), lambda p, c: (p, 0, 0, c))
    return pl.pallas_call(
        functools.partial(pack_kernel, tiles),
        grid=(panels, n // LANES),
        in_specs=[part(layers), part(layers), part(npat), pl.BlockSpec((1, rows, LANES), lambda p, c: (p, 0, c))],
        out_specs=[
            pl.BlockSpec((1, CH, LANES), lambda p, c: (p, 0, 0)),
            line,
            line,
            full(3, CH, LANES),
            full(tiles, CH + 8, LANES),
        ],
        out_shape=[
            jax.ShapeDtypeStruct((panels, CH, LANES), F32),
            jax.ShapeDtypeStruct((panels, 2, CH, n), F32),
            jax.ShapeDtypeStruct((panels, 2, CH, n), F32),
            jax.ShapeDtypeStruct((3, CH, LANES), F32),
            jax.ShapeDtypeStruct((tiles, CH + 8, LANES), F32),
        ],
        scratch_shapes=[pltpu.VMEM((8, 1, rows, LANES), F32)],
        compiler_params=pltpu.CompilerParams(vmem_limit_bytes=48 * 1024 * 1024),
        name="pack",
    )(s, w, pat, b)


def mix_kernel(s_ref, w_ref, pat_ref, fwd_ref, bwd_ref, sel_ref, p_ref, v_ref, y_ref, pf):
    rows = s_ref.shape[2]
    npat = pat_ref.shape[0]
    pf[...] = jnp.zeros(pf.shape, F32)
    pf[0:npat, 0] = pat_ref[:, 0].astype(F32)
    fwd, bwd, sel = fwd_ref[...], bwd_ref[...], sel_ref[...]
    for r in range(rows):
        s = layer_rows(s_ref, r)
        p_ref[0, r] = mix(fwd, s)
        v_ref[0, r] = mix(bwd, layer_rows(w_ref, r))
        f = jnp.dot(sel, layer_rows(pf, r).astype(jnp.bfloat16), preferred_element_type=F32)
        y_ref[0, r] = 3.0 * s + STEP_FACTOR * f


def mix_all(s, w, pat, fwd, bwd, sel):
    layers, panels, rows, n = s.shape
    npat = pat.shape[0]
    full = lambda x: pl.BlockSpec(x.shape, lambda p, c: (0,) * x.ndim)
    part = lambda size: pl.BlockSpec((size, 1, rows, LANES), lambda p, c: (0, p, 0, c))
    out = pl.BlockSpec((1, rows, layers, LANES), lambda p, c: (p, 0, 0, c))
    size = layers * panels * rows * n * 4
    return pl.pallas_call(
        mix_kernel,
        grid=(panels, n // LANES),
        in_specs=[part(layers), part(layers), part(npat), full(fwd), full(bwd), full(sel)],
        out_specs=[out] * 3,
        out_shape=[jax.ShapeDtypeStruct((panels, rows, layers, n), F32)] * 3,
        scratch_shapes=[pltpu.VMEM((8, 1, rows, LANES), F32)],
        compiler_params=pltpu.CompilerParams(vmem_limit_bytes=48 * 1024 * 1024),
        cost_estimate=pl.CostEstimate(flops=size * 48, bytes_accessed=5 * size, transcendentals=0),
        name="mix",
    )(s, w, pat, fwd, bwd, sel)


def halo_kernel(
    tiles, layers, rows,
    west_ref, east_ref, em_ref, mm_ref, mu_ref, md_ref, aa_ref, fwd_ref, bwd_ref, sel_ref,
    hrp_ref, hrv_ref, hry_ref, hrb_ref, hlp_ref, hlv_ref, hly_ref, hlb_ref, hcp_ref, hcv_ref, hcb_ref,
    line,
):
    panels, n = west_ref.shape[0], west_ref.shape[3]
    place = lax.axis_index("tile")
    first, final = place == 0, place == tiles - 1
    fwd, bwd, sel = fwd_ref[...], bwd_ref[...], sel_ref[...]
    lane = lane_iota((CH, LANES))
    side = lane % 4
    blocks = n // LANES
    per = LANES // rows

    for p in range(panels):
        @pl.when(jnp.logical_not(first))
        def _(p=p):
            line[p, 0:2] = west_ref[p]

        @pl.when(jnp.logical_not(final))
        def _(p=p):
            line[p, 2:4] = east_ref[p]

        if p < 4:
            @pl.when(first)
            def _(p=p):
                line[p, 0:2] = west_ref[(p + 3) % 4]

            @pl.when(final)
            def _(p=p):
                line[p, 2:4] = east_ref[(p + 1) % 4]

    def collect(u_of, dest, k, backward):
        within = lane % rows
        idx = 4 * (rows - 1 - within) + k if backward else 4 * within + k
        p, at = dest
        for block in range(blocks):
            out = jnp.zeros((CH, LANES), F32)
            for q in range(per):
                u = block * per + q
                u = tiles - 1 - u if backward else u
                out = jnp.where(lane // rows == q, lane_gather(u_of(u), idx), out)
            line[p, at, :, block * LANES : (block + 1) * LANES] = out

    @pl.when(first)
    def _():
        def of(u):
            return em_ref[3] if u == 0 else mm_ref[2] if u == tiles - 1 else aa_ref[u, 0:CH, :]

        collect(of, (4, 1), 1, True)
        collect(of, (4, 0), 0, True)
        collect(of, (5, 1), 2, False)
        collect(of, (5, 0), 3, False)

    @pl.when(final)
    def _():
        def of(u):
            return mm_ref[2] if u == 0 else em_ref[1] if u == tiles - 1 else aa_ref[u, 0:CH, :]

        collect(of, (4, 2), 1, False)
        collect(of, (4, 3), 0, False)
        collect(of, (5, 2), 2, True)
        collect(of, (5, 3), 3, True)

    def force(x):
        return 3.0 * x[0:layers] + STEP_FACTOR * jnp.dot(
            sel, x[2 * layers : CH].astype(jnp.bfloat16), preferred_element_type=F32
        )

    for p in range(panels):
        for k in range(4):
            x = line[p, k]
            hrp_ref[p, k] = mix(fwd, x[0:layers])
            hrv_ref[p, k] = mix(bwd, x[layers : 2 * layers])
            hrb_ref[p, k : k + 1, :] = line[p, k, CH - 4 : CH - 3, :]
            if k in (1, 2):
                hry_ref[p, k - 1] = force(x)

    span = 4 * rows
    turn = jnp.where(lane < span, span - 1 - lane, 0)
    back0 = lane_gather(mm_ref[0], turn)
    back1 = lane_gather(mm_ref[1], turn)
    columns = (
        jnp.where(side < 2, em_ref[5], em_ref[4]),
        aa_ref[tiles - 1, 0:CH, :],
        back1,
        aa_ref[0, 0:CH, :],
        jnp.where(side < 2, em_ref[0], back0),
        jnp.where(side < 2, back0, em_ref[0]),
    )
    at_end = lane == LANES - 1
    pad = jnp.zeros((LANES - 8, LANES), F32)
    for p in range(panels):
        x = columns[p]
        hlp_ref[p] = mix(fwd, x[0:layers])
        hlv_ref[p] = mix(bwd, x[layers : 2 * layers])
        hly_ref[p] = force(x)
        depth = x[CH - 4 : CH - 3]
        hlb_ref[p] = jnp.broadcast_to(depth, (8, LANES))
        if p in (1, 3):
            turned = jnp.concatenate([aa_ref[tiles - 1 if p == 1 else 0, CH:, :], pad], axis=0).T[0:CH]
        for edge in range(2):
            at = 1 + edge
            at_cut = lambda q, block: line[q, at, :, block * LANES : (block + 1) * LANES]
            cells = (1, 2) if edge == 0 else (4 * (rows - 1) + 1, 4 * (rows - 1) + 2)
            pick = jnp.where(at_end, cells[1], cells[0])
            other = mu_ref if edge == 0 else md_ref
            if p == 0:
                inner = jnp.where(at_end, at_cut(5, blocks - 1), at_cut(4, 0))
            elif p == 2:
                inner = lane_gather(other[1], pick)
            elif p == 4:
                inner = jnp.where(at_end, at_cut(0, blocks - 1), lane_gather(other[0], pick))
            elif p == 5:
                inner = jnp.where(at_end, lane_gather(other[0], pick), at_cut(0, 0))
            else:
                inner = lane_gather(turned, jnp.where(at_end, 2 * edge, 2 * edge + 1))
            own_row = 0 if edge == 0 else rows - 1
            across = pltpu.roll(x, (126 - 4 * own_row) % LANES, 1)
            along = jnp.where(
                at_end, pltpu.roll(at_cut(p, 0), LANES - 1, 1), pltpu.roll(at_cut(p, blocks - 1), 1, 1)
            )
            corner = first if edge == 0 else final
            for version, own in ((0, across), (1, along)):
                value = jnp.where(corner, own, inner)
                slot = 2 * edge + version
                hcp_ref[p, slot] = mix(fwd, value[0:layers])
                hcv_ref[p, slot] = mix(bwd, value[layers : 2 * layers])
                hcb_ref[p, slot] = jnp.broadcast_to(value[CH - 4 : CH - 3], (8, LANES))


def halos(tiles, layers, rows, west, east, em, mm, mu, md, aa, fwd, bwd, sel):
    panels, n = west.shape[0], west.shape[3]
    shapes = [
        (panels, 4, layers, n), (panels, 4, layers, n), (panels, 2, layers, n), (panels, 8, n),
        (panels, layers, LANES), (panels, layers, LANES), (panels, layers, LANES), (panels, 8, LANES),
        (panels, 4, layers, LANES), (panels, 4, layers, LANES), (panels, 4, 8, LANES),
    ]
    return pl.pallas_call(
        functools.partial(halo_kernel, tiles, layers, rows),
        out_shape=[jax.ShapeDtypeStruct(s, F32) for s in shapes],
        scratch_shapes=[pltpu.VMEM((panels, 4, CH, n), F32)],
        compiler_params=pltpu.CompilerParams(vmem_limit_bytes=48 * 1024 * 1024),
        name="halos",
    )(west, east, em, mm, mu, md, aa, fwd, bwd, sel)


def main_kernel(
    layers, scale,
    p_ref, v_ref, y_ref, b_ref,
    hrp, hrv, hry, hrb, hlp, hlv, hly, hlb, hcp, hcv, hcb,
    g_ref,
    sp, sv, sy, sz, bi, bj, acc,
):
    rows, n = p_ref.shape[1], p_ref.shape[3]
    wide = n + LANES
    halves = layers // 8
    for src, row_src, col_src, cor_src, dst in (
        (p_ref, hrp, hlp, hcp, sp),
        (v_ref, hrv, hlv, hcv, sv),
    ):
        zero = jnp.zeros((layers, LANES), F32)
        for k, (slot, tail) in enumerate(
            ((0, zero), (1, cor_src[0, 1]), (rows + 2, cor_src[0, 3]), (rows + 3, zero))
        ):
            dst[slot, :, 0:n] = row_src[0, k]
            dst[slot, :, n:wide] = tail
        for k, slot, corner in ((1, rows + 4, 0), (2, rows + 5, 2)):
            dst[slot, :, 0:n] = row_src[0, k]
            dst[slot, :, n:wide] = cor_src[0, corner]

    def tail_of(ref, r):
        return pltpu.roll(ref[0], lax.rem(126 - 4 * r + 4 * LANES, LANES), 1)

    def fill(r, carry):
        sp[r + 2, :, 0:n] = p_ref[0, r]
        sp[r + 2, :, n:wide] = tail_of(hlp, r)
        sv[r + 2, :, 0:n] = v_ref[0, r]
        sv[r + 2, :, n:wide] = tail_of(hlv, r)
        return carry

    lax.fori_loop(0, rows, fill, 0, unroll=2)

    half_step = 0.5 * STEP_FACTOR

    def depth_row(r):
        return jnp.concatenate(
            [jnp.broadcast_to(b_ref[0, pl.ds(r, 1), :], (8, n)), tail_of(hlb, r)], axis=1
        )

    def depth_halo(k, tail):
        return jnp.concatenate([jnp.broadcast_to(hrb[0, k : k + 1, :], (8, n)), tail], axis=1)

    def shift_next(x):
        return pltpu.roll(x, wide - 1, 1)

    def shift_back(x):
        return pltpu.roll(x, 1, 1)

    zero = jnp.zeros((8, LANES), F32)
    d_m2, d_m1 = depth_halo(0, zero), depth_halo(1, hcb[0, 1])
    d_p0, d_p1 = depth_halo(2, hcb[0, 3]), depth_halo(3, zero)
    j_m1, j_p0 = depth_halo(1, hcb[0, 0]), depth_halo(2, hcb[0, 2])
    bi[0] = half_step * (d_m2 + d_m1)
    bi[1] = half_step * (d_m1 + depth_row(0))
    bi[rows + 1] = half_step * (depth_row(rows - 1) + d_p0)
    bi[rows + 2] = half_step * (d_p0 + d_p1)
    bj[0] = half_step * (j_m1 + shift_next(j_m1))
    bj[rows + 1] = half_step * (j_p0 + shift_next(j_p0))

    def fill_depth(r, here):
        bj[r + 1] = half_step * (here + shift_next(here))
        after = depth_row(jnp.minimum(r + 1, rows - 1))

        @pl.when(r + 1 < rows)
        def _():
            bi[r + 2] = half_step * (here + after)

        return after

    lax.fori_loop(0, rows, fill_depth, depth_row(0))

    def outflow(ref, h, at, flat, out):
        part = slice(8 * h, 8 * h + 8)
        here = ref[at, part]
        before = bi[out - 1 + 0] * (here - ref[at - 1, part])
        after = bi[out] * (ref[at + 1, part] - here)
        line = here if flat is None else ref[flat, part]
        along = bj[out - 1] * (shift_next(line) - line)
        return after - before + along - shift_back(along)

    def laps(at, flat, y0):
        slot = lax.rem(at, 2) if not isinstance(at, int) else at % 2
        for h in range(halves):
            part = slice(8 * h, 8 * h + 8)
            sy[slot, part] = y0(part) + outflow(sp, h, at, flat, at)
            sz[slot, part] = outflow(sv, h, at, flat, at)

    def halo_y(k):
        def get(part):
            return jnp.concatenate([hry[0, k, part, :], zero], axis=1)

        return get

    def own_y(r):
        tail = tail_of(hly, r)

        def get(part):
            return jnp.concatenate([y_ref[0, r, part, :], tail[part]], axis=1)

        return get

    def between(at):
        slot = lax.rem(at, 2) if not isinstance(at, int) else at % 2
        total = None
        for h in range(halves):
            part = slice(8 * h, 8 * h + 8)
            term = (sv[at, part, 0:n] - sv[at - 1, part, 0:n]) * (sy[slot, part, 0:n] - sy[1 - slot, part, 0:n])
            term += (sz[slot, part, 0:n] - sz[1 - slot, part, 0:n]) * (sp[at, part, 0:n] - sp[at - 1, part, 0:n])
            total = term if total is None else total + term
        return total

    def along_row(at):
        slot = lax.rem(at, 2) if not isinstance(at, int) else at % 2
        total = None
        for h in range(halves):
            part = slice(8 * h, 8 * h + 8)
            v, y, z, q = sv[at, part], sy[slot, part], sz[slot, part], sp[at, part]
            term = (shift_next(v) - v) * (shift_next(y) - y) + (shift_next(z) - z) * (shift_next(q) - q)
            total = term if total is None else total + term
        return (total + shift_back(total))[:, 0:n]

    factor = -half_step * scale

    def finish(r, total):
        g_ref[0, pl.ds(r, 1), :] = factor * jnp.sum(total, axis=0, keepdims=True)

    laps(1, rows + 4, halo_y(0))

    def step(r, carry):
        at = r + 2
        laps(at, None, own_y(r))
        edge = between(at)

        @pl.when(r > 0)
        def _():
            finish(r - 1, acc[...] + edge)

        acc[...] = edge + along_row(at)
        return carry

    lax.fori_loop(0, rows, step, 0)
    laps(rows + 2, rows + 5, halo_y(1))
    finish(rows - 1, acc[...] + between(rows + 2))


def main(scale, fields, depth, halo):
    panels, rows, layers, n = fields[0].shape
    wide = n + LANES
    block = lambda x: pl.BlockSpec((1,) + x.shape[1:], lambda p: (p,) + (0,) * (x.ndim - 1))
    operands = [*fields, depth, *halo]
    return pl.pallas_call(
        functools.partial(main_kernel, layers, scale),
        grid=(panels,),
        in_specs=[block(x) for x in operands],
        out_specs=pl.BlockSpec((1, rows, n), lambda p: (p, 0, 0)),
        out_shape=jax.ShapeDtypeStruct((panels, rows, n), F32),
        scratch_shapes=[
            pltpu.VMEM((rows + 6, layers, wide), F32),
            pltpu.VMEM((rows + 6, layers, wide), F32),
            pltpu.VMEM((2, layers, wide), F32),
            pltpu.VMEM((2, layers, wide), F32),
            pltpu.VMEM((rows + 3, 8, wide), F32),
            pltpu.VMEM((rows + 2, 8, wide), F32),
            pltpu.VMEM((8, n), F32),
        ],
        compiler_params=pltpu.CompilerParams(vmem_limit_bytes=48 * 1024 * 1024),
        name="main",
    )(*operands)


def body(bathymetry, initial_state, patterns, pattern_index, coupling, final_weights):
    tiles, samples = lax.axis_size("tile"), lax.axis_size("samp")
    layers, panels, rows, n = initial_state.shape
    weights = final_weights[0]
    mixing = jnp.eye(layers, dtype=F32) + coupling

    def cat(matrix):
        high = lax.reduce_precision(matrix, 8, 7)
        low = matrix - high
        return jnp.concatenate([high, low, high], axis=1).astype(jnp.bfloat16)

    fwd, bwd = cat(mixing), cat(mixing.T)
    sel = (pattern_index[0][:, None] == jnp.arange(8, dtype=jnp.int32)[None, :]).astype(jnp.bfloat16)

    em, low, high, mm, aa = pack(tiles, initial_state, weights, patterns, bathymetry)
    ring = [(i, (i + 1) % tiles) for i in range(tiles)]
    west = lax.ppermute(high, "tile", ring)
    east = lax.ppermute(low, "tile", [(j, i) for i, j in ring])
    mirrored = lax.ppermute(mm, "tile", [(i, tiles - 1 - i) for i in range(tiles)])
    above = lax.ppermute(mm[0:2], "tile", [(i, tiles - i) for i in range(1, tiles)])
    below = lax.ppermute(mm[0:2], "tile", [(i, tiles - 2 - i) for i in range(tiles - 1)])
    windows = lax.all_to_all(aa, "tile", 0, 0, tiled=True)
    fields = mix_all(initial_state, weights, patterns, fwd, bwd, sel)
    halo = halos(tiles, layers, rows, west, east, em, mirrored, above, below, windows, fwd, bwd, sel)
    gradient = main(1.0 / samples, fields, bathymetry, halo)
    if samples == 2:
        return gradient + lax.ppermute(gradient, "samp", [(0, 1), (1, 0)])
    return lax.psum(gradient, "samp")


def solution(mesh):
    in_specs = (
        P(None, "tile", None),
        P(None, None, "tile", None),
        P(None, None, "tile", None),
        P("samp", None),
        P(),
        P("samp", None, None, "tile", None),
    )
    return jax.shard_map(body, mesh=mesh, in_specs=in_specs, out_specs=P(None, "tile", None), check_vma=False)
```

```python
import functools

import jax
import jax.numpy as jnp
from jax import lax
from jax.experimental import pallas as pl
from jax.experimental.pallas import tpu as pltpu
from jax.sharding import PartitionSpec as P

STEP_FACTOR = 0.1
LANES = 128
GROUP = 4
CH = 40
F32 = jnp.float32


def lane_iota(shape):
    return lax.broadcasted_iota(jnp.int32, shape, len(shape) - 1)


def lane_gather(x, idx):
    return jnp.take_along_axis(x, idx, axis=1, mode="promise_in_bounds")


def mix(cat, x):
    hi = x.astype(jnp.bfloat16)
    lo = (x - hi.astype(F32)).astype(jnp.bfloat16)
    return jnp.dot(cat, jnp.concatenate([hi, hi, lo], axis=0), preferred_element_type=F32)


STRIDED = True


def layer_rows(ref, r):
    size, rows = ref.shape[0], ref.shape[2]
    if not STRIDED:
        return ref[:, 0, r, :]
    return ref.reshape(size * rows, LANES)[pl.ds(r, size, stride=rows), :]


def pack_kernel(tiles, s_ref, w_ref, pat_ref, b_ref, em_ref, lo_ref, hi_ref, mm_ref, aa_ref, aux):
    layers, rows = s_ref.shape[0], s_ref.shape[2]
    p, block, blocks = pl.program_id(0), pl.program_id(1), pl.num_programs(1)
    place = lax.axis_index("tile")
    first, final = place == 0, place == tiles - 1
    npat = pat_ref.shape[0]
    aux[...] = jnp.zeros(aux.shape, F32)
    aux[0:npat, 0] = pat_ref[:, 0].astype(F32)
    aux[npat, 0] = b_ref[0]
    groups = ((0, layers, s_ref), (layers, layers, w_ref), (2 * layers, 8, aux))

    for at, size, ref in groups:
        for c in range(2):
            lo_ref[0, c, at : at + size, :] = layer_rows(ref, c)
            hi_ref[0, c, at : at + size, :] = layer_rows(ref, rows - 2 + c)

    lane = lane_iota((CH, LANES))
    side = lane % 4

    @pl.when((p == 0) & (block == 0))
    def _():
        aa_ref[...] = jnp.zeros(aa_ref.shape, F32)

    @pl.when(block == 0)
    def _():
        em_ref[...] = jnp.zeros(em_ref.shape, F32)

    for mine, at_block in (((0, 1), blocks - 1), ((2, 3), 0)):
        @pl.when(block == at_block)
        def _(mine=mine):
            for at, size, ref in groups:
                ln = lane_iota((size, LANES))
                keep = (ln % 4 == mine[0]) | (ln % 4 == mine[1])
                out = jnp.zeros((size, LANES), F32)
                for r in range(rows):
                    turned = pltpu.roll(layer_rows(ref, r), (4 * r - 126) % LANES, 1)
                    out = jnp.where(ln // 4 == r, turned, out)
                em_ref[0, at : at + size, :] = jnp.where(keep, out, em_ref[0, at : at + size, :])

    @pl.when(block == blocks - 1)
    def _():
        @pl.when(p == 1)
        def _():
            aa_ref[tiles - 1, 0:CH, :] = em_ref[0]
            mm_ref[2] = em_ref[0]

        @pl.when(p == 2)
        def _():
            mm_ref[0] = em_ref[0]

        @pl.when(p == 3)
        def _():
            aa_ref[0, 0:CH, :] = em_ref[0]

        @pl.when((p == 3) & jnp.logical_not(first))
        def _():
            mm_ref[2] = em_ref[0]

        @pl.when(p == 4)
        def _():
            mm_ref[1] = em_ref[0]

        @pl.when(p == 5)
        def _():
            mm_ref[1] = jnp.where(side < 2, mm_ref[1], em_ref[0])

    per = LANES // rows

    def pole(ref, near, far, backward, is_five):
        x, y = ref[0, near], ref[0, far]
        turned = jnp.concatenate([x, jnp.zeros((LANES - CH, LANES), F32)], axis=0).T
        for q in range(per):
            if backward:
                t = (blocks - 1 - block) * per + q
                idx = LANES - 1 - q * rows - lane // 4
            else:
                t = block * per + q
                idx = q * rows + lane // 4
            idx = jnp.clip(idx, 0, LANES - 1)
            a, b = lane_gather(x, idx), lane_gather(y, idx)
            if is_five:
                aa_ref[t, 0:CH, :] = jnp.where(side == 1, a, jnp.where(side == 0, b, aa_ref[t, 0:CH, :]))
            else:
                aa_ref[t, 0:CH, :] = jnp.where(side == 2, a, b)
            low, high = q * rows, (q + 1) * rows - 1
            if backward:
                before, at_before = tiles - block * per - q, low
                after, at_after = tiles - 1 - block * per - (q + 1), high
            else:
                before, at_before = block * per + q + 1, high
                after, at_after = block * per + q - 1, low
            m = 0 if is_five else 1

            @pl.when(before < tiles)
            def _(before=before, at=at_before):
                aa_ref[before, CH + m : CH + m + 1, :] = turned[at : at + 1, :]

            @pl.when(after >= 0)
            def _(after=after, at=at_after):
                aa_ref[after, CH + m + 2 : CH + m + 3, :] = turned[at : at + 1, :]

    for panel in (4, 5):
        @pl.when((p == panel) & first)
        def _(panel=panel):
            pole(lo_ref, 0, 1, panel == 4, panel == 5)

        @pl.when((p == panel) & final)
        def _(panel=panel):
            pole(hi_ref, 1, 0, panel == 5, panel == 5)


def pack(tiles, s, w, pat, b):
    layers, panels, rows, n = s.shape
    npat = pat.shape[0]
    full = lambda *shape: pl.BlockSpec(shape, lambda p, c: (0,) * len(shape))
    part = lambda size: pl.BlockSpec((size, 1, rows, LANES), lambda p, c: (0, p, 0, c))
    line = pl.BlockSpec((1, 2, CH, LANES), lambda p, c: (p, 0, 0, c))
    return pl.pallas_call(
        functools.partial(pack_kernel, tiles),
        grid=(panels, n // LANES),
        in_specs=[part(layers), part(layers), part(npat), pl.BlockSpec((1, rows, LANES), lambda p, c: (p, 0, c))],
        out_specs=[
            pl.BlockSpec((1, CH, LANES), lambda p, c: (p, 0, 0)),
            line,
            line,
            full(3, CH, LANES),
            full(tiles, CH + 8, LANES),
        ],
        out_shape=[
            jax.ShapeDtypeStruct((panels, CH, LANES), F32),
            jax.ShapeDtypeStruct((panels, 2, CH, n), F32),
            jax.ShapeDtypeStruct((panels, 2, CH, n), F32),
            jax.ShapeDtypeStruct((3, CH, LANES), F32),
            jax.ShapeDtypeStruct((tiles, CH + 8, LANES), F32),
        ],
        scratch_shapes=[pltpu.VMEM((8, 1, rows, LANES), F32)],
        compiler_params=pltpu.CompilerParams(vmem_limit_bytes=48 * 1024 * 1024),
        name="pack",
    )(s, w, pat, b)


def mix_kernel(s_ref, w_ref, pat_ref, fwd_ref, bwd_ref, sel_ref, p_ref, v_ref, y_ref, pf):
    rows = s_ref.shape[2]
    npat = pat_ref.shape[0]
    pf[...] = jnp.zeros(pf.shape, F32)
    pf[0:npat, 0] = pat_ref[:, 0].astype(F32)
    fwd, bwd, sel = fwd_ref[...], bwd_ref[...], sel_ref[...]
    for r in range(rows):
        s = layer_rows(s_ref, r)
        p_ref[0, r] = mix(fwd, s)
        v_ref[0, r] = mix(bwd, layer_rows(w_ref, r))
        f = jnp.dot(sel, layer_rows(pf, r).astype(jnp.bfloat16), preferred_element_type=F32)
        y_ref[0, r] = 3.0 * s + STEP_FACTOR * f


def mix_all(s, w, pat, fwd, bwd, sel):
    layers, panels, rows, n = s.shape
    npat = pat.shape[0]
    full = lambda x: pl.BlockSpec(x.shape, lambda p, c: (0,) * x.ndim)
    part = lambda size: pl.BlockSpec((size, 1, rows, LANES), lambda p, c: (0, p, 0, c))
    out = pl.BlockSpec((1, rows, layers, LANES), lambda p, c: (p, 0, 0, c))
    size = layers * panels * rows * n * 4
    return pl.pallas_call(
        mix_kernel,
        grid=(panels, n // LANES),
        in_specs=[part(layers), part(layers), part(npat), full(fwd), full(bwd), full(sel)],
        out_specs=[out] * 3,
        out_shape=[jax.ShapeDtypeStruct((panels, rows, layers, n), F32)] * 3,
        scratch_shapes=[pltpu.VMEM((8, 1, rows, LANES), F32)],
        compiler_params=pltpu.CompilerParams(vmem_limit_bytes=48 * 1024 * 1024),
        cost_estimate=pl.CostEstimate(flops=size * 48, bytes_accessed=5 * size, transcendentals=0),
        name="mix",
    )(s, w, pat, fwd, bwd, sel)


def halo_kernel(
    tiles, layers, rows,
    west_ref, east_ref, em_ref, mm_ref, mu_ref, md_ref, aa_ref, fwd_ref, bwd_ref, sel_ref,
    hrp_ref, hrv_ref, hry_ref, hrb_ref, hlp_ref, hlv_ref, hly_ref, hlb_ref, hcp_ref, hcv_ref, hcb_ref,
    line,
):
    panels, n = west_ref.shape[0], west_ref.shape[3]
    place = lax.axis_index("tile")
    first, final = place == 0, place == tiles - 1
    fwd, bwd, sel = fwd_ref[...], bwd_ref[...], sel_ref[...]
    lane = lane_iota((CH, LANES))
    side = lane % 4
    blocks = n // LANES
    per = LANES // rows

    for p in range(panels):
        @pl.when(jnp.logical_not(first))
        def _(p=p):
            line[p, 0:2] = west_ref[p]

        @pl.when(jnp.logical_not(final))
        def _(p=p):
            line[p, 2:4] = east_ref[p]

        if p < 4:
            @pl.when(first)
            def _(p=p):
                line[p, 0:2] = west_ref[(p + 3) % 4]

            @pl.when(final)
            def _(p=p):
                line[p, 2:4] = east_ref[(p + 1) % 4]

    def collect(u_of, dest, k, backward):
        within = lane % rows
        idx = 4 * (rows - 1 - within) + k if backward else 4 * within + k
        p, at = dest
        for block in range(blocks):
            out = jnp.zeros((CH, LANES), F32)
            for q in range(per):
                u = block * per + q
                u = tiles - 1 - u if backward else u
                out = jnp.where(lane // rows == q, lane_gather(u_of(u), idx), out)
            line[p, at, :, block * LANES : (block + 1) * LANES] = out

    @pl.when(first)
    def _():
        def of(u):
            return em_ref[3] if u == 0 else mm_ref[2] if u == tiles - 1 else aa_ref[u, 0:CH, :]

        collect(of, (4, 1), 1, True)
        collect(of, (4, 0), 0, True)
        collect(of, (5, 1), 2, False)
        collect(of, (5, 0), 3, False)

    @pl.when(final)
    def _():
        def of(u):
            return mm_ref[2] if u == 0 else em_ref[1] if u == tiles - 1 else aa_ref[u, 0:CH, :]

        collect(of, (4, 2), 1, False)
        collect(of, (4, 3), 0, False)
        collect(of, (5, 2), 2, True)
        collect(of, (5, 3), 3, True)

    def force(x):
        return 3.0 * x[0:layers] + STEP_FACTOR * jnp.dot(
            sel, x[2 * layers : CH].astype(jnp.bfloat16), preferred_element_type=F32
        )

    for p in range(panels):
        for k in range(4):
            x = line[p, k]
            hrp_ref[p, k] = mix(fwd, x[0:layers])
            hrv_ref[p, k] = mix(bwd, x[layers : 2 * layers])
            hrb_ref[p, k : k + 1, :] = line[p, k, CH - 4 : CH - 3, :]
            if k in (1, 2):
                hry_ref[p, k - 1] = force(x)

    span = 4 * rows
    turn = jnp.where(lane < span, span - 1 - lane, 0)
    back0 = lane_gather(mm_ref[0], turn)
    back1 = lane_gather(mm_ref[1], turn)
    columns = (
        jnp.where(side < 2, em_ref[5], em_ref[4]),
        aa_ref[tiles - 1, 0:CH, :],
        back1,
        aa_ref[0, 0:CH, :],
        jnp.where(side < 2, em_ref[0], back0),
        jnp.where(side < 2, back0, em_ref[0]),
    )
    at_end = lane == LANES - 1
    pad = jnp.zeros((LANES - 8, LANES), F32)
    for p in range(panels):
        x = columns[p]
        hlp_ref[p] = mix(fwd, x[0:layers])
        hlv_ref[p] = mix(bwd, x[layers : 2 * layers])
        hly_ref[p] = force(x)
        depth = x[CH - 4 : CH - 3]
        hlb_ref[p] = jnp.broadcast_to(depth, (8, LANES))
        if p in (1, 3):
            turned = jnp.concatenate([aa_ref[tiles - 1 if p == 1 else 0, CH:, :], pad], axis=0).T[0:CH]
        for edge in range(2):
            at = 1 + edge
            at_cut = lambda q, block: line[q, at, :, block * LANES : (block + 1) * LANES]
            cells = (1, 2) if edge == 0 else (4 * (rows - 1) + 1, 4 * (rows - 1) + 2)
            pick = jnp.where(at_end, cells[1], cells[0])
            other = mu_ref if edge == 0 else md_ref
            if p == 0:
                inner = jnp.where(at_end, at_cut(5, blocks - 1), at_cut(4, 0))
            elif p == 2:
                inner = lane_gather(other[1], pick)
            elif p == 4:
                inner = jnp.where(at_end, at_cut(0, blocks - 1), lane_gather(other[0], pick))
            elif p == 5:
                inner = jnp.where(at_end, lane_gather(other[0], pick), at_cut(0, 0))
            else:
                inner = lane_gather(turned, jnp.where(at_end, 2 * edge, 2 * edge + 1))
            own_row = 0 if edge == 0 else rows - 1
            across = pltpu.roll(x, (126 - 4 * own_row) % LANES, 1)
            along = jnp.where(
                at_end, pltpu.roll(at_cut(p, 0), LANES - 1, 1), pltpu.roll(at_cut(p, blocks - 1), 1, 1)
            )
            corner = first if edge == 0 else final
            for version, own in ((0, across), (1, along)):
                value = jnp.where(corner, own, inner)
                slot = 2 * edge + version
                hcp_ref[p, slot] = mix(fwd, value[0:layers])
                hcv_ref[p, slot] = mix(bwd, value[layers : 2 * layers])
                hcb_ref[p, slot] = jnp.broadcast_to(value[CH - 4 : CH - 3], (8, LANES))


def halos(tiles, layers, rows, west, east, em, mm, mu, md, aa, fwd, bwd, sel):
    panels, n = west.shape[0], west.shape[3]
    shapes = [
        (panels, 4, layers, n), (panels, 4, layers, n), (panels, 2, layers, n), (panels, 8, n),
        (panels, layers, LANES), (panels, layers, LANES), (panels, layers, LANES), (panels, 8, LANES),
        (panels, 4, layers, LANES), (panels, 4, layers, LANES), (panels, 4, 8, LANES),
    ]
    return pl.pallas_call(
        functools.partial(halo_kernel, tiles, layers, rows),
        out_shape=[jax.ShapeDtypeStruct(s, F32) for s in shapes],
        scratch_shapes=[pltpu.VMEM((panels, 4, CH, n), F32)],
        compiler_params=pltpu.CompilerParams(vmem_limit_bytes=48 * 1024 * 1024),
        name="halos",
    )(west, east, em, mm, mu, md, aa, fwd, bwd, sel)


def main_kernel(
    layers, scale,
    p_ref, v_ref, y_ref, b_ref,
    hrp, hrv, hry, hrb, hlp, hlv, hly, hlb, hcp, hcv, hcb,
    g_ref,
    sp, sv, sy, sz, ip, iv, jp, jv, ty, bi, bj, acc,
):
    rows, n = p_ref.shape[1], p_ref.shape[3]
    wide = n + LANES
    halves = layers // 8
    for src, row_src, col_src, cor_src, dst in (
        (p_ref, hrp, hlp, hcp, sp),
        (v_ref, hrv, hlv, hcv, sv),
    ):
        zero = jnp.zeros((layers, LANES), F32)
        for k, (slot, tail) in enumerate(
            ((0, zero), (1, cor_src[0, 1]), (rows + 2, cor_src[0, 3]), (rows + 3, zero))
        ):
            dst[slot, :, 0:n] = row_src[0, k]
            dst[slot, :, n:wide] = tail
        for k, slot, corner in ((1, rows + 4, 0), (2, rows + 5, 2)):
            dst[slot, :, 0:n] = row_src[0, k]
            dst[slot, :, n:wide] = cor_src[0, corner]

    def tail_of(x, r):
        return pltpu.roll(x, (126 - 4 * r) % LANES, 1)

    def shift_next(x):
        return pltpu.roll(x, wide - 1, 1)

    def shift_back(x):
        return pltpu.roll(x, 1, 1)

    edges_p, edges_v, edges_y, edges_b = hlp[0], hlv[0], hly[0], hlb[0]
    half_step = 0.5 * STEP_FACTOR
    zero = jnp.zeros((8, LANES), F32)

    def depth_halo(k, tail):
        return jnp.concatenate([jnp.broadcast_to(hrb[0, k : k + 1, :], (8, n)), tail], axis=1)

    d_m2, d_m1 = depth_halo(0, zero), depth_halo(1, hcb[0, 1])
    d_p0, d_p1 = depth_halo(2, hcb[0, 3]), depth_halo(3, zero)
    j_m1, j_p0 = depth_halo(1, hcb[0, 0]), depth_halo(2, hcb[0, 2])
    bi[0] = half_step * (d_m2 + d_m1)
    bi[rows + 2] = half_step * (d_p0 + d_p1)
    bj[0] = half_step * (j_m1 + shift_next(j_m1))
    bj[rows + 1] = half_step * (j_p0 + shift_next(j_p0))
    last = d_m1
    for r in range(rows):
        sp[r + 2, :, 0:n] = p_ref[0, r]
        sp[r + 2, :, n:wide] = tail_of(edges_p, r)
        sv[r + 2, :, 0:n] = v_ref[0, r]
        sv[r + 2, :, n:wide] = tail_of(edges_v, r)
        ty[r] = tail_of(edges_y, r)
        here = jnp.concatenate([jnp.broadcast_to(b_ref[0, r : r + 1, :], (8, n)), tail_of(edges_b, r)], axis=1)
        bi[r + 1] = half_step * (last + here)
        bj[r + 1] = half_step * (here + shift_next(here))
        last = here
    bi[rows + 1] = half_step * (last + d_p0)

    def lap(ref, at, flat, bases, outs, by_i, by_j, count):
        for h in range(halves):
            part = slice(8 * h, 8 * h + 8)
            here = ref[at, part]
            before = bi[at - 1] * (here - ref[at - 1, part])
            for u in range(count):
                after_row = ref[at + u + 1, part]
                step_i = after_row - here
                if by_i is not None:
                    by_i[at + u - 1, part] = step_i[:, 0:n]
                after = bi[at + u] * step_i
                line = here if flat is None else ref[flat, part]
                step_j = shift_next(line) - line
                if by_j is not None:
                    by_j[at + u - 2, part] = step_j
                along = bj[at + u - 1] * step_j
                out = after - before + along - shift_back(along)
                if bases is not None:
                    out = out + bases(u, part)
                outs[at + u - 1, part] = out
                here, before = after_row, after

    def halo_y(k):
        return lambda u, part: jnp.concatenate([hry[0, k, part, :], zero], axis=1)

    lap(sp, 1, rows + 4, halo_y(0), sy, ip, None, 1)
    lap(sv, 1, rows + 4, None, sz, iv, None, 1)
    lap(sp, rows + 2, rows + 5, halo_y(1), sy, None, None, 1)
    lap(sv, rows + 2, rows + 5, None, sz, None, None, 1)

    group = GROUP

    def lap_rows(i, carry):
        r = i * group

        def own_y(u, part):
            return jnp.concatenate([y_ref[0, r + u, part, :], ty[r + u, part]], axis=1)

        lap(sp, r + 2, None, own_y, sy, ip, jp, group)
        lap(sv, r + 2, None, None, sz, iv, jv, group)
        return carry

    lax.fori_loop(0, rows // group, lap_rows, 0)

    def between(k):
        total = None
        for h in range(halves):
            part = slice(8 * h, 8 * h + 8)
            term = iv[k, part] * (sy[k + 1, part, 0:n] - sy[k, part, 0:n])
            term += ip[k, part] * (sz[k + 1, part, 0:n] - sz[k, part, 0:n])
            total = term if total is None else total + term
        return total

    def along_row(r):
        total = None
        for h in range(halves):
            part = slice(8 * h, 8 * h + 8)
            y, z = sy[r + 1, part], sz[r + 1, part]
            term = jv[r, part] * (shift_next(y) - y) + jp[r, part] * (shift_next(z) - z)
            total = term if total is None else total + term
        return (total + shift_back(total))[:, 0:n]

    def products(i, before):
        r = i * group
        for u in range(group):
            after = between(r + u + 1)
            acc[r + u] = before + after + along_row(r + u)
            before = after
        return before

    lax.fori_loop(0, rows // group, products, between(0))

    x = acc[...].reshape(8 * rows, n)
    at_row = lax.broadcasted_iota(jnp.int32, (rows, 8 * rows), 0)
    ones = (lax.broadcasted_iota(jnp.int32, (rows, 8 * rows), 1) // 8 == at_row).astype(F32).astype(jnp.bfloat16)
    hi = x.astype(jnp.bfloat16)
    rest = x - hi.astype(F32)
    lo = rest.astype(jnp.bfloat16)
    total = jnp.dot(ones, hi, preferred_element_type=F32) + jnp.dot(ones, lo, preferred_element_type=F32)
    g_ref[0] = (-half_step * scale) * total


def main(scale, fields, depth, halo):
    panels, rows, layers, n = fields[0].shape
    wide = n + LANES
    block = lambda x: pl.BlockSpec((1,) + x.shape[1:], lambda p: (p,) + (0,) * (x.ndim - 1))
    operands = [*fields, depth, *halo]
    return pl.pallas_call(
        functools.partial(main_kernel, layers, scale),
        grid=(panels,),
        in_specs=[block(x) for x in operands],
        out_specs=pl.BlockSpec((1, rows, n), lambda p: (p, 0, 0)),
        out_shape=jax.ShapeDtypeStruct((panels, rows, n), F32),
        scratch_shapes=[
            pltpu.VMEM((rows + 6, layers, wide), F32),
            pltpu.VMEM((rows + 6, layers, wide), F32),
            pltpu.VMEM((rows + 2, layers, wide), F32),
            pltpu.VMEM((rows + 2, layers, wide), F32),
            pltpu.VMEM((rows + 1, layers, n), F32),
            pltpu.VMEM((rows + 1, layers, n), F32),
            pltpu.VMEM((rows, layers, wide), F32),
            pltpu.VMEM((rows, layers, wide), F32),
            pltpu.VMEM((rows, layers, LANES), F32),
            pltpu.VMEM((rows + 3, 8, wide), F32),
            pltpu.VMEM((rows + 2, 8, wide), F32),
            pltpu.VMEM((rows, 8, n), F32),
        ],
        compiler_params=pltpu.CompilerParams(vmem_limit_bytes=48 * 1024 * 1024),
        name="main",
    )(*operands)


def body(bathymetry, initial_state, patterns, pattern_index, coupling, final_weights):
    tiles, samples = lax.axis_size("tile"), lax.axis_size("samp")
    layers, panels, rows, n = initial_state.shape
    weights = final_weights[0]
    mixing = jnp.eye(layers, dtype=F32) + coupling

    def cat(matrix):
        high = lax.reduce_precision(matrix, 8, 7)
        low = matrix - high
        return jnp.concatenate([high, low, high], axis=1).astype(jnp.bfloat16)

    fwd, bwd = cat(mixing), cat(mixing.T)
    sel = (pattern_index[0][:, None] == jnp.arange(8, dtype=jnp.int32)[None, :]).astype(jnp.bfloat16)

    em, low, high, mm, aa = pack(tiles, initial_state, weights, patterns, bathymetry)
    ring = [(i, (i + 1) % tiles) for i in range(tiles)]
    west = lax.ppermute(high, "tile", ring)
    east = lax.ppermute(low, "tile", [(j, i) for i, j in ring])
    mirrored = lax.ppermute(mm, "tile", [(i, tiles - 1 - i) for i in range(tiles)])
    above = lax.ppermute(mm[0:2], "tile", [(i, tiles - i) for i in range(1, tiles)])
    below = lax.ppermute(mm[0:2], "tile", [(i, tiles - 2 - i) for i in range(tiles - 1)])
    windows = lax.all_to_all(aa, "tile", 0, 0, tiled=True)
    fields = mix_all(initial_state, weights, patterns, fwd, bwd, sel)
    halo = halos(tiles, layers, rows, west, east, em, mirrored, above, below, windows, fwd, bwd, sel)
    gradient = main(1.0 / samples, fields, bathymetry, halo)
    if samples == 2:
        return gradient + lax.ppermute(gradient, "samp", [(0, 1), (1, 0)])
    return lax.psum(gradient, "samp")


def solution(mesh):
    in_specs = (
        P(None, "tile", None),
        P(None, None, "tile", None),
        P(None, None, "tile", None),
        P("samp", None),
        P(),
        P("samp", None, None, "tile", None),
    )
    return jax.shard_map(body, mesh=mesh, in_specs=in_specs, out_specs=P(None, "tile", None), check_vma=False)
```

```python
import functools

import jax
import jax.numpy as jnp
from jax import lax
from jax.experimental import pallas as pl
from jax.experimental.pallas import tpu as pltpu
from jax.sharding import PartitionSpec as P

STEP_FACTOR = 0.1
LANES = 128
GROUP = 4
CH = 40
F32 = jnp.float32


def lane_iota(shape):
    return lax.broadcasted_iota(jnp.int32, shape, len(shape) - 1)


def lane_gather(x, idx):
    return jnp.take_along_axis(x, idx, axis=1, mode="promise_in_bounds")


def mix(cat, x):
    hi = x.astype(jnp.bfloat16)
    lo = (x - hi.astype(F32)).astype(jnp.bfloat16)
    return jnp.dot(cat, jnp.concatenate([hi, hi, lo], axis=0), preferred_element_type=F32)


STRIDED = True
VMEM = 60 * 1024 * 1024


def layer_rows(ref, r):
    size, rows = ref.shape[0], ref.shape[2]
    if not STRIDED:
        return ref[:, 0, r, :]
    return ref.reshape(size * rows, LANES)[pl.ds(r, size, stride=rows), :]


def pack_kernel(tiles, blocks, layers, npat, *refs):
    s_refs, w_refs, pat_refs = (refs[k * blocks : (k + 1) * blocks] for k in range(3))
    b_ref, em_ref, lo_ref, hi_ref, mm_ref, aa_ref, aux = refs[3 * blocks :]
    rows = b_ref.shape[1]
    p = pl.program_id(0)
    place = lax.axis_index("tile")
    first, final = place == 0, place == tiles - 1
    aux[...] = jnp.zeros(aux.shape, F32)
    for c in range(blocks):
        aux[c, 0:npat, 0] = pat_refs[c][:, 0].astype(F32)
        aux[c, npat, 0] = b_ref[0, :, c * LANES : (c + 1) * LANES]
    groups = (
        (0, layers, s_refs),
        (layers, layers, w_refs),
        (2 * layers, 8, [aux.at[c] for c in range(blocks)]),
    )
    for at, size, parts in groups:
        for c in range(blocks):
            cut = slice(c * LANES, (c + 1) * LANES)
            for k in range(2):
                lo_ref[0, k, at : at + size, cut] = layer_rows(parts[c], k)
                hi_ref[0, k, at : at + size, cut] = layer_rows(parts[c], rows - 2 + k)

    for at, size, parts in groups:
        shape = (8 * size, LANES)
        ln, row = lane_iota(shape), lax.broadcasted_iota(jnp.int32, shape, 0) % 8
        source = (ln % 4 + LANES - 2) % LANES
        total = jnp.zeros(shape, F32)
        for g in range(rows // 8):
            cut = slice(8 * g, 8 * g + 8)
            head = parts[0][:, 0, cut, :].reshape(shape)
            tail = parts[blocks - 1][:, 0, cut, :].reshape(shape)
            spread = lane_gather(jnp.where(ln < LANES // 2, head, tail), source)
            total = jnp.where(ln // 4 == 8 * g + row, spread, total)
        em_ref[0, at : at + size, :] = jnp.sum(total.reshape(size, 8, LANES), axis=1)

    lane = lane_iota((CH, LANES))
    side = lane % 4
    pad = jnp.zeros((LANES - CH, LANES), F32)

    @pl.when(p == 0)
    def _():
        aa_ref[...] = jnp.zeros(aa_ref.shape, F32)

    @pl.when(p == 1)
    def _():
        aa_ref[tiles - 1, 0:CH, :] = em_ref[0]
        mm_ref[2] = em_ref[0]

    @pl.when(p == 2)
    def _():
        mm_ref[0] = em_ref[0]

    @pl.when(p == 3)
    def _():
        aa_ref[0, 0:CH, :] = em_ref[0]

    @pl.when((p == 3) & jnp.logical_not(first))
    def _():
        mm_ref[2] = em_ref[0]

    @pl.when(p == 4)
    def _():
        mm_ref[1] = em_ref[0]

    per = LANES // rows

    def pole(ref, near, far, backward, is_five):
        for block in range(blocks):
            cut = slice(block * LANES, (block + 1) * LANES)
            x, y = ref[0, near, :, cut], ref[0, far, :, cut]
            turned = jnp.concatenate([x, pad], axis=0).T
            for q in range(per):
                if backward:
                    t = (blocks - 1 - block) * per + q
                    idx = LANES - 1 - q * rows - lane // 4
                else:
                    t = block * per + q
                    idx = q * rows + lane // 4
                idx = jnp.clip(idx, 0, LANES - 1)
                a, b = lane_gather(x, idx), lane_gather(y, idx)
                if is_five:
                    aa_ref[t, 0:CH, :] = jnp.where(side == 1, a, jnp.where(side == 0, b, aa_ref[t, 0:CH, :]))
                else:
                    aa_ref[t, 0:CH, :] = jnp.where(side == 2, a, b)
                low, high = q * rows, (q + 1) * rows - 1
                if backward:
                    before, at_before = tiles - block * per - q, low
                    after, at_after = tiles - 1 - block * per - (q + 1), high
                else:
                    before, at_before = block * per + q + 1, high
                    after, at_after = block * per + q - 1, low
                m = CH if is_five else CH + 1
                if before < tiles:
                    aa_ref[before, m : m + 1, :] = turned[at_before : at_before + 1, :]
                if after >= 0:
                    aa_ref[after, m + 2 : m + 3, :] = turned[at_after : at_after + 1, :]

    for panel in (4, 5):
        @pl.when((p == panel) & first)
        def _(panel=panel):
            pole(lo_ref, 0, 1, panel == 4, panel == 5)

        @pl.when((p == panel) & final)
        def _(panel=panel):
            pole(hi_ref, 1, 0, panel == 5, panel == 5)

    @pl.when(p == 5)
    def _():
        mm_ref[1] = jnp.where(side < 2, mm_ref[1], em_ref[0])
        for k in range(2):
            turned = jnp.concatenate([mm_ref[k], pad], axis=0).T
            m = CH + 4 + 2 * k

            @pl.when(jnp.logical_not(first))
            def _(turned=turned, m=m):
                aa_ref[tiles - place, m : m + 2, :] = turned[1:3, :]

            @pl.when(jnp.logical_not(final))
            def _(turned=turned, m=m):
                at = 4 * (rows - 1) + 1
                aa_ref[tiles - 2 - place, m : m + 2, :] = turned[at : at + 2, :]


def pack(tiles, s, w, pat, b):
    layers, panels, rows, n = s.shape
    npat, blocks = pat.shape[0], n // LANES
    full = lambda *shape: pl.BlockSpec(shape, lambda p: (0,) * len(shape))
    part = lambda size, c: pl.BlockSpec((size, 1, rows, LANES), lambda p: (0, p, 0, c))
    line = pl.BlockSpec((1, 2, CH, n), lambda p: (p, 0, 0, 0))
    return pl.pallas_call(
        functools.partial(pack_kernel, tiles, blocks, layers, npat),
        grid=(panels,),
        in_specs=[part(size, c) for size in (layers, layers, npat) for c in range(blocks)]
        + [pl.BlockSpec((1, rows, n), lambda p: (p, 0, 0))],
        out_specs=[
            pl.BlockSpec((1, CH, LANES), lambda p: (p, 0, 0)),
            line,
            line,
            full(3, CH, LANES),
            full(tiles, CH + 8, LANES),
        ],
        out_shape=[
            jax.ShapeDtypeStruct((panels, CH, LANES), F32),
            jax.ShapeDtypeStruct((panels, 2, CH, n), F32),
            jax.ShapeDtypeStruct((panels, 2, CH, n), F32),
            jax.ShapeDtypeStruct((3, CH, LANES), F32),
            jax.ShapeDtypeStruct((tiles, CH + 8, LANES), F32),
        ],
        scratch_shapes=[pltpu.VMEM((blocks, 8, 1, rows, LANES), F32)],
        compiler_params=pltpu.CompilerParams(vmem_limit_bytes=VMEM),
        name="pack",
    )(*[s] * blocks, *[w] * blocks, *[pat] * blocks, b)


def mix_kernel(s_ref, w_ref, pat_ref, fwd_ref, bwd_ref, sel_ref, p_ref, v_ref, y_ref, left_s, left_w, pf):
    layers, n = s_ref.shape[0], s_ref.shape[3]
    npat, rows = pat_ref.shape[0], pat_ref.shape[2]
    size = 8 * layers
    p, g = pl.program_id(0), pl.program_id(1)

    @pl.when((p == 0) & (g == 0))
    def _():
        def spread(matrix, count):
            down = lax.broadcasted_iota(jnp.int32, (size, layers), 0) % layers
            down = (down == lax.broadcasted_iota(jnp.int32, (size, layers), 1)).astype(F32).astype(jnp.bfloat16)
            over = lax.broadcasted_iota(jnp.int32, (count, 8 * count), 1) // 8
            over = (over == lax.broadcasted_iota(jnp.int32, (count, 8 * count), 0)).astype(F32).astype(jnp.bfloat16)
            x = jnp.dot(down, matrix, preferred_element_type=F32).astype(jnp.bfloat16)
            x = jnp.dot(x, over, preferred_element_type=F32)
            same = lax.broadcasted_iota(jnp.int32, x.shape, 0) // layers
            same = same == lax.broadcasted_iota(jnp.int32, x.shape, 1) % 8
            return jnp.where(same, x, 0.0).astype(jnp.bfloat16)

        def parts(ref):
            return spread(ref[:, 0:layers], layers), spread(ref[:, layers : 2 * layers], layers)

        eye = lax.broadcasted_iota(jnp.int32, (layers, layers), 0) == lax.broadcasted_iota(
            jnp.int32, (layers, layers), 1
        )
        thirty = spread(jnp.where(eye, 30.0, 0.0).astype(jnp.bfloat16), layers)
        high, low = parts(fwd_ref)
        none = jnp.zeros((size, size), jnp.bfloat16)
        pattern = spread(sel_ref[...], 8)
        left_s[0:size, :] = jnp.concatenate([high, high, low, none[:, 0:64]], axis=1)
        left_s[size:, :] = jnp.concatenate([thirty, thirty, none, pattern], axis=1)
        high, low = parts(bwd_ref)
        left_w[...] = jnp.concatenate([high, high, low], axis=1)

    @pl.when(g == 0)
    def _():
        pf[...] = jnp.zeros(pf.shape, F32)
        pf[0:npat] = pat_ref[:, 0].astype(F32)

    def pieces(x):
        hi = x.astype(jnp.bfloat16)
        return hi, (x - hi.astype(F32)).astype(jnp.bfloat16)

    step = min(n, 256)
    for at in range(0, n, step):
        cut = slice(at, at + step)
        hi, lo = pieces(s_ref[:, 0, :, cut].reshape(size, step))
        f = pf[:, pl.ds(pl.multiple_of(8 * g, 8), 8), cut].reshape(64, step).astype(jnp.bfloat16)
        both = jnp.dot(left_s[...], jnp.concatenate([hi, lo, hi, f], axis=0), preferred_element_type=F32)
        p_ref[0, :, :, cut] = both[0:size].reshape(8, layers, step)
        y_ref[0, :, :, cut] = both[size:].reshape(8, layers, step)
        hi, lo = pieces(w_ref[:, 0, :, cut].reshape(size, step))
        v = jnp.dot(left_w[...], jnp.concatenate([hi, lo, hi], axis=0), preferred_element_type=F32)
        v_ref[0, :, :, cut] = v.reshape(8, layers, step)


def mix_all(s, w, pat, fwd, bwd, sel):
    layers, panels, rows, n = s.shape
    npat = pat.shape[0]
    full = lambda x: pl.BlockSpec(x.shape, lambda p, g: (0,) * x.ndim)
    part = pl.BlockSpec((layers, 1, 8, n), lambda p, g: (0, p, g, 0))
    out = pl.BlockSpec((1, 8, layers, n), lambda p, g: (p, g, 0, 0))
    size = layers * panels * rows * n * 4
    wide = 8 * layers
    return pl.pallas_call(
        mix_kernel,
        grid=(panels, rows // 8),
        in_specs=[part, part, pl.BlockSpec((npat, 1, rows, n), lambda p, g: (0, p, 0, 0)), full(fwd), full(bwd), full(sel)],
        out_specs=[out] * 3,
        out_shape=[jax.ShapeDtypeStruct((panels, rows, layers, n), F32)] * 3,
        scratch_shapes=[
            pltpu.VMEM((2 * wide, 3 * wide + 64), jnp.bfloat16),
            pltpu.VMEM((wide, 3 * wide), jnp.bfloat16),
            pltpu.VMEM((8, rows, n), F32),
        ],
        compiler_params=pltpu.CompilerParams(vmem_limit_bytes=VMEM),
        cost_estimate=pl.CostEstimate(flops=size * 48, bytes_accessed=5 * size, transcendentals=0),
        name="mix",
    )(s, w, pat, fwd, bwd, sel)


def halo_kernel(
    tiles, layers, rows,
    west_ref, east_ref, em_ref, mm_ref, aa_ref, fwd_ref, bwd_ref, sel_ref,
    hrp_ref, hrv_ref, hry_ref, hrb_ref, hlp_ref, hlv_ref, hly_ref, hlb_ref, hcp_ref, hcv_ref, hcb_ref,
    line,
):
    panels, n = west_ref.shape[0], west_ref.shape[3]
    place = lax.axis_index("tile")
    first, final = place == 0, place == tiles - 1
    fwd, bwd, sel = fwd_ref[...], bwd_ref[...], sel_ref[...]
    lane = lane_iota((CH, LANES))
    side = lane % 4
    blocks = n // LANES
    per = LANES // rows

    for p in range(panels):
        @pl.when(jnp.logical_not(first))
        def _(p=p):
            line[p, 0:2] = west_ref[p]

        @pl.when(jnp.logical_not(final))
        def _(p=p):
            line[p, 2:4] = east_ref[p]

        if p < 4:
            @pl.when(first)
            def _(p=p):
                line[p, 0:2] = west_ref[(p + 3) % 4]

            @pl.when(final)
            def _(p=p):
                line[p, 2:4] = east_ref[(p + 1) % 4]

    def collect(u_of, dest, k, backward):
        within = lane % rows
        idx = 4 * (rows - 1 - within) + k if backward else 4 * within + k
        p, at = dest
        for block in range(blocks):
            out = jnp.zeros((CH, LANES), F32)
            for q in range(per):
                u = block * per + q
                u = tiles - 1 - u if backward else u
                out = jnp.where(lane // rows == q, lane_gather(u_of(u), idx), out)
            line[p, at, :, block * LANES : (block + 1) * LANES] = out

    @pl.when(first)
    def _():
        def of(u):
            return em_ref[3] if u == 0 else mm_ref[2] if u == tiles - 1 else aa_ref[u, 0:CH, :]

        collect(of, (4, 1), 1, True)
        collect(of, (4, 0), 0, True)
        collect(of, (5, 1), 2, False)
        collect(of, (5, 0), 3, False)

    @pl.when(final)
    def _():
        def of(u):
            return mm_ref[2] if u == 0 else em_ref[1] if u == tiles - 1 else aa_ref[u, 0:CH, :]

        collect(of, (4, 2), 1, False)
        collect(of, (4, 3), 0, False)
        collect(of, (5, 2), 2, True)
        collect(of, (5, 3), 3, True)

    def force(x):
        return (3.0 / STEP_FACTOR) * x[0:layers] + jnp.dot(
            sel, x[2 * layers : CH].astype(jnp.bfloat16), preferred_element_type=F32
        )

    for p in range(panels):
        for k in range(4):
            x = line[p, k]
            hrp_ref[p, k] = mix(fwd, x[0:layers])
            hrv_ref[p, k] = mix(bwd, x[layers : 2 * layers])
            hrb_ref[p, k : k + 1, :] = line[p, k, CH - 4 : CH - 3, :]
            if k in (1, 2):
                hry_ref[p, k - 1] = force(x)

    span = 4 * rows
    turn = jnp.where(lane < span, span - 1 - lane, 0)
    back0 = lane_gather(mm_ref[0], turn)
    back1 = lane_gather(mm_ref[1], turn)
    columns = (
        jnp.where(side < 2, em_ref[5], em_ref[4]),
        aa_ref[tiles - 1, 0:CH, :],
        back1,
        aa_ref[0, 0:CH, :],
        jnp.where(side < 2, em_ref[0], back0),
        jnp.where(side < 2, back0, em_ref[0]),
    )
    at_end = lane == LANES - 1
    pad = jnp.zeros((LANES - 8, LANES), F32)
    mirrored = [
        jnp.concatenate([aa_ref[u, CH:, :], pad], axis=0).T[0:CH]
        for u in (jnp.minimum(tiles - place, tiles - 1), jnp.maximum(tiles - 2 - place, 0))
    ]
    for p in range(panels):
        x = columns[p]
        hlp_ref[p] = mix(fwd, x[0:layers])
        hlv_ref[p] = mix(bwd, x[layers : 2 * layers])
        hly_ref[p] = force(x)
        depth = x[CH - 4 : CH - 3]
        hlb_ref[p] = jnp.broadcast_to(depth, (8, LANES))
        if p in (1, 3):
            turned = jnp.concatenate([aa_ref[tiles - 1 if p == 1 else 0, CH:, :], pad], axis=0).T[0:CH]
        for edge in range(2):
            at = 1 + edge
            at_cut = lambda q, block: line[q, at, :, block * LANES : (block + 1) * LANES]
            beside = lambda k: lane_gather(mirrored[edge], jnp.where(at_end, 5 + 2 * k, 4 + 2 * k))
            if p == 0:
                inner = jnp.where(at_end, at_cut(5, blocks - 1), at_cut(4, 0))
            elif p == 2:
                inner = beside(1)
            elif p == 4:
                inner = jnp.where(at_end, at_cut(0, blocks - 1), beside(0))
            elif p == 5:
                inner = jnp.where(at_end, beside(0), at_cut(0, 0))
            else:
                inner = lane_gather(turned, jnp.where(at_end, 2 * edge, 2 * edge + 1))
            own_row = 0 if edge == 0 else rows - 1
            across = pltpu.roll(x, (126 - 4 * own_row) % LANES, 1)
            along = jnp.where(
                at_end, pltpu.roll(at_cut(p, 0), LANES - 1, 1), pltpu.roll(at_cut(p, blocks - 1), 1, 1)
            )
            corner = first if edge == 0 else final
            for version, own in ((0, across), (1, along)):
                value = jnp.where(corner, own, inner)
                slot = 2 * edge + version
                hcp_ref[p, slot] = mix(fwd, value[0:layers])
                hcv_ref[p, slot] = mix(bwd, value[layers : 2 * layers])
                hcb_ref[p, slot] = jnp.broadcast_to(value[CH - 4 : CH - 3], (8, LANES))


def halos(tiles, layers, rows, west, east, em, mm, aa, fwd, bwd, sel):
    panels, n = west.shape[0], west.shape[3]
    shapes = [
        (panels, 4, layers, n), (panels, 4, layers, n), (panels, 2, layers, n), (panels, 8, n),
        (panels, layers, LANES), (panels, layers, LANES), (panels, layers, LANES), (panels, 8, LANES),
        (panels, 4, layers, LANES), (panels, 4, layers, LANES), (panels, 4, 8, LANES),
    ]
    return pl.pallas_call(
        functools.partial(halo_kernel, tiles, layers, rows),
        out_shape=[jax.ShapeDtypeStruct(s, F32) for s in shapes],
        scratch_shapes=[pltpu.VMEM((panels, 4, CH, n), F32)],
        compiler_params=pltpu.CompilerParams(vmem_limit_bytes=VMEM),
        name="halos",
    )(west, east, em, mm, aa, fwd, bwd, sel)


def main_kernel(
    layers, scale,
    p_ref, v_ref, y_ref, b_ref,
    hrp, hrv, hry, hrb, hlp, hlv, hly, hlb, hcp, hcv, hcb,
    g_ref,
    sp, sv, sy, sz, ip, iv, jp, jv, ty, bi, bj, acc,
):
    rows, n = p_ref.shape[1], p_ref.shape[3]
    wide = n + LANES
    halves = layers // 8
    for src, row_src, col_src, cor_src, dst in (
        (p_ref, hrp, hlp, hcp, sp),
        (v_ref, hrv, hlv, hcv, sv),
    ):
        zero = jnp.zeros((layers, LANES), F32)
        for k, (slot, tail) in enumerate(
            ((0, zero), (1, cor_src[0, 1]), (rows + 2, cor_src[0, 3]), (rows + 3, zero))
        ):
            dst[slot, :, 0:n] = row_src[0, k]
            dst[slot, :, n:wide] = tail
        for k, slot, corner in ((1, rows + 4, 0), (2, rows + 5, 2)):
            dst[slot, :, 0:n] = row_src[0, k]
            dst[slot, :, n:wide] = cor_src[0, corner]

    def tail_of(x, r):
        return pltpu.roll(x, (126 - 4 * r) % LANES, 1)

    def shift_next(x):
        return pltpu.roll(x, wide - 1, 1)

    def shift_back(x):
        return pltpu.roll(x, 1, 1)

    edges_p, edges_v, edges_y, edges_b = hlp[0], hlv[0], hly[0], hlb[0]
    zero = jnp.zeros((8, LANES), F32)

    def depth_halo(k, tail):
        return jnp.concatenate([jnp.broadcast_to(hrb[0, k : k + 1, :], (8, n)), tail], axis=1)

    d_m2, d_m1 = depth_halo(0, zero), depth_halo(1, hcb[0, 1])
    d_p0, d_p1 = depth_halo(2, hcb[0, 3]), depth_halo(3, zero)
    j_m1, j_p0 = depth_halo(1, hcb[0, 0]), depth_halo(2, hcb[0, 2])
    bi[0] = 0.5 * (d_m2 + d_m1)
    bi[rows + 2] = 0.5 * (d_p0 + d_p1)
    bj[0] = 0.5 * (j_m1 + shift_next(j_m1))
    bj[rows + 1] = 0.5 * (j_p0 + shift_next(j_p0))
    last = d_m1
    for r in range(rows):
        sp[r + 2, :, 0:n] = p_ref[0, r]
        sp[r + 2, :, n:wide] = tail_of(edges_p, r)
        sv[r + 2, :, 0:n] = v_ref[0, r]
        sv[r + 2, :, n:wide] = tail_of(edges_v, r)
        ty[r] = tail_of(edges_y, r)
        here = jnp.concatenate([jnp.broadcast_to(b_ref[0, r : r + 1, :], (8, n)), tail_of(edges_b, r)], axis=1)
        bi[r + 1] = 0.5 * (last + here)
        bj[r + 1] = 0.5 * (here + shift_next(here))
        last = here
    bi[rows + 1] = 0.5 * (last + d_p0)

    def lap(ref, at, flat, bases, outs, by_i, by_j, count):
        for h in range(halves):
            part = slice(8 * h, 8 * h + 8)
            here = ref[at, part]
            before = bi[at - 1] * (here - ref[at - 1, part])
            for u in range(count):
                after_row = ref[at + u + 1, part]
                step_i = after_row - here
                if by_i is not None:
                    by_i[at + u - 1, part] = step_i[:, 0:n]
                after = bi[at + u] * step_i
                line = here if flat is None else ref[flat, part]
                step_j = shift_next(line) - line
                if by_j is not None:
                    by_j[at + u - 2, part] = step_j
                along = bj[at + u - 1] * step_j
                out = after - before + along - shift_back(along)
                if bases is not None:
                    out = out + bases(u, part)
                outs[at + u - 1, part] = out
                here, before = after_row, after

    def halo_y(k):
        return lambda u, part: jnp.concatenate([hry[0, k, part, :], zero], axis=1)

    lap(sp, 1, rows + 4, halo_y(0), sy, ip, None, 1)
    lap(sv, 1, rows + 4, None, sz, iv, None, 1)
    lap(sp, rows + 2, rows + 5, halo_y(1), sy, None, None, 1)
    lap(sv, rows + 2, rows + 5, None, sz, None, None, 1)

    group = GROUP

    def lap_rows(i, carry):
        r = i * group

        def own_y(u, part):
            return jnp.concatenate([y_ref[0, r + u, part, :], ty[r + u, part]], axis=1)

        lap(sp, r + 2, None, own_y, sy, ip, jp, group)
        lap(sv, r + 2, None, None, sz, iv, jv, group)
        return carry

    lax.fori_loop(0, rows // group, lap_rows, 0)

    def between(k):
        total = None
        for h in range(halves):
            part = slice(8 * h, 8 * h + 8)
            term = iv[k, part] * (sy[k + 1, part, 0:n] - sy[k, part, 0:n])
            term += ip[k, part] * (sz[k + 1, part, 0:n] - sz[k, part, 0:n])
            total = term if total is None else total + term
        return total

    def along_row(r):
        total = None
        for h in range(halves):
            part = slice(8 * h, 8 * h + 8)
            y, z = sy[r + 1, part], sz[r + 1, part]
            term = jv[r, part] * (shift_next(y) - y) + jp[r, part] * (shift_next(z) - z)
            total = term if total is None else total + term
        return (total + shift_back(total))[:, 0:n]

    def products(i, before):
        r = i * group
        for u in range(group):
            after = between(r + u + 1)
            acc[r + u] = before + after + along_row(r + u)
            before = after
        return before

    lax.fori_loop(0, rows // group, products, between(0))

    x = acc[...].reshape(8 * rows, n)
    at_row = lax.broadcasted_iota(jnp.int32, (rows, 8 * rows), 0)
    ones = (lax.broadcasted_iota(jnp.int32, (rows, 8 * rows), 1) // 8 == at_row).astype(F32).astype(jnp.bfloat16)
    hi = x.astype(jnp.bfloat16)
    rest = x - hi.astype(F32)
    lo = rest.astype(jnp.bfloat16)
    total = jnp.dot(ones, hi, preferred_element_type=F32) + jnp.dot(ones, lo, preferred_element_type=F32)
    g_ref[0] = (-0.5 * STEP_FACTOR * STEP_FACTOR * scale) * total


def main(scale, begin, count, fields, depth, halo):
    _, rows, layers, n = fields[0].shape
    wide = n + LANES
    block = lambda x: pl.BlockSpec((1,) + x.shape[1:], lambda p: (p + begin,) + (0,) * (x.ndim - 1))
    operands = [*fields, depth, *halo]
    return pl.pallas_call(
        functools.partial(main_kernel, layers, scale),
        grid=(count,),
        in_specs=[block(x) for x in operands],
        out_specs=pl.BlockSpec((1, rows, n), lambda p: (p, 0, 0)),
        out_shape=jax.ShapeDtypeStruct((count, rows, n), F32),
        scratch_shapes=[
            pltpu.VMEM((rows + 6, layers, wide), F32),
            pltpu.VMEM((rows + 6, layers, wide), F32),
            pltpu.VMEM((rows + 2, layers, wide), F32),
            pltpu.VMEM((rows + 2, layers, wide), F32),
            pltpu.VMEM((rows + 1, layers, n), F32),
            pltpu.VMEM((rows + 1, layers, n), F32),
            pltpu.VMEM((rows, layers, wide), F32),
            pltpu.VMEM((rows, layers, wide), F32),
            pltpu.VMEM((rows, layers, LANES), F32),
            pltpu.VMEM((rows + 3, 8, wide), F32),
            pltpu.VMEM((rows + 2, 8, wide), F32),
            pltpu.VMEM((rows, 8, n), F32),
        ],
        compiler_params=pltpu.CompilerParams(vmem_limit_bytes=VMEM),
        cost_estimate=pl.CostEstimate(
            flops=count * rows * layers * wide * 60, bytes_accessed=count * rows * layers * n * 16, transcendentals=0
        ),
        name="main",
    )(*operands)


def body(bathymetry, initial_state, patterns, pattern_index, coupling, final_weights):
    tiles, samples = lax.axis_size("tile"), lax.axis_size("samp")
    layers, panels, rows, n = initial_state.shape
    weights = final_weights[0]
    mixing = jnp.eye(layers, dtype=F32) + coupling

    def cat(matrix):
        high = lax.reduce_precision(matrix, 8, 7)
        low = matrix - high
        return jnp.concatenate([high, low, high], axis=1).astype(jnp.bfloat16)

    fwd, bwd = cat(mixing), cat(mixing.T)
    sel = (pattern_index[0][:, None] == jnp.arange(8, dtype=jnp.int32)[None, :]).astype(jnp.bfloat16)

    em, low, high, mm, aa = pack(tiles, initial_state, weights, patterns, bathymetry)
    ring = [(i, (i + 1) % tiles) for i in range(tiles)]
    west = lax.ppermute(high, "tile", ring)
    east = lax.ppermute(low, "tile", [(j, i) for i, j in ring])
    mirrored = lax.ppermute(mm, "tile", [(i, tiles - 1 - i) for i in range(tiles)])
    windows = lax.all_to_all(aa, "tile", 0, 0, tiled=True)
    fields = mix_all(initial_state, weights, patterns, fwd, bwd, sel)
    halo = halos(tiles, layers, rows, west, east, em, mirrored, windows, fwd, bwd, sel)
    totals = []
    for begin, end in ((0, panels // 2), (panels // 2, panels)):
        part = main(1.0 / samples, begin, end - begin, fields, bathymetry, halo)
        if samples == 2:
            totals.append(part + lax.ppermute(part, "samp", [(0, 1), (1, 0)]))
        else:
            totals.append(lax.psum(part, "samp"))
    return jnp.concatenate(totals, axis=0)


def solution(mesh):
    in_specs = (
        P(None, "tile", None),
        P(None, None, "tile", None),
        P(None, None, "tile", None),
        P("samp", None),
        P(),
        P("samp", None, None, "tile", None),
    )
    return jax.shard_map(body, mesh=mesh, in_specs=in_specs, out_specs=P(None, "tile", None), check_vma=False)
```

```python
import functools

import jax
import jax.numpy as jnp
from jax import lax
from jax.experimental import pallas as pl
from jax.experimental.pallas import tpu as pltpu
from jax.sharding import PartitionSpec as P

STEP_FACTOR = 0.1
LANES = 128
GROUP = 4
CH = 40
F32 = jnp.float32


def lane_iota(shape):
    return lax.broadcasted_iota(jnp.int32, shape, len(shape) - 1)


def lane_gather(x, idx):
    return jnp.take_along_axis(x, idx, axis=1, mode="promise_in_bounds")


def mix(cat, x):
    hi = x.astype(jnp.bfloat16)
    lo = (x - hi.astype(F32)).astype(jnp.bfloat16)
    return jnp.dot(cat, jnp.concatenate([hi, hi, lo], axis=0), preferred_element_type=F32)


STRIDED = True
VMEM = 60 * 1024 * 1024


def layer_rows(ref, r):
    size, rows = ref.shape[0], ref.shape[2]
    if not STRIDED:
        return ref[:, 0, r, :]
    return ref.reshape(size * rows, LANES)[pl.ds(r, size, stride=rows), :]


def pack_kernel(tiles, blocks, layers, npat, *refs):
    s_refs, w_refs, pat_refs = (refs[k * blocks : (k + 1) * blocks] for k in range(3))
    b_ref, em_ref, lo_ref, hi_ref, mm_ref, aa_ref, aux = refs[3 * blocks :]
    rows = b_ref.shape[1]
    p = pl.program_id(0)
    place = lax.axis_index("tile")
    first, final = place == 0, place == tiles - 1
    aux[...] = jnp.zeros(aux.shape, F32)
    for c in range(blocks):
        aux[c, 0:npat, 0] = pat_refs[c][:, 0].astype(F32)
        aux[c, npat, 0] = b_ref[0, :, c * LANES : (c + 1) * LANES]
    groups = (
        (0, layers, s_refs),
        (layers, layers, w_refs),
        (2 * layers, 8, [aux.at[c] for c in range(blocks)]),
    )
    for at, size, parts in groups:
        for c in range(blocks):
            cut = slice(c * LANES, (c + 1) * LANES)
            for k in range(2):
                lo_ref[0, k, at : at + size, cut] = layer_rows(parts[c], k)
                hi_ref[0, k, at : at + size, cut] = layer_rows(parts[c], rows - 2 + k)

    for at, size, parts in groups:
        shape = (8 * size, LANES)
        ln, row = lane_iota(shape), lax.broadcasted_iota(jnp.int32, shape, 0) % 8
        source = (ln % 4 + LANES - 2) % LANES
        total = jnp.zeros(shape, F32)
        for g in range(rows // 8):
            cut = slice(8 * g, 8 * g + 8)
            head = parts[0][:, 0, cut, :].reshape(shape)
            tail = parts[blocks - 1][:, 0, cut, :].reshape(shape)
            spread = lane_gather(jnp.where(ln < LANES // 2, head, tail), source)
            total = jnp.where(ln // 4 == 8 * g + row, spread, total)
        em_ref[0, at : at + size, :] = jnp.sum(total.reshape(size, 8, LANES), axis=1)

    lane = lane_iota((CH, LANES))
    side = lane % 4
    pad = jnp.zeros((LANES - CH, LANES), F32)

    @pl.when(p == 0)
    def _():
        aa_ref[...] = jnp.zeros(aa_ref.shape, F32)

    @pl.when(p == 1)
    def _():
        aa_ref[tiles - 1, 0:CH, :] = em_ref[0]
        mm_ref[2] = em_ref[0]

    @pl.when(p == 2)
    def _():
        mm_ref[0] = em_ref[0]

    @pl.when(p == 3)
    def _():
        aa_ref[0, 0:CH, :] = em_ref[0]

    @pl.when((p == 3) & jnp.logical_not(first))
    def _():
        mm_ref[2] = em_ref[0]

    @pl.when(p == 4)
    def _():
        mm_ref[1] = em_ref[0]

    per = LANES // rows

    def pole(ref, near, far, backward, is_five):
        for block in range(blocks):
            cut = slice(block * LANES, (block + 1) * LANES)
            x, y = ref[0, near, :, cut], ref[0, far, :, cut]
            turned = jnp.concatenate([x, pad], axis=0).T
            for q in range(per):
                if backward:
                    t = (blocks - 1 - block) * per + q
                    idx = LANES - 1 - q * rows - lane // 4
                else:
                    t = block * per + q
                    idx = q * rows + lane // 4
                idx = jnp.clip(idx, 0, LANES - 1)
                a, b = lane_gather(x, idx), lane_gather(y, idx)
                if is_five:
                    aa_ref[t, 0:CH, :] = jnp.where(side == 1, a, jnp.where(side == 0, b, aa_ref[t, 0:CH, :]))
                else:
                    aa_ref[t, 0:CH, :] = jnp.where(side == 2, a, b)
                low, high = q * rows, (q + 1) * rows - 1
                if backward:
                    before, at_before = tiles - block * per - q, low
                    after, at_after = tiles - 1 - block * per - (q + 1), high
                else:
                    before, at_before = block * per + q + 1, high
                    after, at_after = block * per + q - 1, low
                m = CH if is_five else CH + 1
                if before < tiles:
                    aa_ref[before, m : m + 1, :] = turned[at_before : at_before + 1, :]
                if after >= 0:
                    aa_ref[after, m + 2 : m + 3, :] = turned[at_after : at_after + 1, :]

    for panel in (4, 5):
        @pl.when((p == panel) & first)
        def _(panel=panel):
            pole(lo_ref, 0, 1, panel == 4, panel == 5)

        @pl.when((p == panel) & final)
        def _(panel=panel):
            pole(hi_ref, 1, 0, panel == 5, panel == 5)

    @pl.when(p == 5)
    def _():
        mm_ref[1] = jnp.where(side < 2, mm_ref[1], em_ref[0])
        for k in range(2):
            turned = jnp.concatenate([mm_ref[k], pad], axis=0).T
            m = CH + 4 + 2 * k

            @pl.when(jnp.logical_not(first))
            def _(turned=turned, m=m):
                aa_ref[tiles - place, m : m + 2, :] = turned[1:3, :]

            @pl.when(jnp.logical_not(final))
            def _(turned=turned, m=m):
                at = 4 * (rows - 1) + 1
                aa_ref[tiles - 2 - place, m : m + 2, :] = turned[at : at + 2, :]


def pack(tiles, s, w, pat, b):
    layers, panels, rows, n = s.shape
    npat, blocks = pat.shape[0], n // LANES
    full = lambda *shape: pl.BlockSpec(shape, lambda p: (0,) * len(shape))
    part = lambda size, c: pl.BlockSpec((size, 1, rows, LANES), lambda p: (0, p, 0, c))
    line = pl.BlockSpec((1, 2, CH, n), lambda p: (p, 0, 0, 0))
    return pl.pallas_call(
        functools.partial(pack_kernel, tiles, blocks, layers, npat),
        grid=(panels,),
        in_specs=[part(size, c) for size in (layers, layers, npat) for c in range(blocks)]
        + [pl.BlockSpec((1, rows, n), lambda p: (p, 0, 0))],
        out_specs=[
            pl.BlockSpec((1, CH, LANES), lambda p: (p, 0, 0)),
            line,
            line,
            full(3, CH, LANES),
            full(tiles, CH + 8, LANES),
        ],
        out_shape=[
            jax.ShapeDtypeStruct((panels, CH, LANES), F32),
            jax.ShapeDtypeStruct((panels, 2, CH, n), F32),
            jax.ShapeDtypeStruct((panels, 2, CH, n), F32),
            jax.ShapeDtypeStruct((3, CH, LANES), F32),
            jax.ShapeDtypeStruct((tiles, CH + 8, LANES), F32),
        ],
        scratch_shapes=[pltpu.VMEM((blocks, 8, 1, rows, LANES), F32)],
        compiler_params=pltpu.CompilerParams(vmem_limit_bytes=VMEM),
        name="pack",
    )(*[s] * blocks, *[w] * blocks, *[pat] * blocks, b)


def mix_kernel(s_ref, w_ref, pat_ref, fwd_ref, bwd_ref, sel_ref, p_ref, v_ref, y_ref, left_s, left_w, left_f, pf):
    layers, n = s_ref.shape[0], s_ref.shape[3]
    npat, rows = pat_ref.shape[0], pat_ref.shape[2]
    size = 8 * layers

    @pl.when(pl.program_id(0) == 0)
    def _():
        def spread(matrix, count):
            down = lax.broadcasted_iota(jnp.int32, (size, layers), 0) % layers
            down = (down == lax.broadcasted_iota(jnp.int32, (size, layers), 1)).astype(F32).astype(jnp.bfloat16)
            over = lax.broadcasted_iota(jnp.int32, (count, 8 * count), 1) // 8
            over = (over == lax.broadcasted_iota(jnp.int32, (count, 8 * count), 0)).astype(F32).astype(jnp.bfloat16)
            x = jnp.dot(down, matrix, preferred_element_type=F32).astype(jnp.bfloat16)
            x = jnp.dot(x, over, preferred_element_type=F32)
            same = lax.broadcasted_iota(jnp.int32, x.shape, 0) // layers
            same = same == lax.broadcasted_iota(jnp.int32, x.shape, 1) % 8
            return jnp.where(same, x, 0.0).astype(jnp.bfloat16)

        def parts(ref):
            return spread(ref[:, 0:layers], layers), spread(ref[:, layers : 2 * layers], layers)

        eye = lax.broadcasted_iota(jnp.int32, (layers, layers), 0) == lax.broadcasted_iota(
            jnp.int32, (layers, layers), 1
        )
        thirty = spread(jnp.where(eye, 30.0, 0.0).astype(jnp.bfloat16), layers)
        high, low = parts(fwd_ref)
        for k, x in enumerate((high, low, thirty)):
            left_s[k * size : (k + 1) * size, :] = jnp.concatenate([x, x], axis=1)
        for k, x in enumerate(parts(bwd_ref)):
            left_w[k * size : (k + 1) * size, :] = jnp.concatenate([x, x], axis=1)
        left_f[...] = spread(sel_ref[...], 8)

    pf[...] = jnp.zeros(pf.shape, F32)
    pf[0:npat] = pat_ref[:, 0].astype(F32)

    def pieces(x):
        hi = x.astype(jnp.bfloat16)
        return jnp.concatenate([hi, (x - hi.astype(F32)).astype(jnp.bfloat16)], axis=0)

    def dot(a, b):
        return jnp.dot(a, b, preferred_element_type=F32)

    step = min(n, 256)
    for g in range(rows // 8):
        own = slice(8 * g, 8 * g + 8)
        for at in range(0, n, step):
            cut = slice(at, at + step)
            x = dot(left_s[...], pieces(s_ref[:, 0, own, cut].reshape(size, step)))
            f = dot(left_f[...], pf[:, own, cut].reshape(64, step).astype(jnp.bfloat16))
            p_ref[0, own, :, cut] = (x[0:size] + x[size : 2 * size]).reshape(8, layers, step)
            y_ref[0, own, :, cut] = (x[2 * size :] + f).reshape(8, layers, step)
            x = dot(left_w[...], pieces(w_ref[:, 0, own, cut].reshape(size, step)))
            v_ref[0, own, :, cut] = (x[0:size] + x[size:]).reshape(8, layers, step)


def mix_all(s, w, pat, fwd, bwd, sel):
    layers, panels, rows, n = s.shape
    npat = pat.shape[0]
    full = lambda x: pl.BlockSpec(x.shape, lambda p: (0,) * x.ndim)
    part = lambda count: pl.BlockSpec((count, 1, rows, n), lambda p: (0, p, 0, 0))
    out = pl.BlockSpec((1, rows, layers, n), lambda p: (p, 0, 0, 0))
    size = layers * panels * rows * n * 4
    wide = 8 * layers
    return pl.pallas_call(
        mix_kernel,
        grid=(panels,),
        in_specs=[part(layers), part(layers), part(npat), full(fwd), full(bwd), full(sel)],
        out_specs=[out] * 3,
        out_shape=[jax.ShapeDtypeStruct((panels, rows, layers, n), F32)] * 3,
        scratch_shapes=[
            pltpu.VMEM((3 * wide, 2 * wide), jnp.bfloat16),
            pltpu.VMEM((2 * wide, 2 * wide), jnp.bfloat16),
            pltpu.VMEM((wide, 64), jnp.bfloat16),
            pltpu.VMEM((8, rows, n), F32),
        ],
        compiler_params=pltpu.CompilerParams(vmem_limit_bytes=VMEM),
        cost_estimate=pl.CostEstimate(flops=size * 48, bytes_accessed=5 * size, transcendentals=0),
        name="mix",
    )(s, w, pat, fwd, bwd, sel)


def halo_kernel(
    tiles, layers, rows,
    west_ref, east_ref, em_ref, mm_ref, aa_ref, fwd_ref, bwd_ref, sel_ref,
    hrp_ref, hrv_ref, hry_ref, hrb_ref, hlp_ref, hlv_ref, hly_ref, hlb_ref, hcp_ref, hcv_ref, hcb_ref,
    line,
):
    panels, n = west_ref.shape[0], west_ref.shape[3]
    place = lax.axis_index("tile")
    first, final = place == 0, place == tiles - 1
    fwd, bwd, sel = fwd_ref[...], bwd_ref[...], sel_ref[...]
    lane = lane_iota((CH, LANES))
    side = lane % 4
    blocks = n // LANES
    per = LANES // rows

    for p in range(panels):
        @pl.when(jnp.logical_not(first))
        def _(p=p):
            line[p, 0:2] = west_ref[p]

        @pl.when(jnp.logical_not(final))
        def _(p=p):
            line[p, 2:4] = east_ref[p]

        if p < 4:
            @pl.when(first)
            def _(p=p):
                line[p, 0:2] = west_ref[(p + 3) % 4]

            @pl.when(final)
            def _(p=p):
                line[p, 2:4] = east_ref[(p + 1) % 4]

    def collect(u_of, dest, k, backward):
        within = lane % rows
        idx = 4 * (rows - 1 - within) + k if backward else 4 * within + k
        p, at = dest
        for block in range(blocks):
            out = jnp.zeros((CH, LANES), F32)
            for q in range(per):
                u = block * per + q
                u = tiles - 1 - u if backward else u
                out = jnp.where(lane // rows == q, lane_gather(u_of(u), idx), out)
            line[p, at, :, block * LANES : (block + 1) * LANES] = out

    @pl.when(first)
    def _():
        def of(u):
            return em_ref[3] if u == 0 else mm_ref[2] if u == tiles - 1 else aa_ref[u, 0:CH, :]

        collect(of, (4, 1), 1, True)
        collect(of, (4, 0), 0, True)
        collect(of, (5, 1), 2, False)
        collect(of, (5, 0), 3, False)

    @pl.when(final)
    def _():
        def of(u):
            return mm_ref[2] if u == 0 else em_ref[1] if u == tiles - 1 else aa_ref[u, 0:CH, :]

        collect(of, (4, 2), 1, False)
        collect(of, (4, 3), 0, False)
        collect(of, (5, 2), 2, True)
        collect(of, (5, 3), 3, True)

    def force(x):
        return (3.0 / STEP_FACTOR) * x[0:layers] + jnp.dot(
            sel, x[2 * layers : CH].astype(jnp.bfloat16), preferred_element_type=F32
        )

    for p in range(panels):
        for k in range(4):
            x = line[p, k]
            hrp_ref[p, k] = mix(fwd, x[0:layers])
            hrv_ref[p, k] = mix(bwd, x[layers : 2 * layers])
            hrb_ref[p, k : k + 1, :] = line[p, k, CH - 4 : CH - 3, :]
            if k in (1, 2):
                hry_ref[p, k - 1] = force(x)

    span = 4 * rows
    turn = jnp.where(lane < span, span - 1 - lane, 0)
    back0 = lane_gather(mm_ref[0], turn)
    back1 = lane_gather(mm_ref[1], turn)
    columns = (
        jnp.where(side < 2, em_ref[5], em_ref[4]),
        aa_ref[tiles - 1, 0:CH, :],
        back1,
        aa_ref[0, 0:CH, :],
        jnp.where(side < 2, em_ref[0], back0),
        jnp.where(side < 2, back0, em_ref[0]),
    )
    at_end = lane == LANES - 1
    pad = jnp.zeros((LANES - 8, LANES), F32)
    mirrored = [
        jnp.concatenate([aa_ref[u, CH:, :], pad], axis=0).T[0:CH]
        for u in (jnp.minimum(tiles - place, tiles - 1), jnp.maximum(tiles - 2 - place, 0))
    ]
    for p in range(panels):
        x = columns[p]
        hlp_ref[p] = mix(fwd, x[0:layers])
        hlv_ref[p] = mix(bwd, x[layers : 2 * layers])
        hly_ref[p] = force(x)
        depth = x[CH - 4 : CH - 3]
        hlb_ref[p] = jnp.broadcast_to(depth, (8, LANES))
        if p in (1, 3):
            turned = jnp.concatenate([aa_ref[tiles - 1 if p == 1 else 0, CH:, :], pad], axis=0).T[0:CH]
        for edge in range(2):
            at = 1 + edge
            at_cut = lambda q, block: line[q, at, :, block * LANES : (block + 1) * LANES]
            beside = lambda k: lane_gather(mirrored[edge], jnp.where(at_end, 5 + 2 * k, 4 + 2 * k))
            if p == 0:
                inner = jnp.where(at_end, at_cut(5, blocks - 1), at_cut(4, 0))
            elif p == 2:
                inner = beside(1)
            elif p == 4:
                inner = jnp.where(at_end, at_cut(0, blocks - 1), beside(0))
            elif p == 5:
                inner = jnp.where(at_end, beside(0), at_cut(0, 0))
            else:
                inner = lane_gather(turned, jnp.where(at_end, 2 * edge, 2 * edge + 1))
            own_row = 0 if edge == 0 else rows - 1
            across = pltpu.roll(x, (126 - 4 * own_row) % LANES, 1)
            along = jnp.where(
                at_end, pltpu.roll(at_cut(p, 0), LANES - 1, 1), pltpu.roll(at_cut(p, blocks - 1), 1, 1)
            )
            corner = first if edge == 0 else final
            for version, own in ((0, across), (1, along)):
                value = jnp.where(corner, own, inner)
                slot = 2 * edge + version
                hcp_ref[p, slot] = mix(fwd, value[0:layers])
                hcv_ref[p, slot] = mix(bwd, value[layers : 2 * layers])
                hcb_ref[p, slot] = jnp.broadcast_to(value[CH - 4 : CH - 3], (8, LANES))


def halos(tiles, layers, rows, west, east, em, mm, aa, fwd, bwd, sel):
    panels, n = west.shape[0], west.shape[3]
    shapes = [
        (panels, 4, layers, n), (panels, 4, layers, n), (panels, 2, layers, n), (panels, 8, n),
        (panels, layers, LANES), (panels, layers, LANES), (panels, layers, LANES), (panels, 8, LANES),
        (panels, 4, layers, LANES), (panels, 4, layers, LANES), (panels, 4, 8, LANES),
    ]
    return pl.pallas_call(
        functools.partial(halo_kernel, tiles, layers, rows),
        out_shape=[jax.ShapeDtypeStruct(s, F32) for s in shapes],
        scratch_shapes=[pltpu.VMEM((panels, 4, CH, n), F32)],
        compiler_params=pltpu.CompilerParams(vmem_limit_bytes=VMEM),
        name="halos",
    )(west, east, em, mm, aa, fwd, bwd, sel)


def main_kernel(
    layers, scale,
    p_ref, v_ref, y_ref, b_ref,
    hrp, hrv, hry, hrb, hlp, hlv, hly, hlb, hcp, hcv, hcb,
    g_ref,
    sp, sv, sy, sz, ip, iv, jp, jv, ty, depth, bi, bj, acc,
):
    rows, n = p_ref.shape[1], p_ref.shape[3]
    wide = n + LANES
    halves = layers // 8
    for src, row_src, col_src, cor_src, dst in (
        (p_ref, hrp, hlp, hcp, sp),
        (v_ref, hrv, hlv, hcv, sv),
    ):
        zero = jnp.zeros((layers, LANES), F32)
        for k, (slot, tail) in enumerate(
            ((0, zero), (1, cor_src[0, 1]), (rows + 2, cor_src[0, 3]), (rows + 3, zero))
        ):
            dst[slot, :, 0:n] = row_src[0, k]
            dst[slot, :, n:wide] = tail
        for k, slot, corner in ((1, rows + 4, 0), (2, rows + 5, 2)):
            dst[slot, :, 0:n] = row_src[0, k]
            dst[slot, :, n:wide] = cor_src[0, corner]

    def tail_of(x, r):
        return pltpu.roll(x, (126 - 4 * r) % LANES, 1)

    def shift_next(x):
        return pltpu.roll(x, wide - 1, 1)

    def shift_back(x):
        return pltpu.roll(x, 1, 1)

    edges_p, edges_v, edges_y = hlp[0], hlv[0], hly[0]
    zero = jnp.zeros((8, LANES), F32)
    parts = [slice(c * LANES, (c + 1) * LANES) for c in range(wide // LANES)]

    ln, row = lane_iota((rows, LANES)), lax.broadcasted_iota(jnp.int32, (rows, LANES), 0)
    tails = lane_gather(jnp.broadcast_to(hlb[0, 0:1, :], (rows, LANES)), (ln + 4 * row + 2) % LANES)
    depth[...] = jnp.zeros(depth.shape, F32)
    depth[8 : 8 + rows, 0:n] = b_ref[0]
    depth[8 : 8 + rows, n:wide] = tails
    for at, k, corner in ((6, 0, None), (7, 1, 1), (8 + rows, 2, 3), (9 + rows, 3, None)):
        depth[at : at + 1, 0:n] = hrb[0, k : k + 1, :]
        if corner is not None:
            depth[at : at + 1, n:wide] = hcb[0, corner, 0:1, :]
    between_rows = 0.5 * (depth[0 : rows + 16, :] + depth[1 : rows + 17, :])
    own = depth[8 : 8 + rows, :]
    along_own = 0.5 * (own + shift_next(own))
    for c, cut in enumerate(parts):
        bi[c] = between_rows[:, cut]
        bj[c, 8 : 8 + rows, :] = along_own[:, cut]
    for at, k, corner in ((7, 1, 0), (8 + rows, 2, 2)):
        x = jnp.concatenate([jnp.broadcast_to(hrb[0, k : k + 1, :], (8, n)), hcb[0, corner]], axis=1)
        x = 0.5 * (x + shift_next(x))
        for c, cut in enumerate(parts):
            bj[c, at : at + 1, :] = x[0:1, cut]

    def spread(ref, at):
        return jnp.concatenate([ref[c, pl.ds(at, 8, stride=0), :] for c in range(len(parts))], axis=1)

    for r in range(rows):
        sp[r + 2, :, 0:n] = p_ref[0, r]
        sp[r + 2, :, n:wide] = tail_of(edges_p, r)
        sv[r + 2, :, 0:n] = v_ref[0, r]
        sv[r + 2, :, n:wide] = tail_of(edges_v, r)
        ty[r] = tail_of(edges_y, r)

    def lap(ref, at, flat, bases, outs, by_i, by_j, count):
        for h in range(halves):
            part = slice(8 * h, 8 * h + 8)
            here = ref[at, part]
            before = spread(bi, at + 5) * (here - ref[at - 1, part])
            for u in range(count):
                after_row = ref[at + u + 1, part]
                step_i = after_row - here
                if by_i is not None:
                    by_i[at + u - 1, part] = step_i[:, 0:n]
                after = spread(bi, at + u + 6) * step_i
                line = here if flat is None else ref[flat, part]
                step_j = shift_next(line) - line
                if by_j is not None:
                    by_j[at + u - 2, part] = step_j
                along = spread(bj, at + u + 6) * step_j
                out = after - before + along - shift_back(along)
                if bases is not None:
                    out = out + bases(u, part)
                outs[at + u - 1, part] = out
                here, before = after_row, after

    def halo_y(k):
        return lambda u, part: jnp.concatenate([hry[0, k, part, :], zero], axis=1)

    lap(sp, 1, rows + 4, halo_y(0), sy, ip, None, 1)
    lap(sv, 1, rows + 4, None, sz, iv, None, 1)
    lap(sp, rows + 2, rows + 5, halo_y(1), sy, None, None, 1)
    lap(sv, rows + 2, rows + 5, None, sz, None, None, 1)

    group = GROUP

    def lap_rows(i, carry):
        r = i * group

        def own_y(u, part):
            return jnp.concatenate([y_ref[0, r + u, part, :], ty[r + u, part]], axis=1)

        lap(sp, r + 2, None, own_y, sy, ip, jp, group)
        lap(sv, r + 2, None, None, sz, iv, jv, group)
        return carry

    lax.fori_loop(0, rows // group, lap_rows, 0)

    def between(k):
        total = None
        for h in range(halves):
            part = slice(8 * h, 8 * h + 8)
            term = iv[k, part] * (sy[k + 1, part, 0:n] - sy[k, part, 0:n])
            term += ip[k, part] * (sz[k + 1, part, 0:n] - sz[k, part, 0:n])
            total = term if total is None else total + term
        return total

    def along_row(r):
        total = None
        for h in range(halves):
            part = slice(8 * h, 8 * h + 8)
            y, z = sy[r + 1, part], sz[r + 1, part]
            term = jv[r, part] * (shift_next(y) - y) + jp[r, part] * (shift_next(z) - z)
            total = term if total is None else total + term
        return (total + shift_back(total))[:, 0:n]

    def products(i, before):
        r = i * group
        for u in range(group):
            after = between(r + u + 1)
            acc[r + u] = before + after + along_row(r + u)
            before = after
        return before

    lax.fori_loop(0, rows // group, products, between(0))

    x = acc[...].reshape(8 * rows, n)
    at_row = lax.broadcasted_iota(jnp.int32, (rows, 8 * rows), 0)
    ones = (lax.broadcasted_iota(jnp.int32, (rows, 8 * rows), 1) // 8 == at_row).astype(F32).astype(jnp.bfloat16)
    hi = x.astype(jnp.bfloat16)
    rest = x - hi.astype(F32)
    lo = rest.astype(jnp.bfloat16)
    total = jnp.dot(ones, hi, preferred_element_type=F32) + jnp.dot(ones, lo, preferred_element_type=F32)
    g_ref[0] = (-0.5 * STEP_FACTOR * STEP_FACTOR * scale) * total


def main(scale, begin, count, fields, depth, halo):
    _, rows, layers, n = fields[0].shape
    wide = n + LANES
    block = lambda x: pl.BlockSpec((1,) + x.shape[1:], lambda p: (p + begin,) + (0,) * (x.ndim - 1))
    operands = [*fields, depth, *halo]
    return pl.pallas_call(
        functools.partial(main_kernel, layers, scale),
        grid=(count,),
        in_specs=[block(x) for x in operands],
        out_specs=pl.BlockSpec((1, rows, n), lambda p: (p, 0, 0)),
        out_shape=jax.ShapeDtypeStruct((count, rows, n), F32),
        scratch_shapes=[
            pltpu.VMEM((rows + 6, layers, wide), F32),
            pltpu.VMEM((rows + 6, layers, wide), F32),
            pltpu.VMEM((rows + 2, layers, wide), F32),
            pltpu.VMEM((rows + 2, layers, wide), F32),
            pltpu.VMEM((rows + 1, layers, n), F32),
            pltpu.VMEM((rows + 1, layers, n), F32),
            pltpu.VMEM((rows, layers, wide), F32),
            pltpu.VMEM((rows, layers, wide), F32),
            pltpu.VMEM((rows, layers, LANES), F32),
            pltpu.VMEM((rows + 24, wide), F32),
            pltpu.VMEM((wide // LANES, rows + 16, LANES), F32),
            pltpu.VMEM((wide // LANES, rows + 16, LANES), F32),
            pltpu.VMEM((rows, 8, n), F32),
        ],
        compiler_params=pltpu.CompilerParams(vmem_limit_bytes=VMEM),
        cost_estimate=pl.CostEstimate(
            flops=count * rows * layers * wide * 60, bytes_accessed=count * rows * layers * n * 16, transcendentals=0
        ),
        name="main",
    )(*operands)


def body(bathymetry, initial_state, patterns, pattern_index, coupling, final_weights):
    tiles, samples = lax.axis_size("tile"), lax.axis_size("samp")
    layers, panels, rows, n = initial_state.shape
    weights = final_weights[0]
    mixing = jnp.eye(layers, dtype=F32) + coupling

    def cat(matrix):
        high = lax.reduce_precision(matrix, 8, 7)
        low = matrix - high
        return jnp.concatenate([high, low, high], axis=1).astype(jnp.bfloat16)

    fwd, bwd = cat(mixing), cat(mixing.T)
    sel = (pattern_index[0][:, None] == jnp.arange(8, dtype=jnp.int32)[None, :]).astype(jnp.bfloat16)

    em, low, high, mm, aa = pack(tiles, initial_state, weights, patterns, bathymetry)
    ring = [(i, (i + 1) % tiles) for i in range(tiles)]
    west = lax.ppermute(high, "tile", ring)
    east = lax.ppermute(low, "tile", [(j, i) for i, j in ring])
    mirrored = lax.ppermute(mm, "tile", [(i, tiles - 1 - i) for i in range(tiles)])
    windows = lax.all_to_all(aa, "tile", 0, 0, tiled=True)
    fields = mix_all(initial_state, weights, patterns, fwd, bwd, sel)
    halo = halos(tiles, layers, rows, west, east, em, mirrored, windows, fwd, bwd, sel)
    totals = []
    for begin, end in ((0, panels - 1), (panels - 1, panels)):
        part = main(1.0 / samples, begin, end - begin, fields, bathymetry, halo)
        if samples == 2:
            totals.append(part + lax.ppermute(part, "samp", [(0, 1), (1, 0)]))
        else:
            totals.append(lax.psum(part, "samp"))
    return jnp.concatenate(totals, axis=0)


def solution(mesh):
    in_specs = (
        P(None, "tile", None),
        P(None, None, "tile", None),
        P(None, None, "tile", None),
        P("samp", None),
        P(),
        P("samp", None, None, "tile", None),
    )
    return jax.shard_map(body, mesh=mesh, in_specs=in_specs, out_specs=P(None, "tile", None), check_vma=False)
```

```python
import functools

import jax
import jax.numpy as jnp
from jax import lax
from jax.experimental import pallas as pl
from jax.experimental.pallas import tpu as pltpu
from jax.sharding import PartitionSpec as P

STEP_FACTOR = 0.1
LANES = 128
GROUP = 4
CH = 40
F32 = jnp.float32


def lane_iota(shape):
    return lax.broadcasted_iota(jnp.int32, shape, len(shape) - 1)


def lane_gather(x, idx):
    return jnp.take_along_axis(x, idx, axis=1, mode="promise_in_bounds")


def mix(cat, x):
    hi = x.astype(jnp.bfloat16)
    lo = (x - hi.astype(F32)).astype(jnp.bfloat16)
    return jnp.dot(cat, jnp.concatenate([hi, hi, lo], axis=0), preferred_element_type=F32)


STRIDED = True
VMEM = 60 * 1024 * 1024


def layer_rows(ref, r):
    size, rows = ref.shape[0], ref.shape[2]
    if not STRIDED:
        return ref[:, 0, r, :]
    return ref.reshape(size * rows, LANES)[pl.ds(r, size, stride=rows), :]


def pack_kernel(tiles, blocks, layers, npat, *refs):
    s_refs, w_refs, pat_refs = (refs[k * blocks : (k + 1) * blocks] for k in range(3))
    b_ref, em_ref, lo_ref, hi_ref, mm_ref, aa_ref, aux = refs[3 * blocks :]
    rows = b_ref.shape[1]
    p = pl.program_id(0)
    place = lax.axis_index("tile")
    first, final = place == 0, place == tiles - 1
    aux[...] = jnp.zeros(aux.shape, F32)
    for c in range(blocks):
        aux[c, 0:npat, 0] = pat_refs[c][:, 0].astype(F32)
        aux[c, npat, 0] = b_ref[0, :, c * LANES : (c + 1) * LANES]
    groups = (
        (0, layers, s_refs),
        (layers, layers, w_refs),
        (2 * layers, 8, [aux.at[c] for c in range(blocks)]),
    )
    for at, size, parts in groups:
        for c in range(blocks):
            cut = slice(c * LANES, (c + 1) * LANES)
            for k in range(2):
                lo_ref[0, k, at : at + size, cut] = layer_rows(parts[c], k)
                hi_ref[0, k, at : at + size, cut] = layer_rows(parts[c], rows - 2 + k)

    for at, size, parts in groups:
        shape = (8 * size, LANES)
        ln, row = lane_iota(shape), lax.broadcasted_iota(jnp.int32, shape, 0) % 8
        source = (ln % 4 + LANES - 2) % LANES
        total = jnp.zeros(shape, F32)
        for g in range(rows // 8):
            cut = slice(8 * g, 8 * g + 8)
            head = parts[0][:, 0, cut, :].reshape(shape)
            tail = parts[blocks - 1][:, 0, cut, :].reshape(shape)
            spread = lane_gather(jnp.where(ln < LANES // 2, head, tail), source)
            total = jnp.where(ln // 4 == 8 * g + row, spread, total)
        em_ref[0, at : at + size, :] = jnp.sum(total.reshape(size, 8, LANES), axis=1)

    lane = lane_iota((CH, LANES))
    side = lane % 4
    pad = jnp.zeros((LANES - CH, LANES), F32)

    @pl.when(p == 0)
    def _():
        aa_ref[...] = jnp.zeros(aa_ref.shape, F32)

    @pl.when(p == 1)
    def _():
        aa_ref[tiles - 1, 0:CH, :] = em_ref[0]
        mm_ref[2] = em_ref[0]

    @pl.when(p == 2)
    def _():
        mm_ref[0] = em_ref[0]

    @pl.when(p == 3)
    def _():
        aa_ref[0, 0:CH, :] = em_ref[0]

    @pl.when((p == 3) & jnp.logical_not(first))
    def _():
        mm_ref[2] = em_ref[0]

    @pl.when(p == 4)
    def _():
        mm_ref[1] = em_ref[0]

    per = LANES // rows

    def pole(ref, near, far, backward, is_five):
        for block in range(blocks):
            cut = slice(block * LANES, (block + 1) * LANES)
            x, y = ref[0, near, :, cut], ref[0, far, :, cut]
            turned = jnp.concatenate([x, pad], axis=0).T
            for q in range(per):
                if backward:
                    t = (blocks - 1 - block) * per + q
                    idx = LANES - 1 - q * rows - lane // 4
                else:
                    t = block * per + q
                    idx = q * rows + lane // 4
                idx = jnp.clip(idx, 0, LANES - 1)
                a, b = lane_gather(x, idx), lane_gather(y, idx)
                if is_five:
                    aa_ref[t, 0:CH, :] = jnp.where(side == 1, a, jnp.where(side == 0, b, aa_ref[t, 0:CH, :]))
                else:
                    aa_ref[t, 0:CH, :] = jnp.where(side == 2, a, b)
                low, high = q * rows, (q + 1) * rows - 1
                if backward:
                    before, at_before = tiles - block * per - q, low
                    after, at_after = tiles - 1 - block * per - (q + 1), high
                else:
                    before, at_before = block * per + q + 1, high
                    after, at_after = block * per + q - 1, low
                m = CH if is_five else CH + 1
                if before < tiles:
                    aa_ref[before, m : m + 1, :] = turned[at_before : at_before + 1, :]
                if after >= 0:
                    aa_ref[after, m + 2 : m + 3, :] = turned[at_after : at_after + 1, :]

    for panel in (4, 5):
        @pl.when((p == panel) & first)
        def _(panel=panel):
            pole(lo_ref, 0, 1, panel == 4, panel == 5)

        @pl.when((p == panel) & final)
        def _(panel=panel):
            pole(hi_ref, 1, 0, panel == 5, panel == 5)

    @pl.when(p == 5)
    def _():
        mm_ref[1] = jnp.where(side < 2, mm_ref[1], em_ref[0])
        for k in range(2):
            turned = jnp.concatenate([mm_ref[k], pad], axis=0).T
            m = CH + 4 + 2 * k

            @pl.when(jnp.logical_not(first))
            def _(turned=turned, m=m):
                aa_ref[tiles - place, m : m + 2, :] = turned[1:3, :]

            @pl.when(jnp.logical_not(final))
            def _(turned=turned, m=m):
                at = 4 * (rows - 1) + 1
                aa_ref[tiles - 2 - place, m : m + 2, :] = turned[at : at + 2, :]


def pack(tiles, s, w, pat, b):
    layers, panels, rows, n = s.shape
    npat, blocks = pat.shape[0], n // LANES
    full = lambda *shape: pl.BlockSpec(shape, lambda p: (0,) * len(shape))
    part = lambda size, c: pl.BlockSpec((size, 1, rows, LANES), lambda p: (0, p, 0, c))
    line = pl.BlockSpec((1, 2, CH, n), lambda p: (p, 0, 0, 0))
    return pl.pallas_call(
        functools.partial(pack_kernel, tiles, blocks, layers, npat),
        grid=(panels,),
        in_specs=[part(size, c) for size in (layers, layers, npat) for c in range(blocks)]
        + [pl.BlockSpec((1, rows, n), lambda p: (p, 0, 0))],
        out_specs=[
            pl.BlockSpec((1, CH, LANES), lambda p: (p, 0, 0)),
            line,
            line,
            full(3, CH, LANES),
            full(tiles, CH + 8, LANES),
        ],
        out_shape=[
            jax.ShapeDtypeStruct((panels, CH, LANES), F32),
            jax.ShapeDtypeStruct((panels, 2, CH, n), F32),
            jax.ShapeDtypeStruct((panels, 2, CH, n), F32),
            jax.ShapeDtypeStruct((3, CH, LANES), F32),
            jax.ShapeDtypeStruct((tiles, CH + 8, LANES), F32),
        ],
        scratch_shapes=[pltpu.VMEM((blocks, 8, 1, rows, LANES), F32)],
        compiler_params=pltpu.CompilerParams(vmem_limit_bytes=VMEM),
        name="pack",
    )(*[s] * blocks, *[w] * blocks, *[pat] * blocks, b)


def mix_kernel(s_ref, w_ref, pat_ref, fwd_ref, bwd_ref, sel_ref, p_ref, v_ref, y_ref, left_s, left_w, left_f, pf):
    layers, n = s_ref.shape[0], s_ref.shape[3]
    npat, rows = pat_ref.shape[0], pat_ref.shape[2]
    size = 8 * layers

    @pl.when(pl.program_id(0) == 0)
    def _():
        def spread(matrix, count):
            down = lax.broadcasted_iota(jnp.int32, (size, layers), 0) % layers
            down = (down == lax.broadcasted_iota(jnp.int32, (size, layers), 1)).astype(F32).astype(jnp.bfloat16)
            over = lax.broadcasted_iota(jnp.int32, (count, 8 * count), 1) // 8
            over = (over == lax.broadcasted_iota(jnp.int32, (count, 8 * count), 0)).astype(F32).astype(jnp.bfloat16)
            x = jnp.dot(down, matrix, preferred_element_type=F32).astype(jnp.bfloat16)
            x = jnp.dot(x, over, preferred_element_type=F32)
            same = lax.broadcasted_iota(jnp.int32, x.shape, 0) // layers
            same = same == lax.broadcasted_iota(jnp.int32, x.shape, 1) % 8
            return jnp.where(same, x, 0.0).astype(jnp.bfloat16)

        def parts(ref):
            return spread(ref[:, 0:layers], layers), spread(ref[:, layers : 2 * layers], layers)

        eye = lax.broadcasted_iota(jnp.int32, (layers, layers), 0) == lax.broadcasted_iota(
            jnp.int32, (layers, layers), 1
        )
        thirty = spread(jnp.where(eye, 30.0, 0.0).astype(jnp.bfloat16), layers)
        high, low = parts(fwd_ref)
        for k, x in enumerate((high, low, thirty)):
            left_s[k * size : (k + 1) * size, :] = jnp.concatenate([x, x], axis=1)
        for k, x in enumerate(parts(bwd_ref)):
            left_w[k * size : (k + 1) * size, :] = jnp.concatenate([x, x], axis=1)
        left_f[...] = spread(sel_ref[...], 8)

    pf[...] = jnp.zeros(pf.shape, F32)
    pf[0:npat] = pat_ref[:, 0].astype(F32)

    def pieces(x):
        hi = x.astype(jnp.bfloat16)
        return jnp.concatenate([hi, (x - hi.astype(F32)).astype(jnp.bfloat16)], axis=0)

    def dot(a, b):
        return jnp.dot(a, b, preferred_element_type=F32)

    step = min(n, 256)
    for g in range(rows // 8):
        own = slice(8 * g, 8 * g + 8)
        for at in range(0, n, step):
            cut = slice(at, at + step)
            x = dot(left_s[...], pieces(s_ref[:, 0, own, cut].reshape(size, step)))
            f = dot(left_f[...], pf[:, own, cut].reshape(64, step).astype(jnp.bfloat16))
            p_ref[0, own, :, cut] = (x[0:size] + x[size : 2 * size]).reshape(8, layers, step)
            y_ref[0, own, :, cut] = (x[2 * size :] + f).reshape(8, layers, step)
            x = dot(left_w[...], pieces(w_ref[:, 0, own, cut].reshape(size, step)))
            v_ref[0, own, :, cut] = (x[0:size] + x[size:]).reshape(8, layers, step)


def mix_all(s, w, pat, fwd, bwd, sel):
    layers, panels, rows, n = s.shape
    npat = pat.shape[0]
    full = lambda x: pl.BlockSpec(x.shape, lambda p: (0,) * x.ndim)
    part = lambda count: pl.BlockSpec((count, 1, rows, n), lambda p: (0, p, 0, 0))
    out = pl.BlockSpec((1, rows, layers, n), lambda p: (p, 0, 0, 0))
    size = layers * panels * rows * n * 4
    wide = 8 * layers
    return pl.pallas_call(
        mix_kernel,
        grid=(panels,),
        in_specs=[part(layers), part(layers), part(npat), full(fwd), full(bwd), full(sel)],
        out_specs=[out] * 3,
        out_shape=[jax.ShapeDtypeStruct((panels, rows, layers, n), F32)] * 3,
        scratch_shapes=[
            pltpu.VMEM((3 * wide, 2 * wide), jnp.bfloat16),
            pltpu.VMEM((2 * wide, 2 * wide), jnp.bfloat16),
            pltpu.VMEM((wide, 64), jnp.bfloat16),
            pltpu.VMEM((8, rows, n), F32),
        ],
        compiler_params=pltpu.CompilerParams(vmem_limit_bytes=VMEM),
        cost_estimate=pl.CostEstimate(flops=size * 48, bytes_accessed=5 * size, transcendentals=0),
        name="mix",
    )(s, w, pat, fwd, bwd, sel)


def halo_kernel(
    tiles, layers, rows,
    west_ref, east_ref, em_ref, mm_ref, aa_ref, fwd_ref, bwd_ref, sel_ref,
    hrp_ref, hrv_ref, hry_ref, hrb_ref, fix_ref,
    line,
):
    panels, n = west_ref.shape[0], west_ref.shape[3]
    place = lax.axis_index("tile")
    first, final = place == 0, place == tiles - 1
    fwd, bwd, sel = fwd_ref[...], bwd_ref[...], sel_ref[...]
    lane = lane_iota((CH, LANES))
    side = lane % 4
    blocks = n // LANES
    per = LANES // rows

    for p in range(panels):
        @pl.when(jnp.logical_not(first))
        def _(p=p):
            line[p, 0:2] = west_ref[p]

        @pl.when(jnp.logical_not(final))
        def _(p=p):
            line[p, 2:4] = east_ref[p]

        if p < 4:
            @pl.when(first)
            def _(p=p):
                line[p, 0:2] = west_ref[(p + 3) % 4]

            @pl.when(final)
            def _(p=p):
                line[p, 2:4] = east_ref[(p + 1) % 4]

    def collect(u_of, dest, k, backward):
        within = lane % rows
        idx = 4 * (rows - 1 - within) + k if backward else 4 * within + k
        p, at = dest
        for block in range(blocks):
            out = jnp.zeros((CH, LANES), F32)
            for q in range(per):
                u = block * per + q
                u = tiles - 1 - u if backward else u
                out = jnp.where(lane // rows == q, lane_gather(u_of(u), idx), out)
            line[p, at, :, block * LANES : (block + 1) * LANES] = out

    @pl.when(first)
    def _():
        def of(u):
            return em_ref[3] if u == 0 else mm_ref[2] if u == tiles - 1 else aa_ref[u, 0:CH, :]

        collect(of, (4, 1), 1, True)
        collect(of, (4, 0), 0, True)
        collect(of, (5, 1), 2, False)
        collect(of, (5, 0), 3, False)

    @pl.when(final)
    def _():
        def of(u):
            return mm_ref[2] if u == 0 else em_ref[1] if u == tiles - 1 else aa_ref[u, 0:CH, :]

        collect(of, (4, 2), 1, False)
        collect(of, (4, 3), 0, False)
        collect(of, (5, 2), 2, True)
        collect(of, (5, 3), 3, True)

    def force(x):
        return (3.0 / STEP_FACTOR) * x[0:layers] + jnp.dot(
            sel, x[2 * layers : CH].astype(jnp.bfloat16), preferred_element_type=F32
        )

    for p in range(panels):
        for k in range(4):
            x = line[p, k]
            hrp_ref[p, k] = mix(fwd, x[0:layers])
            hrv_ref[p, k] = mix(bwd, x[layers : 2 * layers])
            hrb_ref[p, k : k + 1, :] = line[p, k, CH - 4 : CH - 3, :]
            if k in (1, 2):
                hry_ref[p, k - 1] = force(x)

    span = 4 * rows
    turn = jnp.where(lane < span, span - 1 - lane, 0)
    back0 = lane_gather(mm_ref[0], turn)
    back1 = lane_gather(mm_ref[1], turn)
    columns = (
        jnp.where(side < 2, em_ref[5], em_ref[4]),
        aa_ref[tiles - 1, 0:CH, :],
        back1,
        aa_ref[0, 0:CH, :],
        jnp.where(side < 2, em_ref[0], back0),
        jnp.where(side < 2, back0, em_ref[0]),
    )
    at_end = lane == LANES - 1
    pad = jnp.zeros((LANES - 8, LANES), F32)
    mirrored = [
        jnp.concatenate([aa_ref[u, CH:, :], pad], axis=0).T[0:CH]
        for u in (jnp.minimum(tiles - place, tiles - 1), jnp.maximum(tiles - 2 - place, 0))
    ]
    ln = lane_iota((layers, LANES))
    k_of, r_of = ln % 4, ln // 4
    end = ln == LANES - 1
    depth_at = CH - 4

    def mixed(x):
        depth = jnp.broadcast_to(x[depth_at : depth_at + 1], (layers, LANES))
        return mix(fwd, x[0:layers]), mix(bwd, x[layers : 2 * layers]), depth

    def turn(x, by):
        return pltpu.roll(x, by % LANES, 1)

    def fold(x):
        return jnp.sum(x, axis=0, keepdims=True)

    for p in range(panels):
        raw = columns[p]
        if p in (1, 3):
            turned = jnp.concatenate([aa_ref[tiles - 1 if p == 1 else 0, CH:, :], pad], axis=0).T[0:CH]
        outer, inner_own = mixed(raw), mixed(em_ref[p])
        force_outer, force_own = force(raw), force(em_ref[p])
        beyond = []
        for edge in range(2):
            at = 1 + edge
            at_cut = lambda q, block: line[q, at, :, block * LANES : (block + 1) * LANES]
            beside = lambda k: lane_gather(mirrored[edge], jnp.where(at_end, 5 + 2 * k, 4 + 2 * k))
            if p == 0:
                inner = jnp.where(at_end, at_cut(5, blocks - 1), at_cut(4, 0))
            elif p == 2:
                inner = beside(1)
            elif p == 4:
                inner = jnp.where(at_end, at_cut(0, blocks - 1), beside(0))
            elif p == 5:
                inner = jnp.where(at_end, beside(0), at_cut(0, 0))
            else:
                inner = lane_gather(turned, jnp.where(at_end, 2 * edge, 2 * edge + 1))
            own_row = 0 if edge == 0 else rows - 1
            across = turn(raw, 126 - 4 * own_row)
            along = jnp.where(at_end, turn(at_cut(p, 0), LANES - 1), turn(at_cut(p, blocks - 1), 1))
            corner = first if edge == 0 else final
            sideways = mixed(jnp.where(corner, across, inner))
            onward = mixed(jnp.where(corner, along, inner))
            head, tail = mixed(at_cut(p, 0)), mixed(at_cut(p, blocks - 1))
            base = 4 * own_row
            here = [
                [turn(jnp.where(end, o, h), base + 2) for o, h in zip(onward, head)],
                [turn(jnp.where(end, t, o), base + 2) for o, t in zip(onward, tail)],
            ]
            lateral = [[turn(x, base + 3) for x in sideways], [turn(x, base + 1) for x in sideways]]
            beyond.append((here, lateral))
        total = None
        for right in range(2):
            own_k = 1 if right else 2
            halves = (inner_own, outer) if right else (outer, inner_own)
            q, v, b = (jnp.where(k_of < 2, x, y) for x, y in zip(*halves))
            y0 = jnp.where(k_of < 2, *((force_own, force_outer) if right else (force_outer, force_own)))
            (here_m, lat_m), (here_p, lat_p) = [(h[right], t[right]) for h, t in beyond]
            at_first, at_last, is_own = r_of == 0, r_of == rows - 1, k_of == own_k
            bj = 0.5 * (b + turn(b, -1))
            bi = 0.5 * (b + jnp.where(at_last, here_p[2], turn(b, -4)))
            bi_m = 0.5 * (b + here_m[2])
            laps, di, dj, extra, extra_m, extra_p, di_m = [], [], [], [], [], [], []
            for f, x in enumerate((q, v)):
                step_i = jnp.where(at_last, here_p[f], turn(x, -4)) - x
                step_m = x - here_m[f]
                step_j = turn(x, -1) - x
                flow_i, flow_j = bi * step_i, bj * step_j
                before = jnp.where(at_first, bi_m * step_m, turn(flow_i, 4))
                laps.append(flow_i - before + flow_j - turn(flow_j, 1))
                cross = flow_j if right else -turn(flow_j, 1)
                extra.append(jnp.where(is_own, cross, 0.0))
                extra_m.append(0.5 * (here_m[2] + lat_m[2]) * (lat_m[f] - here_m[f]))
                extra_p.append(0.5 * (here_p[2] + lat_p[2]) * (lat_p[f] - here_p[f]))
                di.append(step_i)
                di_m.append(step_m)
                dj.append(step_j)
            y, z = y0 + laps[0], laps[1]
            cross_edge = fold(dj[1] * (turn(y, -1) - y) + (turn(z, -1) - z) * dj[0])
            after = [jnp.where(at_last, e, turn(x, -4)) for x, e in zip(extra, extra_p)]
            along_i = fold(di[1] * (after[0] - extra[0]) + di[0] * (after[1] - extra[1]))
            along_m = fold(di_m[1] * (extra[0] - extra_m[0]) + di_m[0] * (extra[1] - extra_m[1]))
            if right:
                inside = fold(dj[1] * turn(extra[0], -1) + dj[0] * turn(extra[1], -1))
            else:
                inside = -fold(dj[1] * extra[0] + dj[0] * extra[1])
            k1, r1 = k_of[0:1], r_of[0:1]
            whole = along_i + jnp.where(r1 == 0, along_m, turn(along_i, 4))
            if right:
                whole = whole + cross_edge + turn(inside, 1)
                result = jnp.where(k1 == 1, whole, inside)
            else:
                whole = whole + turn(cross_edge, 1) + inside
                result = jnp.where(k1 == 2, whole, turn(inside, 1))
            if right:
                total = jnp.where(k1 < 2, result, total)
            else:
                total = result
        fix_ref[p] = jnp.broadcast_to(total, (8, LANES))


def halos(tiles, layers, rows, west, east, em, mm, aa, fwd, bwd, sel):
    panels, n = west.shape[0], west.shape[3]
    shapes = [
        (panels, 4, layers, n), (panels, 4, layers, n), (panels, 2, layers, n), (panels, 8, n),
        (panels, 8, LANES),
    ]
    return pl.pallas_call(
        functools.partial(halo_kernel, tiles, layers, rows),
        out_shape=[jax.ShapeDtypeStruct(s, F32) for s in shapes],
        scratch_shapes=[pltpu.VMEM((panels, 4, CH, n), F32)],
        compiler_params=pltpu.CompilerParams(vmem_limit_bytes=VMEM),
        name="halos",
    )(west, east, em, mm, aa, fwd, bwd, sel)


def main_kernel(
    layers, scale,
    p_ref, v_ref, y_ref, b_ref,
    hrp, hrv, hry, hrb, fix,
    g_ref,
    sp, sv, sy, sz, ip, iv, jp, jv, depth, bi, bj, acc,
):
    rows, n = p_ref.shape[1], p_ref.shape[3]
    halves = layers // 8

    def shift_next(x):
        return pltpu.roll(x, n - 1, 1)

    def shift_back(x):
        return pltpu.roll(x, 1, 1)

    parts = [slice(c * LANES, (c + 1) * LANES) for c in range(n // LANES)]

    depth[...] = jnp.zeros(depth.shape, F32)
    depth[8 : 8 + rows, :] = b_ref[0]
    depth[6:8, :] = hrb[0, 0:2, :]
    depth[8 + rows : 10 + rows, :] = hrb[0, 2:4, :]
    all_rows = depth[0 : rows + 16, :]
    between_rows = 0.5 * (all_rows + depth[1 : rows + 17, :])
    along_rows = 0.5 * (all_rows + shift_next(all_rows))
    along_rows = jnp.where(lane_iota(along_rows.shape) == n - 1, 0.0, along_rows)
    for c, cut in enumerate(parts):
        bi[c] = between_rows[:, cut]
        bj[c] = along_rows[:, cut]

    def spread(ref, at):
        return jnp.concatenate([ref[c, pl.ds(at, 8, stride=0), :] for c in range(len(parts))], axis=1)

    for src, row_src, dst in ((p_ref, hrp, sp), (v_ref, hrv, sv)):
        for k, slot in enumerate((0, 1, rows + 2, rows + 3)):
            dst[slot] = row_src[0, k]
        for r in range(rows):
            dst[r + 2] = src[0, r]

    def lap(ref, at, bases, outs, by_i, by_j, count):
        for h in range(halves):
            part = slice(8 * h, 8 * h + 8)
            here = ref[at, part]
            before = spread(bi, at + 5) * (here - ref[at - 1, part])
            for u in range(count):
                after_row = ref[at + u + 1, part]
                step_i = after_row - here
                if by_i is not None:
                    by_i[at + u - 1, part] = step_i
                after = spread(bi, at + u + 6) * step_i
                step_j = shift_next(here) - here
                if by_j is not None:
                    by_j[at + u - 2, part] = step_j
                along = spread(bj, at + u + 6) * step_j
                out = after - before + along - shift_back(along)
                if bases is not None:
                    out = out + bases(u, part)
                outs[at + u - 1, part] = out
                here, before = after_row, after

    def halo_y(k):
        return lambda u, part: hry[0, k, part, :]

    lap(sp, 1, halo_y(0), sy, ip, None, 1)
    lap(sv, 1, None, sz, iv, None, 1)
    lap(sp, rows + 2, halo_y(1), sy, None, None, 1)
    lap(sv, rows + 2, None, sz, None, None, 1)

    group = GROUP

    def lap_rows(i, carry):
        r = i * group

        def own_y(u, part):
            return y_ref[0, r + u, part, :]

        lap(sp, r + 2, own_y, sy, ip, jp, group)
        lap(sv, r + 2, None, sz, iv, jv, group)
        return carry

    lax.fori_loop(0, rows // group, lap_rows, 0)

    def between(k):
        total = None
        for h in range(halves):
            part = slice(8 * h, 8 * h + 8)
            term = iv[k, part] * (sy[k + 1, part] - sy[k, part])
            term += ip[k, part] * (sz[k + 1, part] - sz[k, part])
            total = term if total is None else total + term
        return total

    def along_row(r):
        total = None
        for h in range(halves):
            part = slice(8 * h, 8 * h + 8)
            y, z = sy[r + 1, part], sz[r + 1, part]
            term = jv[r, part] * (shift_next(y) - y) + jp[r, part] * (shift_next(z) - z)
            total = term if total is None else total + term
        total = jnp.where(lane_iota(total.shape) == n - 1, 0.0, total)
        return total + shift_back(total)

    def products(i, before):
        r = i * group
        for u in range(group):
            after = between(r + u + 1)
            acc[r + u] = before + after + along_row(r + u)
            before = after
        return before

    lax.fori_loop(0, rows // group, products, between(0))

    x = acc[...].reshape(8 * rows, n)
    at_row = lax.broadcasted_iota(jnp.int32, (rows, 8 * rows), 0)
    ones = (lax.broadcasted_iota(jnp.int32, (rows, 8 * rows), 1) // 8 == at_row).astype(F32).astype(jnp.bfloat16)
    hi = x.astype(jnp.bfloat16)
    rest = x - hi.astype(F32)
    lo = rest.astype(jnp.bfloat16)
    total = jnp.dot(ones, hi, preferred_element_type=F32) + jnp.dot(ones, lo, preferred_element_type=F32)
    ln, row = lane_iota((rows, LANES)), lax.broadcasted_iota(jnp.int32, (rows, LANES), 0)
    edges = lane_gather(jnp.broadcast_to(fix[0, 0:1, :], (rows, LANES)), (ln + 4 * row + 2) % LANES)
    left = jnp.where(ln < 2, edges, 0.0)
    right = jnp.where(ln >= LANES - 2, edges, 0.0)
    columns = [total[:, cut] for cut in parts]
    columns[0] = columns[0] + left
    columns[-1] = columns[-1] + right
    total = jnp.concatenate(columns, axis=1)
    g_ref[0] = (-0.5 * STEP_FACTOR * STEP_FACTOR * scale) * total


def main(scale, begin, count, fields, depth, halo):
    _, rows, layers, n = fields[0].shape
    wide = n
    block = lambda x: pl.BlockSpec((1,) + x.shape[1:], lambda p: (p + begin,) + (0,) * (x.ndim - 1))
    operands = [*fields, depth, *halo]
    return pl.pallas_call(
        functools.partial(main_kernel, layers, scale),
        grid=(count,),
        in_specs=[block(x) for x in operands],
        out_specs=pl.BlockSpec((1, rows, n), lambda p: (p, 0, 0)),
        out_shape=jax.ShapeDtypeStruct((count, rows, n), F32),
        scratch_shapes=[
            pltpu.VMEM((rows + 4, layers, wide), F32),
            pltpu.VMEM((rows + 4, layers, wide), F32),
            pltpu.VMEM((rows + 2, layers, wide), F32),
            pltpu.VMEM((rows + 2, layers, wide), F32),
            pltpu.VMEM((rows + 1, layers, n), F32),
            pltpu.VMEM((rows + 1, layers, n), F32),
            pltpu.VMEM((rows, layers, wide), F32),
            pltpu.VMEM((rows, layers, wide), F32),
            pltpu.VMEM((rows + 24, wide), F32),
            pltpu.VMEM((wide // LANES, rows + 16, LANES), F32),
            pltpu.VMEM((wide // LANES, rows + 16, LANES), F32),
            pltpu.VMEM((rows, 8, n), F32),
        ],
        compiler_params=pltpu.CompilerParams(vmem_limit_bytes=VMEM),
        cost_estimate=pl.CostEstimate(
            flops=count * rows * layers * wide * 60, bytes_accessed=count * rows * layers * n * 16, transcendentals=0
        ),
        name="main",
    )(*operands)


def body(bathymetry, initial_state, patterns, pattern_index, coupling, final_weights):
    tiles, samples = lax.axis_size("tile"), lax.axis_size("samp")
    layers, panels, rows, n = initial_state.shape
    weights = final_weights[0]
    mixing = jnp.eye(layers, dtype=F32) + coupling

    def cat(matrix):
        high = lax.reduce_precision(matrix, 8, 7)
        low = matrix - high
        return jnp.concatenate([high, low, high], axis=1).astype(jnp.bfloat16)

    fwd, bwd = cat(mixing), cat(mixing.T)
    sel = (pattern_index[0][:, None] == jnp.arange(8, dtype=jnp.int32)[None, :]).astype(jnp.bfloat16)

    em, low, high, mm, aa = pack(tiles, initial_state, weights, patterns, bathymetry)
    ring = [(i, (i + 1) % tiles) for i in range(tiles)]
    west = lax.ppermute(high, "tile", ring)
    east = lax.ppermute(low, "tile", [(j, i) for i, j in ring])
    mirrored = lax.ppermute(mm, "tile", [(i, tiles - 1 - i) for i in range(tiles)])
    windows = lax.all_to_all(aa, "tile", 0, 0, tiled=True)
    fields = mix_all(initial_state, weights, patterns, fwd, bwd, sel)
    halo = halos(tiles, layers, rows, west, east, em, mirrored, windows, fwd, bwd, sel)
    totals = []
    for begin, end in ((0, panels - 1), (panels - 1, panels)):
        part = main(1.0 / samples, begin, end - begin, fields, bathymetry, halo)
        if samples == 2:
            totals.append(part + lax.ppermute(part, "samp", [(0, 1), (1, 0)]))
        else:
            totals.append(lax.psum(part, "samp"))
    return jnp.concatenate(totals, axis=0)


def solution(mesh):
    in_specs = (
        P(None, "tile", None),
        P(None, None, "tile", None),
        P(None, None, "tile", None),
        P("samp", None),
        P(),
        P("samp", None, None, "tile", None),
    )
    return jax.shard_map(body, mesh=mesh, in_specs=in_specs, out_specs=P(None, "tile", None), check_vma=False)
```

```python
import functools

import jax
import jax.numpy as jnp
from jax import lax
from jax.experimental import pallas as pl
from jax.experimental.pallas import tpu as pltpu
from jax.sharding import PartitionSpec as P


STEP_FACTOR = 0.1
LANES = 128
GROUP = 4
CH = 40
F32 = jnp.float32


def lane_iota(shape):
    return lax.broadcasted_iota(jnp.int32, shape, len(shape) - 1)


def lane_gather(x, idx):
    return jnp.take_along_axis(x, idx, axis=1, mode="promise_in_bounds")


def mix(cat, x):
    hi = x.astype(jnp.bfloat16)
    lo = (x - hi.astype(F32)).astype(jnp.bfloat16)
    return jnp.dot(cat, jnp.concatenate([hi, hi, lo], axis=0), preferred_element_type=F32)


STRIDED = True
VMEM = 60 * 1024 * 1024


def layer_rows(ref, r):
    size, rows = ref.shape[0], ref.shape[2]
    if not STRIDED:
        return ref[:, 0, r, :]
    return ref.reshape(size * rows, LANES)[pl.ds(r, size, stride=rows), :]


def pack_kernel(tiles, blocks, layers, npat, *refs):
    s_refs, w_refs, pat_refs = (refs[k * blocks : (k + 1) * blocks] for k in range(3))
    b_ref, em_ref, lo_ref, hi_ref, mm_ref, aa_ref, aux = refs[3 * blocks :]
    rows = b_ref.shape[1]
    p = pl.program_id(0)
    place = lax.axis_index("tile")
    first, final = place == 0, place == tiles - 1
    aux[...] = jnp.zeros(aux.shape, F32)
    for c in range(blocks):
        aux[c, 0:npat, 0] = pat_refs[c][:, 0].astype(F32)
        aux[c, npat, 0] = b_ref[0, :, c * LANES : (c + 1) * LANES]
    groups = (
        (0, layers, s_refs),
        (layers, layers, w_refs),
        (2 * layers, 8, [aux.at[c] for c in range(blocks)]),
    )
    for at, size, parts in groups:
        for c in range(blocks):
            cut = slice(c * LANES, (c + 1) * LANES)
            for k in range(2):
                lo_ref[0, k, at : at + size, cut] = layer_rows(parts[c], k)
                hi_ref[0, k, at : at + size, cut] = layer_rows(parts[c], rows - 2 + k)

    for at, size, parts in groups:
        shape = (8 * size, LANES)
        ln, row = lane_iota(shape), lax.broadcasted_iota(jnp.int32, shape, 0) % 8
        source = (ln % 4 + LANES - 2) % LANES
        total = jnp.zeros(shape, F32)
        for g in range(rows // 8):
            cut = slice(8 * g, 8 * g + 8)
            head = parts[0][:, 0, cut, :].reshape(shape)
            tail = parts[blocks - 1][:, 0, cut, :].reshape(shape)
            spread = lane_gather(jnp.where(ln < LANES // 2, head, tail), source)
            total = jnp.where(ln // 4 == 8 * g + row, spread, total)
        em_ref[0, at : at + size, :] = jnp.sum(total.reshape(size, 8, LANES), axis=1)

    lane = lane_iota((CH, LANES))
    side = lane % 4
    pad = jnp.zeros((LANES - CH, LANES), F32)

    @pl.when(p == 0)
    def _():
        aa_ref[...] = jnp.zeros(aa_ref.shape, F32)

    @pl.when(p == 1)
    def _():
        aa_ref[tiles - 1, 0:CH, :] = em_ref[0]
        mm_ref[2] = em_ref[0]

    @pl.when(p == 2)
    def _():
        mm_ref[0] = em_ref[0]

    @pl.when(p == 3)
    def _():
        aa_ref[0, 0:CH, :] = em_ref[0]

    @pl.when((p == 3) & jnp.logical_not(first))
    def _():
        mm_ref[2] = em_ref[0]

    @pl.when(p == 4)
    def _():
        mm_ref[1] = em_ref[0]

    per = LANES // rows

    def pole(ref, near, far, backward, is_five):
        for block in range(blocks):
            cut = slice(block * LANES, (block + 1) * LANES)
            x, y = ref[0, near, :, cut], ref[0, far, :, cut]
            turned = jnp.concatenate([x, pad], axis=0).T
            for q in range(per):
                if backward:
                    t = (blocks - 1 - block) * per + q
                    idx = LANES - 1 - q * rows - lane // 4
                else:
                    t = block * per + q
                    idx = q * rows + lane // 4
                idx = jnp.clip(idx, 0, LANES - 1)
                a, b = lane_gather(x, idx), lane_gather(y, idx)
                if is_five:
                    aa_ref[t, 0:CH, :] = jnp.where(side == 1, a, jnp.where(side == 0, b, aa_ref[t, 0:CH, :]))
                else:
                    aa_ref[t, 0:CH, :] = jnp.where(side == 2, a, b)
                low, high = q * rows, (q + 1) * rows - 1
                if backward:
                    before, at_before = tiles - block * per - q, low
                    after, at_after = tiles - 1 - block * per - (q + 1), high
                else:
                    before, at_before = block * per + q + 1, high
                    after, at_after = block * per + q - 1, low
                m = CH if is_five else CH + 1
                if before < tiles:
                    aa_ref[before, m : m + 1, :] = turned[at_before : at_before + 1, :]
                if after >= 0:
                    aa_ref[after, m + 2 : m + 3, :] = turned[at_after : at_after + 1, :]

    for panel in (4, 5):
        @pl.when((p == panel) & first)
        def _(panel=panel):
            pole(lo_ref, 0, 1, panel == 4, panel == 5)

        @pl.when((p == panel) & final)
        def _(panel=panel):
            pole(hi_ref, 1, 0, panel == 5, panel == 5)

    @pl.when(p == 5)
    def _():
        mm_ref[1] = jnp.where(side < 2, mm_ref[1], em_ref[0])
        for k in range(2):
            turned = jnp.concatenate([mm_ref[k], pad], axis=0).T
            m = CH + 4 + 2 * k

            @pl.when(jnp.logical_not(first))
            def _(turned=turned, m=m):
                aa_ref[tiles - place, m : m + 2, :] = turned[1:3, :]

            @pl.when(jnp.logical_not(final))
            def _(turned=turned, m=m):
                at = 4 * (rows - 1) + 1
                aa_ref[tiles - 2 - place, m : m + 2, :] = turned[at : at + 2, :]


def pack(tiles, s, w, pat, b):
    layers, panels, rows, n = s.shape
    npat, blocks = pat.shape[0], n // LANES
    full = lambda *shape: pl.BlockSpec(shape, lambda p: (0,) * len(shape))
    part = lambda size, c: pl.BlockSpec((size, 1, rows, LANES), lambda p: (0, p, 0, c))
    line = pl.BlockSpec((1, 2, CH, n), lambda p: (p, 0, 0, 0))
    return pl.pallas_call(
        functools.partial(pack_kernel, tiles, blocks, layers, npat),
        grid=(panels,),
        in_specs=[part(size, c) for size in (layers, layers, npat) for c in range(blocks)]
        + [pl.BlockSpec((1, rows, n), lambda p: (p, 0, 0))],
        out_specs=[
            pl.BlockSpec((1, CH, LANES), lambda p: (p, 0, 0)),
            line,
            line,
            full(3, CH, LANES),
            full(tiles, CH + 8, LANES),
        ],
        out_shape=[
            jax.ShapeDtypeStruct((panels, CH, LANES), F32),
            jax.ShapeDtypeStruct((panels, 2, CH, n), F32),
            jax.ShapeDtypeStruct((panels, 2, CH, n), F32),
            jax.ShapeDtypeStruct((3, CH, LANES), F32),
            jax.ShapeDtypeStruct((tiles, CH + 8, LANES), F32),
        ],
        scratch_shapes=[pltpu.VMEM((blocks, 8, 1, rows, LANES), F32)],
        compiler_params=pltpu.CompilerParams(vmem_limit_bytes=VMEM),
        name="pack",
    )(*[s] * blocks, *[w] * blocks, *[pat] * blocks, b)


def mix_kernel(
    s_ref, w_ref, pat_ref, mat_ref, index_ref,
    p_ref, v_ref, y_ref, fwd_ref, bwd_ref, sel_ref,
    left_s, left_w, left_f, pf,
):
    layers, n = s_ref.shape[0], s_ref.shape[3]
    npat, rows = pat_ref.shape[0], pat_ref.shape[2]
    size = 8 * layers
    half = jnp.bfloat16

    def matrices(_, carry):
        def iotas(shape):
            return (lax.broadcasted_iota(jnp.int32, shape, d) for d in range(2))

        def one(cond):
            return cond.astype(F32).astype(half)

        def product(a, b, flipped=False):
            dims = (((1,), (1 if flipped else 0,)), ((), ()))
            return lax.dot_general(a, b, dims, preferred_element_type=F32).astype(half)

        def spread(matrix, flipped=False):
            i, j = iotas((size, layers))
            x = product(one(i % layers == j), matrix, flipped)
            i, j = iotas((x.shape[1], 8 * x.shape[1]))
            x = jnp.dot(x, one(j // 8 == i), preferred_element_type=F32)
            i, j = iotas(x.shape)
            return jnp.where(i // layers == j % 8, x, 0.0).astype(half)

        i, j = iotas((layers, layers))
        eye = one(i == j)
        mixing = mat_ref[...] + eye.astype(F32)
        high = mixing.astype(half)
        low = (mixing - high.astype(F32)).astype(half)
        q = lax.broadcasted_iota(jnp.int32, (8, layers), 0)
        chosen = one(jnp.broadcast_to(index_ref[...], (8, layers)) == q)
        for k, x in enumerate((spread(high), spread(low), spread((30.0 * eye.astype(F32)).astype(half)))):
            left_s[k * size : (k + 1) * size, :] = jnp.concatenate([x, x], axis=1)
        for k, x in enumerate((spread(high, True), spread(low, True))):
            left_w[k * size : (k + 1) * size, :] = jnp.concatenate([x, x], axis=1)
        left_f[...] = spread(chosen, True)
        high_t, low_t = product(eye, high, True), product(eye, low, True)
        for k, (x, y) in enumerate(((high, high_t), (low, low_t), (high, high_t))):
            fwd_ref[:, k * layers : (k + 1) * layers] = x
            bwd_ref[:, k * layers : (k + 1) * layers] = y
        sel_ref[...] = product(eye, chosen, True)
        return carry

    start = (pl.program_id(0) == 0) & (pl.program_id(1) == 0)
    lax.fori_loop(0, jnp.where(start, 1, 0), matrices, 0)

    pf[...] = jnp.zeros(pf.shape, F32)
    pf[0:npat] = pat_ref[:, 0].astype(F32)

    def pieces(x):
        hi = x.astype(jnp.bfloat16)
        return jnp.concatenate([hi, (x - hi.astype(F32)).astype(jnp.bfloat16)], axis=0)

    def dot(a, b):
        return jnp.dot(a, b, preferred_element_type=F32)

    step = min(n, 256)
    for g in range(rows // 8):
        own = slice(8 * g, 8 * g + 8)
        for at in range(0, n, step):
            cut = slice(at, at + step)
            x = dot(left_s[...], pieces(s_ref[:, 0, own, cut].reshape(size, step)))
            f = dot(left_f[...], pf[:, own, cut].reshape(64, step).astype(jnp.bfloat16))
            p_ref[0, own, :, cut] = (x[0:size] + x[size : 2 * size]).reshape(8, layers, step)
            y_ref[0, own, :, cut] = (x[2 * size :] + f).reshape(8, layers, step)
            x = dot(left_w[...], pieces(w_ref[:, 0, own, cut].reshape(size, step)))
            v_ref[0, own, :, cut] = (x[0:size] + x[size:]).reshape(8, layers, step)


def mix_all(s, w, pat, matrix, index):
    layers, panels, rows, n = s.shape
    npat, each = pat.shape[0], rows
    full = lambda *shape: pl.BlockSpec(shape, lambda p, g: (0, 0))
    part = lambda count: pl.BlockSpec((count, 1, each, n), lambda p, g: (0, p, g, 0))
    out = pl.BlockSpec((1, each, layers, n), lambda p, g: (p, g, 0, 0))
    size = layers * panels * rows * n * 4
    wide = 8 * layers
    small = [(layers, 3 * layers), (layers, 3 * layers), (layers, 8)]
    *fields, fwd, bwd, sel = pl.pallas_call(
        mix_kernel,
        grid=(panels, rows // each),
        in_specs=[part(layers), part(layers), part(npat), full(layers, layers), full(1, layers)],
        out_specs=[out] * 3 + [full(*x) for x in small],
        out_shape=[jax.ShapeDtypeStruct((panels, rows, layers, n), F32)] * 3
        + [jax.ShapeDtypeStruct(x, jnp.bfloat16) for x in small],
        scratch_shapes=[
            pltpu.VMEM((3 * wide, 2 * wide), jnp.bfloat16),
            pltpu.VMEM((2 * wide, 2 * wide), jnp.bfloat16),
            pltpu.VMEM((wide, 64), jnp.bfloat16),
            pltpu.VMEM((8, each, n), F32),
        ],
        compiler_params=pltpu.CompilerParams(vmem_limit_bytes=VMEM),
        cost_estimate=pl.CostEstimate(flops=size * 48, bytes_accessed=5 * size, transcendentals=0),
        name="mix",
    )(s, w, pat, matrix, index)
    return fields, fwd, bwd, sel


def halo_kernel(
    tiles, layers, rows,
    west_ref, east_ref, low_ref, high_ref, em_ref, mm_ref, aa_ref, fwd_ref, bwd_ref, sel_ref,
    fix_ref,
    line, hrp_ref, hrv_ref, hrb_ref,
):
    panels, n = west_ref.shape[0], west_ref.shape[3]
    place = lax.axis_index("tile")
    first, final = place == 0, place == tiles - 1
    fwd, bwd, sel = fwd_ref[...], bwd_ref[...], sel_ref[...]
    lane = lane_iota((CH, LANES))
    side = lane % 4
    blocks = n // LANES
    per = LANES // rows

    for p in range(panels):
        @pl.when(jnp.logical_not(first))
        def _(p=p):
            line[p, 0:2] = west_ref[p]

        @pl.when(jnp.logical_not(final))
        def _(p=p):
            line[p, 2:4] = east_ref[p]

        if p < 4:
            @pl.when(first)
            def _(p=p):
                line[p, 0:2] = west_ref[(p + 3) % 4]

            @pl.when(final)
            def _(p=p):
                line[p, 2:4] = east_ref[(p + 1) % 4]

    def collect(u_of, dest, k, backward):
        within = lane % rows
        idx = 4 * (rows - 1 - within) + k if backward else 4 * within + k
        p, at = dest
        for block in range(blocks):
            out = jnp.zeros((CH, LANES), F32)
            for q in range(per):
                u = block * per + q
                u = tiles - 1 - u if backward else u
                out = jnp.where(lane // rows == q, lane_gather(u_of(u), idx), out)
            line[p, at, :, block * LANES : (block + 1) * LANES] = out

    @pl.when(first)
    def _():
        def of(u):
            return em_ref[3] if u == 0 else mm_ref[2] if u == tiles - 1 else aa_ref[u, 0:CH, :]

        collect(of, (4, 1), 1, True)
        collect(of, (4, 0), 0, True)
        collect(of, (5, 1), 2, False)
        collect(of, (5, 0), 3, False)

    @pl.when(final)
    def _():
        def of(u):
            return mm_ref[2] if u == 0 else em_ref[1] if u == tiles - 1 else aa_ref[u, 0:CH, :]

        collect(of, (4, 2), 1, False)
        collect(of, (4, 3), 0, False)
        collect(of, (5, 2), 2, True)
        collect(of, (5, 3), 3, True)

    def force(x):
        return (3.0 / STEP_FACTOR) * x[0:layers] + jnp.dot(
            sel, x[2 * layers : CH].astype(jnp.bfloat16), preferred_element_type=F32
        )

    def fold(x):
        return sum(x[k : k + 8] for k in range(0, layers, 8))

    def shift_next(x):
        return pltpu.roll(x, n - 1, 1)

    def shift_back(x):
        return pltpu.roll(x, 1, 1)

    last_lane = lane_iota((1, n)) == n - 1

    def row_edges(p, carry):
        fix_ref[p] = jnp.zeros((8, n), F32)
        for bottom in range(2):
            own = 1 if bottom else 2
            far = 2 if bottom else 1
            lines = (high_ref, line) if bottom else (line, low_ref)
            raw = [lines[0].at[p, 0], lines[0].at[p, 1]]
            raw += [line.at[p, 2], line.at[p, 3]] if bottom else [low_ref.at[p, 0], low_ref.at[p, 1]]
            fields = (
                [mix(fwd, x[0:layers, :]) for x in raw],
                [mix(bwd, x[layers : 2 * layers, :]) for x in raw],
            )
            bases = {k: force(raw[k][...]) for k in (1, 2)}
            depth = [x[CH - 4 : CH - 3, :] for x in raw]
            hrp_ref[p, bottom], hrv_ref[p, bottom] = fields[0][far], fields[1][far]
            hrb_ref[p, bottom : bottom + 1, :] = depth[far]
            wi = [0.5 * (depth[k] + depth[k + 1]) for k in range(3)]
            wj = {k: jnp.where(last_lane, 0.0, 0.5 * (depth[k] + shift_next(depth[k]))) for k in (1, 2)}
            steps, sides, flows, laps = [], [], [], []
            for x in fields:
                step = [x[k + 1] - x[k] for k in range(3)]
                flow = [w * d for w, d in zip(wi, step)]
                side = {k: shift_next(x[k]) - x[k] for k in (1, 2)}
                out = {}
                for k in (1, 2):
                    along = wj[k] * side[k]
                    out[k] = flow[k] - flow[k - 1] + along - shift_back(along)
                steps.append(step)
                sides.append(side[own])
                flows.append(flow[1] if bottom else -flow[1])
                laps.append(out)
            y = {k: bases[k] + laps[0][k] for k in (1, 2)}
            cross = fold(steps[1][1] * (y[2] - y[1]) + steps[0][1] * (laps[1][2] - laps[1][1]))
            at = 0 if bottom else 2
            inside = fold(steps[1][at] * flows[0] + steps[0][at] * flows[1])
            inside = inside if bottom else -inside
            beside = fold(sides[1] * (shift_next(flows[0]) - flows[0]) + sides[0] * (shift_next(flows[1]) - flows[1]))
            beside = jnp.where(last_lane, 0.0, beside)
            whole = jnp.sum(cross + inside + beside + shift_back(beside), axis=0, keepdims=True)
            inside = jnp.sum(inside, axis=0, keepdims=True)
            slots = (2, 3) if bottom else (1, 0)
            fix_ref[p, slots[0] : slots[0] + 1, :] = inside
            fix_ref[p, slots[1] : slots[1] + 1, :] = whole
        return carry

    lax.fori_loop(0, panels, row_edges, 0)

    span = 4 * rows
    turn = jnp.where(lane < span, span - 1 - lane, 0)
    back0 = lane_gather(mm_ref[0], turn)
    back1 = lane_gather(mm_ref[1], turn)
    columns = (
        jnp.where(side < 2, em_ref[5], em_ref[4]),
        aa_ref[tiles - 1, 0:CH, :],
        back1,
        aa_ref[0, 0:CH, :],
        jnp.where(side < 2, em_ref[0], back0),
        jnp.where(side < 2, back0, em_ref[0]),
    )
    at_end = lane == LANES - 1
    pad = jnp.zeros((LANES - 8, LANES), F32)
    mirrored = [
        jnp.concatenate([aa_ref[u, CH:, :], pad], axis=0).T[0:CH]
        for u in (jnp.minimum(tiles - place, tiles - 1), jnp.maximum(tiles - 2 - place, 0))
    ]
    ln = lane_iota((layers, LANES))
    k_of, r_of = ln % 4, ln // 4
    end = ln == LANES - 1
    depth_at = CH - 4

    def mixed(x):
        depth = jnp.broadcast_to(x[depth_at : depth_at + 1], (layers, LANES))
        return mix(fwd, x[0:layers]), mix(bwd, x[layers : 2 * layers]), depth

    def turn(x, by):
        return pltpu.roll(x, by % LANES, 1)

    for p in range(panels):
        raw = columns[p]
        if p in (1, 3):
            turned = jnp.concatenate([aa_ref[tiles - 1 if p == 1 else 0, CH:, :], pad], axis=0).T[0:CH]
        outer, inner_own = mixed(raw), mixed(em_ref[p])
        force_outer, force_own = force(raw), force(em_ref[p])
        beyond = []
        for edge in range(2):
            at = 1 + edge
            at_cut = lambda q, block: line[q, at, :, block * LANES : (block + 1) * LANES]
            beside = lambda k: lane_gather(mirrored[edge], jnp.where(at_end, 5 + 2 * k, 4 + 2 * k))
            if p == 0:
                inner = jnp.where(at_end, at_cut(5, blocks - 1), at_cut(4, 0))
            elif p == 2:
                inner = beside(1)
            elif p == 4:
                inner = jnp.where(at_end, at_cut(0, blocks - 1), beside(0))
            elif p == 5:
                inner = jnp.where(at_end, beside(0), at_cut(0, 0))
            else:
                inner = lane_gather(turned, jnp.where(at_end, 2 * edge, 2 * edge + 1))
            own_row = 0 if edge == 0 else rows - 1
            across = turn(raw, 126 - 4 * own_row)
            along = jnp.where(at_end, turn(at_cut(p, 0), LANES - 1), turn(at_cut(p, blocks - 1), 1))
            corner = first if edge == 0 else final
            sideways = mixed(jnp.where(corner, across, inner))
            onward = mixed(jnp.where(corner, along, inner))
            head, tail = (
                (hrp_ref[p, edge, :, cut], hrv_ref[p, edge, :, cut], jnp.broadcast_to(hrb_ref[p, edge : edge + 1, cut], (layers, LANES)))
                for cut in (slice(0, LANES), slice(n - LANES, n))
            )
            base = 4 * own_row
            here = [
                [turn(jnp.where(end, o, h), base + 2) for o, h in zip(onward, head)],
                [turn(jnp.where(end, t, o), base + 2) for o, t in zip(onward, tail)],
            ]
            lateral = [[turn(x, base + 3) for x in sideways], [turn(x, base + 1) for x in sideways]]
            beyond.append((here, lateral))
        total = None
        for right in range(2):
            own_k = 1 if right else 2
            halves = (inner_own, outer) if right else (outer, inner_own)
            q, v, b = (jnp.where(k_of < 2, x, y) for x, y in zip(*halves))
            y0 = jnp.where(k_of < 2, *((force_own, force_outer) if right else (force_outer, force_own)))
            (here_m, lat_m), (here_p, lat_p) = [(h[right], t[right]) for h, t in beyond]
            at_first, at_last, is_own = r_of == 0, r_of == rows - 1, k_of == own_k
            bj = 0.5 * (b + turn(b, -1))
            bi = 0.5 * (b + jnp.where(at_last, here_p[2], turn(b, -4)))
            bi_m = 0.5 * (b + here_m[2])
            laps, di, dj, extra, extra_m, extra_p, di_m = [], [], [], [], [], [], []
            for f, x in enumerate((q, v)):
                step_i = jnp.where(at_last, here_p[f], turn(x, -4)) - x
                step_m = x - here_m[f]
                step_j = turn(x, -1) - x
                flow_i, flow_j = bi * step_i, bj * step_j
                before = jnp.where(at_first, bi_m * step_m, turn(flow_i, 4))
                laps.append(flow_i - before + flow_j - turn(flow_j, 1))
                cross = flow_j if right else -turn(flow_j, 1)
                extra.append(jnp.where(is_own, cross, 0.0))
                extra_m.append(0.5 * (here_m[2] + lat_m[2]) * (lat_m[f] - here_m[f]))
                extra_p.append(0.5 * (here_p[2] + lat_p[2]) * (lat_p[f] - here_p[f]))
                di.append(step_i)
                di_m.append(step_m)
                dj.append(step_j)
            y, z = y0 + laps[0], laps[1]
            cross_edge = fold(dj[1] * (turn(y, -1) - y) + (turn(z, -1) - z) * dj[0])
            after = [jnp.where(at_last, e, turn(x, -4)) for x, e in zip(extra, extra_p)]
            along_i = fold(di[1] * (after[0] - extra[0]) + di[0] * (after[1] - extra[1]))
            along_m = fold(di_m[1] * (extra[0] - extra_m[0]) + di_m[0] * (extra[1] - extra_m[1]))
            if right:
                inside = fold(dj[1] * turn(extra[0], -1) + dj[0] * turn(extra[1], -1))
            else:
                inside = -fold(dj[1] * extra[0] + dj[0] * extra[1])
            k1, r1 = k_of[0:8], r_of[0:8]
            whole = along_i + jnp.where(r1 == 0, along_m, turn(along_i, 4))
            if right:
                whole = whole + cross_edge + turn(inside, 1)
                result = jnp.where(k1 == 1, whole, inside)
            else:
                whole = whole + turn(cross_edge, 1) + inside
                result = jnp.where(k1 == 2, whole, turn(inside, 1))
            if right:
                total = jnp.where(k1 < 2, result, total)
            else:
                total = result
        fix_ref[p, 4:5, 0:LANES] = jnp.sum(total, axis=0, keepdims=True)


def halos(tiles, layers, rows, west, east, *others):
    panels, n = west.shape[0], west.shape[3]
    return pl.pallas_call(
        functools.partial(halo_kernel, tiles, layers, rows),
        out_shape=jax.ShapeDtypeStruct((panels, 8, n), F32),
        scratch_shapes=[
            pltpu.VMEM((panels, 4, CH, n), F32),
            pltpu.VMEM((panels, 2, layers, n), F32),
            pltpu.VMEM((panels, 2, layers, n), F32),
            pltpu.VMEM((panels, 8, n), F32),
        ],
        compiler_params=pltpu.CompilerParams(vmem_limit_bytes=VMEM),
        cost_estimate=pl.CostEstimate(flops=100 * panels * n * layers, bytes_accessed=4 * panels * n * CH * 8, transcendentals=0),
        name="halos",
    )(west, east, *others)


def main_kernel(
    layers, scale,
    p_ref, v_ref, y_ref, b_ref,
    g_ref,
    sp, sv, sy, sz, ip, iv, jp, jv, depth, bi, bj, acc,
):
    rows, n = p_ref.shape[1], p_ref.shape[3]
    halves = layers // 8

    def shift_next(x):
        return pltpu.roll(x, n - 1, 1)

    def shift_back(x):
        return pltpu.roll(x, 1, 1)

    parts = [slice(c * LANES, (c + 1) * LANES) for c in range(n // LANES)]

    depth[...] = jnp.zeros(depth.shape, F32)
    depth[8 : 8 + rows, :] = b_ref[0]
    all_rows = depth[0 : rows + 16, :]
    between_rows = 0.5 * (all_rows + depth[1 : rows + 17, :])
    at = lax.broadcasted_iota(jnp.int32, between_rows.shape, 0)
    between_rows = jnp.where((at >= 8) & (at < 7 + rows), between_rows, 0.0)
    along_rows = 0.5 * (all_rows + shift_next(all_rows))
    along_rows = jnp.where(lane_iota(along_rows.shape) == n - 1, 0.0, along_rows)
    for c, cut in enumerate(parts):
        bi[c] = between_rows[:, cut]
        bj[c] = along_rows[:, cut]

    def spread(ref, at):
        return jnp.concatenate([ref[c, pl.ds(at, 8, stride=0), :] for c in range(len(parts))], axis=1)

    for src, dst in ((p_ref, sp), (v_ref, sv)):
        for slot in (1, rows + 2):
            dst[slot] = jnp.zeros((layers, n), F32)
        for r in range(rows):
            dst[r + 2] = src[0, r]

    def lap(ref, at, bases, outs, by_i, by_j, count):
        for h in range(halves):
            part = slice(8 * h, 8 * h + 8)
            here = ref[at, part]
            before = spread(bi, at + 5) * (here - ref[at - 1, part])
            for u in range(count):
                after_row = ref[at + u + 1, part]
                step_i = after_row - here
                if by_i is not None:
                    by_i[at + u - 1, part] = step_i
                after = spread(bi, at + u + 6) * step_i
                step_j = shift_next(here) - here
                if by_j is not None:
                    by_j[at + u - 2, part] = step_j
                along = spread(bj, at + u + 6) * step_j
                out = after - before + along - shift_back(along)
                if bases is not None:
                    out = out + bases(u, part)
                outs[at + u - 1, part] = out
                here, before = after_row, after

    group = GROUP

    def lap_rows(i, carry):
        r = i * group

        def own_y(u, part):
            return y_ref[0, r + u, part, :]

        lap(sp, r + 2, own_y, sy, ip, jp, group)
        lap(sv, r + 2, None, sz, iv, jv, group)
        return carry

    lax.fori_loop(0, rows // group, lap_rows, 0)
    none = jnp.zeros((layers, n), F32)
    sy[rows + 1], sz[rows + 1], ip[rows], iv[rows] = none, none, none, none

    def between(k):
        total = None
        for h in range(halves):
            part = slice(8 * h, 8 * h + 8)
            term = iv[k, part] * (sy[k + 1, part] - sy[k, part])
            term += ip[k, part] * (sz[k + 1, part] - sz[k, part])
            total = term if total is None else total + term
        return total

    def along_row(r):
        total = None
        for h in range(halves):
            part = slice(8 * h, 8 * h + 8)
            y, z = sy[r + 1, part], sz[r + 1, part]
            term = jv[r, part] * (shift_next(y) - y) + jp[r, part] * (shift_next(z) - z)
            total = term if total is None else total + term
        total = jnp.where(lane_iota(total.shape) == n - 1, 0.0, total)
        return total + shift_back(total)

    def products(i, before):
        r = i * group
        for u in range(group):
            after = between(r + u + 1)
            acc[r + u] = before + after + along_row(r + u)
            before = after
        return before

    lax.fori_loop(0, rows // group, products, jnp.zeros((8, n), F32))

    x = acc[...].reshape(8 * rows, n)
    at_row = lax.broadcasted_iota(jnp.int32, (rows, 8 * rows), 0)
    ones = (lax.broadcasted_iota(jnp.int32, (rows, 8 * rows), 1) // 8 == at_row).astype(F32).astype(jnp.bfloat16)
    hi = x.astype(jnp.bfloat16)
    rest = x - hi.astype(F32)
    lo = rest.astype(jnp.bfloat16)
    total = jnp.dot(ones, hi, preferred_element_type=F32) + jnp.dot(ones, lo, preferred_element_type=F32)
    g_ref[0] = (-0.5 * STEP_FACTOR * STEP_FACTOR * scale) * total


def main(scale, fields, depth):
    count, rows, layers, n = fields[0].shape
    wide = n
    block = lambda x: pl.BlockSpec((1,) + x.shape[1:], lambda p: (p,) + (0,) * (x.ndim - 1))
    operands = [*fields, depth]
    return pl.pallas_call(
        functools.partial(main_kernel, layers, scale),
        grid=(count,),
        in_specs=[block(x) for x in operands],
        out_specs=pl.BlockSpec((1, rows, n), lambda p: (p, 0, 0)),
        out_shape=jax.ShapeDtypeStruct((count, rows, n), F32),
        scratch_shapes=[
            pltpu.VMEM((rows + 4, layers, wide), F32),
            pltpu.VMEM((rows + 4, layers, wide), F32),
            pltpu.VMEM((rows + 2, layers, wide), F32),
            pltpu.VMEM((rows + 2, layers, wide), F32),
            pltpu.VMEM((rows + 1, layers, n), F32),
            pltpu.VMEM((rows + 1, layers, n), F32),
            pltpu.VMEM((rows, layers, wide), F32),
            pltpu.VMEM((rows, layers, wide), F32),
            pltpu.VMEM((rows + 24, wide), F32),
            pltpu.VMEM((wide // LANES, rows + 16, LANES), F32),
            pltpu.VMEM((wide // LANES, rows + 16, LANES), F32),
            pltpu.VMEM((rows, 8, n), F32),
        ],
        compiler_params=pltpu.CompilerParams(vmem_limit_bytes=VMEM),
        cost_estimate=pl.CostEstimate(
            flops=count * rows * layers * wide * 60, bytes_accessed=count * rows * layers * n * 16, transcendentals=0
        ),
        name="main",
    )(*operands)


def finish_kernel(scale, *refs):
    *ins, out_ref = refs
    half = len(ins) // 2
    panels, rows, n = out_ref.shape
    ln, row = lane_iota((rows, LANES)), lax.broadcasted_iota(jnp.int32, (rows, LANES), 0)
    for p in range(panels):
        fix = (-0.5 * STEP_FACTOR * STEP_FACTOR * scale) * sum(x[p] for x in ins[half:])
        out_ref[p] = sum(x[p] for x in ins[:half])
        edges = lane_gather(jnp.broadcast_to(fix[4:5, 0:LANES], (rows, LANES)), (ln + 4 * row + 2) % LANES)
        out_ref[p, :, 0:LANES] += jnp.where(ln < 2, edges, 0.0)
        out_ref[p, :, n - LANES : n] += jnp.where(ln >= LANES - 2, edges, 0.0)
        out_ref[p, 0:2, :] += fix[0:2]
        out_ref[p, rows - 2 : rows, :] += fix[2:4]


def finish(scale, totals, fixes):
    return pl.pallas_call(
        functools.partial(finish_kernel, scale),
        out_shape=jax.ShapeDtypeStruct(totals[0].shape, F32),
        name="finish",
    )(*totals, *fixes)


def body(bathymetry, initial_state, patterns, pattern_index, coupling, final_weights):
    tiles, samples = lax.axis_size("tile"), lax.axis_size("samp")
    layers, _, rows, _ = initial_state.shape
    weights = final_weights[0]
    em, low, high, mm, aa = pack(tiles, initial_state, weights, patterns, bathymetry)
    ring = [(i, (i + 1) % tiles) for i in range(tiles)]
    west = lax.ppermute(high, "tile", ring)
    east = lax.ppermute(low, "tile", [(j, i) for i, j in ring])
    mirrored = lax.ppermute(mm, "tile", [(i, tiles - 1 - i) for i in range(tiles)])
    windows = lax.all_to_all(aa, "tile", 0, 0, tiled=True)
    fields, fwd, bwd, sel = mix_all(initial_state, weights, patterns, coupling, pattern_index)
    total = main(1.0 / samples, fields, bathymetry)
    fix = halos(tiles, layers, rows, west, east, low, high, em, mirrored, windows, fwd, bwd, sel)
    if samples == 2:
        swap = [(0, 1), (1, 0)]
        totals = (total, lax.ppermute(total, "samp", swap))
        fixes = (fix, lax.ppermute(fix, "samp", swap))
    else:
        totals, fixes = (lax.psum(total, "samp"),), (lax.psum(fix, "samp"),)
    return finish(1.0 / samples, totals, fixes)


def solution(mesh):
    in_specs = (
        P(None, "tile", None),
        P(None, None, "tile", None),
        P(None, None, "tile", None),
        P("samp", None),
        P(),
        P("samp", None, None, "tile", None),
    )
    return jax.shard_map(body, mesh=mesh, in_specs=in_specs, out_specs=P(None, "tile", None), check_vma=False)
```

```python
import functools

import jax
import jax.numpy as jnp
from jax import lax
from jax.experimental import pallas as pl
from jax.experimental.pallas import tpu as pltpu
from jax.sharding import PartitionSpec as P


STEP_FACTOR = 0.1
LANES = 128
GROUP = 4
CH = 40
F32 = jnp.float32


def lane_iota(shape):
    return lax.broadcasted_iota(jnp.int32, shape, len(shape) - 1)


def lane_gather(x, idx):
    return jnp.take_along_axis(x, idx, axis=1, mode="promise_in_bounds")


def mix(cat, x):
    hi = x.astype(jnp.bfloat16)
    lo = (x - hi.astype(F32)).astype(jnp.bfloat16)
    return jnp.dot(cat, jnp.concatenate([hi, hi, lo], axis=0), preferred_element_type=F32)


STRIDED = True
VMEM = 60 * 1024 * 1024


def layer_rows(ref, r):
    size, rows = ref.shape[0], ref.shape[2]
    if not STRIDED:
        return ref[:, 0, r, :]
    return ref.reshape(size * rows, LANES)[pl.ds(r, size, stride=rows), :]


def pack_kernel(tiles, blocks, layers, npat, *refs):
    s_refs, w_refs, pat_refs = (refs[k * blocks : (k + 1) * blocks] for k in range(3))
    b_ref, em_ref, lo_ref, hi_ref, mm_ref, aa_ref, aux = refs[3 * blocks :]
    rows = b_ref.shape[1]
    p = pl.program_id(0)
    place = lax.axis_index("tile")
    first, final = place == 0, place == tiles - 1
    aux[...] = jnp.zeros(aux.shape, F32)
    for c in range(blocks):
        aux[c, 0:npat, 0] = pat_refs[c][:, 0].astype(F32)
        aux[c, npat, 0] = b_ref[0, :, c * LANES : (c + 1) * LANES]
    groups = (
        (0, layers, s_refs),
        (layers, layers, w_refs),
        (2 * layers, 8, [aux.at[c] for c in range(blocks)]),
    )
    for at, size, parts in groups:
        for c in range(blocks):
            cut = slice(c * LANES, (c + 1) * LANES)
            for k in range(2):
                lo_ref[0, k, at : at + size, cut] = layer_rows(parts[c], k)
                hi_ref[0, k, at : at + size, cut] = layer_rows(parts[c], rows - 2 + k)

    for at, size, parts in groups:
        shape = (8 * size, LANES)
        ln, row = lane_iota(shape), lax.broadcasted_iota(jnp.int32, shape, 0) % 8
        source = (ln % 4 + LANES - 2) % LANES
        total = jnp.zeros(shape, F32)
        for g in range(rows // 8):
            cut = slice(8 * g, 8 * g + 8)
            head = parts[0][:, 0, cut, :].reshape(shape)
            tail = parts[blocks - 1][:, 0, cut, :].reshape(shape)
            spread = lane_gather(jnp.where(ln < LANES // 2, head, tail), source)
            total = jnp.where(ln // 4 == 8 * g + row, spread, total)
        em_ref[0, at : at + size, :] = jnp.sum(total.reshape(size, 8, LANES), axis=1)

    lane = lane_iota((CH, LANES))
    side = lane % 4
    pad = jnp.zeros((LANES - CH, LANES), F32)

    @pl.when(p == 0)
    def _():
        aa_ref[...] = jnp.zeros(aa_ref.shape, F32)

    @pl.when(p == 1)
    def _():
        aa_ref[tiles - 1, 0:CH, :] = em_ref[0]
        mm_ref[2] = em_ref[0]

    @pl.when(p == 2)
    def _():
        mm_ref[0] = em_ref[0]

    @pl.when(p == 3)
    def _():
        aa_ref[0, 0:CH, :] = em_ref[0]

    @pl.when((p == 3) & jnp.logical_not(first))
    def _():
        mm_ref[2] = em_ref[0]

    @pl.when(p == 4)
    def _():
        mm_ref[1] = em_ref[0]

    per = LANES // rows

    def pole(ref, near, far, backward, is_five):
        for block in range(blocks):
            cut = slice(block * LANES, (block + 1) * LANES)
            x, y = ref[0, near, :, cut], ref[0, far, :, cut]
            turned = jnp.concatenate([x, pad], axis=0).T
            for q in range(per):
                if backward:
                    t = (blocks - 1 - block) * per + q
                    idx = LANES - 1 - q * rows - lane // 4
                else:
                    t = block * per + q
                    idx = q * rows + lane // 4
                idx = jnp.clip(idx, 0, LANES - 1)
                a, b = lane_gather(x, idx), lane_gather(y, idx)
                if is_five:
                    aa_ref[t, 0:CH, :] = jnp.where(side == 1, a, jnp.where(side == 0, b, aa_ref[t, 0:CH, :]))
                else:
                    aa_ref[t, 0:CH, :] = jnp.where(side == 2, a, b)
                low, high = q * rows, (q + 1) * rows - 1
                if backward:
                    before, at_before = tiles - block * per - q, low
                    after, at_after = tiles - 1 - block * per - (q + 1), high
                else:
                    before, at_before = block * per + q + 1, high
                    after, at_after = block * per + q - 1, low
                m = CH if is_five else CH + 1
                if before < tiles:
                    aa_ref[before, m : m + 1, :] = turned[at_before : at_before + 1, :]
                if after >= 0:
                    aa_ref[after, m + 2 : m + 3, :] = turned[at_after : at_after + 1, :]

    for panel in (4, 5):
        @pl.when((p == panel) & first)
        def _(panel=panel):
            pole(lo_ref, 0, 1, panel == 4, panel == 5)

        @pl.when((p == panel) & final)
        def _(panel=panel):
            pole(hi_ref, 1, 0, panel == 5, panel == 5)

    @pl.when(p == 5)
    def _():
        mm_ref[1] = jnp.where(side < 2, mm_ref[1], em_ref[0])
        for k in range(2):
            turned = jnp.concatenate([mm_ref[k], pad], axis=0).T
            m = CH + 4 + 2 * k

            @pl.when(jnp.logical_not(first))
            def _(turned=turned, m=m):
                aa_ref[tiles - place, m : m + 2, :] = turned[1:3, :]

            @pl.when(jnp.logical_not(final))
            def _(turned=turned, m=m):
                at = 4 * (rows - 1) + 1
                aa_ref[tiles - 2 - place, m : m + 2, :] = turned[at : at + 2, :]


def pack(tiles, s, w, pat, b):
    layers, panels, rows, n = s.shape
    npat, blocks = pat.shape[0], n // LANES
    full = lambda *shape: pl.BlockSpec(shape, lambda p: (0,) * len(shape))
    part = lambda size, c: pl.BlockSpec((size, 1, rows, LANES), lambda p: (0, p, 0, c))
    line = pl.BlockSpec((1, 2, CH, n), lambda p: (p, 0, 0, 0))
    return pl.pallas_call(
        functools.partial(pack_kernel, tiles, blocks, layers, npat),
        grid=(panels,),
        in_specs=[part(size, c) for size in (layers, layers, npat) for c in range(blocks)]
        + [pl.BlockSpec((1, rows, n), lambda p: (p, 0, 0))],
        out_specs=[
            pl.BlockSpec((1, CH, LANES), lambda p: (p, 0, 0)),
            line,
            line,
            full(3, CH, LANES),
            full(tiles, CH + 8, LANES),
        ],
        out_shape=[
            jax.ShapeDtypeStruct((panels, CH, LANES), F32),
            jax.ShapeDtypeStruct((panels, 2, CH, n), F32),
            jax.ShapeDtypeStruct((panels, 2, CH, n), F32),
            jax.ShapeDtypeStruct((3, CH, LANES), F32),
            jax.ShapeDtypeStruct((tiles, CH + 8, LANES), F32),
        ],
        scratch_shapes=[pltpu.VMEM((blocks, 8, 1, rows, LANES), F32)],
        compiler_params=pltpu.CompilerParams(vmem_limit_bytes=VMEM),
        name="pack",
    )(*[s] * blocks, *[w] * blocks, *[pat] * blocks, b)


def mix_panel(
    s_ref, w_ref, pat_ref, mat_ref, index_ref,
    sp, sv, ty, fwd_ref, bwd_ref, sel_ref,
    left_s, left_w, left_f, pf,
):
    layers, n = s_ref.shape[0], s_ref.shape[3]
    npat, rows = pat_ref.shape[0], pat_ref.shape[2]
    size = 8 * layers
    half = jnp.bfloat16

    def matrices(_, carry):
        def iotas(shape):
            return (lax.broadcasted_iota(jnp.int32, shape, d) for d in range(2))

        def one(cond):
            return cond.astype(F32).astype(half)

        def product(a, b, flipped=False):
            dims = (((1,), (1 if flipped else 0,)), ((), ()))
            return lax.dot_general(a, b, dims, preferred_element_type=F32).astype(half)

        def spread(matrix, flipped=False):
            i, j = iotas((size, layers))
            x = product(one(i % layers == j), matrix, flipped)
            i, j = iotas((x.shape[1], 8 * x.shape[1]))
            x = jnp.dot(x, one(j // 8 == i), preferred_element_type=F32)
            i, j = iotas(x.shape)
            return jnp.where(i // layers == j % 8, x, 0.0).astype(half)

        i, j = iotas((layers, layers))
        eye = one(i == j)
        mixing = mat_ref[...] + eye.astype(F32)
        high = mixing.astype(half)
        low = (mixing - high.astype(F32)).astype(half)
        q = lax.broadcasted_iota(jnp.int32, (8, layers), 0)
        chosen = one(jnp.broadcast_to(index_ref[...], (8, layers)) == q)
        for k, x in enumerate((spread(high), spread(low), spread((30.0 * eye.astype(F32)).astype(half)))):
            left_s[k * size : (k + 1) * size, :] = jnp.concatenate([x, x], axis=1)
        for k, x in enumerate((spread(high, True), spread(low, True))):
            left_w[k * size : (k + 1) * size, :] = jnp.concatenate([x, x], axis=1)
        left_f[...] = spread(chosen, True)
        high_t, low_t = product(eye, high, True), product(eye, low, True)
        for k, (x, y) in enumerate(((high, high_t), (low, low_t), (high, high_t))):
            fwd_ref[:, k * layers : (k + 1) * layers] = x
            bwd_ref[:, k * layers : (k + 1) * layers] = y
        sel_ref[...] = product(eye, chosen, True)
        return carry

    lax.fori_loop(0, jnp.where(pl.program_id(0) == 0, 1, 0), matrices, 0)

    pf[...] = jnp.zeros(pf.shape, F32)
    pf[0:npat] = pat_ref[:, 0].astype(F32)

    def pieces(x):
        hi = x.astype(jnp.bfloat16)
        return jnp.concatenate([hi, (x - hi.astype(F32)).astype(jnp.bfloat16)], axis=0)

    def dot(a, b):
        return jnp.dot(a, b, preferred_element_type=F32)

    step = min(n, 256)
    for g in range(rows // 8):
        own = slice(8 * g, 8 * g + 8)
        for at in range(0, n, step):
            cut = slice(at, at + step)
            x = dot(left_s[...], pieces(s_ref[:, 0, own, cut].reshape(size, step)))
            f = dot(left_f[...], pf[:, own, cut].reshape(64, step).astype(jnp.bfloat16))
            sp[2 + 8 * g : 10 + 8 * g, :, cut] = (x[0:size] + x[size : 2 * size]).reshape(8, layers, step)
            ty[own, :, cut] = (x[2 * size :] + f).reshape(8, layers, step)
            x = dot(left_w[...], pieces(w_ref[:, 0, own, cut].reshape(size, step)))
            sv[2 + 8 * g : 10 + 8 * g, :, cut] = (x[0:size] + x[size:]).reshape(8, layers, step)


def halo_kernel(
    tiles, layers, rows,
    west_ref, east_ref, low_ref, high_ref, em_ref, mm_ref, aa_ref, fwd_ref, bwd_ref, sel_ref,
    fix_ref,
    line, hrp_ref, hrv_ref, hrb_ref,
):
    panels, n = west_ref.shape[0], west_ref.shape[3]
    place = lax.axis_index("tile")
    first, final = place == 0, place == tiles - 1
    fwd, bwd, sel = fwd_ref[...], bwd_ref[...], sel_ref[...]
    lane = lane_iota((CH, LANES))
    side = lane % 4
    blocks = n // LANES
    per = LANES // rows

    for p in range(panels):
        @pl.when(jnp.logical_not(first))
        def _(p=p):
            line[p, 0:2] = west_ref[p]

        @pl.when(jnp.logical_not(final))
        def _(p=p):
            line[p, 2:4] = east_ref[p]

        if p < 4:
            @pl.when(first)
            def _(p=p):
                line[p, 0:2] = west_ref[(p + 3) % 4]

            @pl.when(final)
            def _(p=p):
                line[p, 2:4] = east_ref[(p + 1) % 4]

    def collect(u_of, dest, k, backward):
        within = lane % rows
        idx = 4 * (rows - 1 - within) + k if backward else 4 * within + k
        p, at = dest
        for block in range(blocks):
            out = jnp.zeros((CH, LANES), F32)
            for q in range(per):
                u = block * per + q
                u = tiles - 1 - u if backward else u
                out = jnp.where(lane // rows == q, lane_gather(u_of(u), idx), out)
            line[p, at, :, block * LANES : (block + 1) * LANES] = out

    @pl.when(first)
    def _():
        def of(u):
            return em_ref[3] if u == 0 else mm_ref[2] if u == tiles - 1 else aa_ref[u, 0:CH, :]

        collect(of, (4, 1), 1, True)
        collect(of, (4, 0), 0, True)
        collect(of, (5, 1), 2, False)
        collect(of, (5, 0), 3, False)

    @pl.when(final)
    def _():
        def of(u):
            return mm_ref[2] if u == 0 else em_ref[1] if u == tiles - 1 else aa_ref[u, 0:CH, :]

        collect(of, (4, 2), 1, False)
        collect(of, (4, 3), 0, False)
        collect(of, (5, 2), 2, True)
        collect(of, (5, 3), 3, True)

    def force(x):
        return (3.0 / STEP_FACTOR) * x[0:layers] + jnp.dot(
            sel, x[2 * layers : CH].astype(jnp.bfloat16), preferred_element_type=F32
        )

    def fold(x):
        return sum(x[k : k + 8] for k in range(0, layers, 8))

    def shift_next(x):
        return pltpu.roll(x, n - 1, 1)

    def shift_back(x):
        return pltpu.roll(x, 1, 1)

    last_lane = lane_iota((1, n)) == n - 1

    def row_edges(p, carry):
        fix_ref[p] = jnp.zeros((8, n), F32)
        for bottom in range(2):
            own = 1 if bottom else 2
            far = 2 if bottom else 1
            lines = (high_ref, line) if bottom else (line, low_ref)
            raw = [lines[0].at[p, 0], lines[0].at[p, 1]]
            raw += [line.at[p, 2], line.at[p, 3]] if bottom else [low_ref.at[p, 0], low_ref.at[p, 1]]
            fields = (
                [mix(fwd, x[0:layers, :]) for x in raw],
                [mix(bwd, x[layers : 2 * layers, :]) for x in raw],
            )
            bases = {k: force(raw[k][...]) for k in (1, 2)}
            depth = [x[CH - 4 : CH - 3, :] for x in raw]
            hrp_ref[p, bottom], hrv_ref[p, bottom] = fields[0][far], fields[1][far]
            hrb_ref[p, bottom : bottom + 1, :] = depth[far]
            wi = [0.5 * (depth[k] + depth[k + 1]) for k in range(3)]
            wj = {k: jnp.where(last_lane, 0.0, 0.5 * (depth[k] + shift_next(depth[k]))) for k in (1, 2)}
            steps, sides, flows, laps = [], [], [], []
            for x in fields:
                step = [x[k + 1] - x[k] for k in range(3)]
                flow = [w * d for w, d in zip(wi, step)]
                side = {k: shift_next(x[k]) - x[k] for k in (1, 2)}
                out = {}
                for k in (1, 2):
                    along = wj[k] * side[k]
                    out[k] = flow[k] - flow[k - 1] + along - shift_back(along)
                steps.append(step)
                sides.append(side[own])
                flows.append(flow[1] if bottom else -flow[1])
                laps.append(out)
            y = {k: bases[k] + laps[0][k] for k in (1, 2)}
            cross = fold(steps[1][1] * (y[2] - y[1]) + steps[0][1] * (laps[1][2] - laps[1][1]))
            at = 0 if bottom else 2
            inside = fold(steps[1][at] * flows[0] + steps[0][at] * flows[1])
            inside = inside if bottom else -inside
            beside = fold(sides[1] * (shift_next(flows[0]) - flows[0]) + sides[0] * (shift_next(flows[1]) - flows[1]))
            beside = jnp.where(last_lane, 0.0, beside)
            whole = jnp.sum(cross + inside + beside + shift_back(beside), axis=0, keepdims=True)
            inside = jnp.sum(inside, axis=0, keepdims=True)
            slots = (2, 3) if bottom else (1, 0)
            fix_ref[p, slots[0] : slots[0] + 1, :] = inside
            fix_ref[p, slots[1] : slots[1] + 1, :] = whole
        return carry

    lax.fori_loop(0, panels, row_edges, 0)

    span = 4 * rows
    turn = jnp.where(lane < span, span - 1 - lane, 0)
    back0 = lane_gather(mm_ref[0], turn)
    back1 = lane_gather(mm_ref[1], turn)
    columns = (
        jnp.where(side < 2, em_ref[5], em_ref[4]),
        aa_ref[tiles - 1, 0:CH, :],
        back1,
        aa_ref[0, 0:CH, :],
        jnp.where(side < 2, em_ref[0], back0),
        jnp.where(side < 2, back0, em_ref[0]),
    )
    at_end = lane == LANES - 1
    pad = jnp.zeros((LANES - 8, LANES), F32)
    mirrored = [
        jnp.concatenate([aa_ref[u, CH:, :], pad], axis=0).T[0:CH]
        for u in (jnp.minimum(tiles - place, tiles - 1), jnp.maximum(tiles - 2 - place, 0))
    ]
    ln = lane_iota((layers, LANES))
    k_of, r_of = ln % 4, ln // 4
    end = ln == LANES - 1
    depth_at = CH - 4

    def mixed(x):
        depth = jnp.broadcast_to(x[depth_at : depth_at + 1], (layers, LANES))
        return mix(fwd, x[0:layers]), mix(bwd, x[layers : 2 * layers]), depth

    def turn(x, by):
        return pltpu.roll(x, by % LANES, 1)

    for p in range(panels):
        raw = columns[p]
        if p in (1, 3):
            turned = jnp.concatenate([aa_ref[tiles - 1 if p == 1 else 0, CH:, :], pad], axis=0).T[0:CH]
        outer, inner_own = mixed(raw), mixed(em_ref[p])
        force_outer, force_own = force(raw), force(em_ref[p])
        beyond = []
        for edge in range(2):
            at = 1 + edge
            at_cut = lambda q, block: line[q, at, :, block * LANES : (block + 1) * LANES]
            beside = lambda k: lane_gather(mirrored[edge], jnp.where(at_end, 5 + 2 * k, 4 + 2 * k))
            if p == 0:
                inner = jnp.where(at_end, at_cut(5, blocks - 1), at_cut(4, 0))
            elif p == 2:
                inner = beside(1)
            elif p == 4:
                inner = jnp.where(at_end, at_cut(0, blocks - 1), beside(0))
            elif p == 5:
                inner = jnp.where(at_end, beside(0), at_cut(0, 0))
            else:
                inner = lane_gather(turned, jnp.where(at_end, 2 * edge, 2 * edge + 1))
            own_row = 0 if edge == 0 else rows - 1
            across = turn(raw, 126 - 4 * own_row)
            along = jnp.where(at_end, turn(at_cut(p, 0), LANES - 1), turn(at_cut(p, blocks - 1), 1))
            corner = first if edge == 0 else final
            sideways = mixed(jnp.where(corner, across, inner))
            onward = mixed(jnp.where(corner, along, inner))
            head, tail = (
                (hrp_ref[p, edge, :, cut], hrv_ref[p, edge, :, cut], jnp.broadcast_to(hrb_ref[p, edge : edge + 1, cut], (layers, LANES)))
                for cut in (slice(0, LANES), slice(n - LANES, n))
            )
            base = 4 * own_row
            here = [
                [turn(jnp.where(end, o, h), base + 2) for o, h in zip(onward, head)],
                [turn(jnp.where(end, t, o), base + 2) for o, t in zip(onward, tail)],
            ]
            lateral = [[turn(x, base + 3) for x in sideways], [turn(x, base + 1) for x in sideways]]
            beyond.append((here, lateral))
        total = None
        for right in range(2):
            own_k = 1 if right else 2
            halves = (inner_own, outer) if right else (outer, inner_own)
            q, v, b = (jnp.where(k_of < 2, x, y) for x, y in zip(*halves))
            y0 = jnp.where(k_of < 2, *((force_own, force_outer) if right else (force_outer, force_own)))
            (here_m, lat_m), (here_p, lat_p) = [(h[right], t[right]) for h, t in beyond]
            at_first, at_last, is_own = r_of == 0, r_of == rows - 1, k_of == own_k
            bj = 0.5 * (b + turn(b, -1))
            bi = 0.5 * (b + jnp.where(at_last, here_p[2], turn(b, -4)))
            bi_m = 0.5 * (b + here_m[2])
            laps, di, dj, extra, extra_m, extra_p, di_m = [], [], [], [], [], [], []
            for f, x in enumerate((q, v)):
                step_i = jnp.where(at_last, here_p[f], turn(x, -4)) - x
                step_m = x - here_m[f]
                step_j = turn(x, -1) - x
                flow_i, flow_j = bi * step_i, bj * step_j
                before = jnp.where(at_first, bi_m * step_m, turn(flow_i, 4))
                laps.append(flow_i - before + flow_j - turn(flow_j, 1))
                cross = flow_j if right else -turn(flow_j, 1)
                extra.append(jnp.where(is_own, cross, 0.0))
                extra_m.append(0.5 * (here_m[2] + lat_m[2]) * (lat_m[f] - here_m[f]))
                extra_p.append(0.5 * (here_p[2] + lat_p[2]) * (lat_p[f] - here_p[f]))
                di.append(step_i)
                di_m.append(step_m)
                dj.append(step_j)
            y, z = y0 + laps[0], laps[1]
            cross_edge = fold(dj[1] * (turn(y, -1) - y) + (turn(z, -1) - z) * dj[0])
            after = [jnp.where(at_last, e, turn(x, -4)) for x, e in zip(extra, extra_p)]
            along_i = fold(di[1] * (after[0] - extra[0]) + di[0] * (after[1] - extra[1]))
            along_m = fold(di_m[1] * (extra[0] - extra_m[0]) + di_m[0] * (extra[1] - extra_m[1]))
            if right:
                inside = fold(dj[1] * turn(extra[0], -1) + dj[0] * turn(extra[1], -1))
            else:
                inside = -fold(dj[1] * extra[0] + dj[0] * extra[1])
            k1, r1 = k_of[0:8], r_of[0:8]
            whole = along_i + jnp.where(r1 == 0, along_m, turn(along_i, 4))
            if right:
                whole = whole + cross_edge + turn(inside, 1)
                result = jnp.where(k1 == 1, whole, inside)
            else:
                whole = whole + turn(cross_edge, 1) + inside
                result = jnp.where(k1 == 2, whole, turn(inside, 1))
            if right:
                total = jnp.where(k1 < 2, result, total)
            else:
                total = result
        fix_ref[p, 4:5, 0:LANES] = jnp.sum(total, axis=0, keepdims=True)


def halos(tiles, layers, rows, west, east, *others):
    panels, n = west.shape[0], west.shape[3]
    return pl.pallas_call(
        functools.partial(halo_kernel, tiles, layers, rows),
        out_shape=jax.ShapeDtypeStruct((panels, 8, n), F32),
        scratch_shapes=[
            pltpu.VMEM((panels, 4, CH, n), F32),
            pltpu.VMEM((panels, 2, layers, n), F32),
            pltpu.VMEM((panels, 2, layers, n), F32),
            pltpu.VMEM((panels, 8, n), F32),
        ],
        compiler_params=pltpu.CompilerParams(vmem_limit_bytes=VMEM),
        cost_estimate=pl.CostEstimate(flops=100 * panels * n * layers, bytes_accessed=4 * panels * n * CH * 8, transcendentals=0),
        name="halos",
    )(west, east, *others)


def main_kernel(
    scale,
    s_ref, w_ref, pat_ref, mat_ref, index_ref, b_ref,
    g_ref, fwd_ref, bwd_ref, sel_ref,
    left_s, left_w, left_f, pf, ty, sp, sv, sy, sz, ip, iv, jp, jv, depth, bi, bj, acc,
):
    layers, rows, n = s_ref.shape[0], s_ref.shape[2], s_ref.shape[3]
    mix_panel(
        s_ref, w_ref, pat_ref, mat_ref, index_ref, sp, sv, ty, fwd_ref, bwd_ref, sel_ref, left_s, left_w, left_f, pf
    )
    halves = layers // 8

    def shift_next(x):
        return pltpu.roll(x, n - 1, 1)

    def shift_back(x):
        return pltpu.roll(x, 1, 1)

    parts = [slice(c * LANES, (c + 1) * LANES) for c in range(n // LANES)]

    depth[...] = jnp.zeros(depth.shape, F32)
    depth[8 : 8 + rows, :] = b_ref[0]
    all_rows = depth[0 : rows + 16, :]
    between_rows = 0.5 * (all_rows + depth[1 : rows + 17, :])
    at = lax.broadcasted_iota(jnp.int32, between_rows.shape, 0)
    between_rows = jnp.where((at >= 8) & (at < 7 + rows), between_rows, 0.0)
    along_rows = 0.5 * (all_rows + shift_next(all_rows))
    along_rows = jnp.where(lane_iota(along_rows.shape) == n - 1, 0.0, along_rows)
    for c, cut in enumerate(parts):
        bi[c] = between_rows[:, cut]
        bj[c] = along_rows[:, cut]

    def spread(ref, at):
        return jnp.concatenate([ref[c, pl.ds(at, 8, stride=0), :] for c in range(len(parts))], axis=1)

    for dst in (sp, sv):
        for slot in (1, rows + 2):
            dst[slot] = jnp.zeros((layers, n), F32)

    def lap(ref, at, bases, outs, by_i, by_j, count):
        for h in range(halves):
            part = slice(8 * h, 8 * h + 8)
            here = ref[at, part]
            before = spread(bi, at + 5) * (here - ref[at - 1, part])
            for u in range(count):
                after_row = ref[at + u + 1, part]
                step_i = after_row - here
                if by_i is not None:
                    by_i[at + u - 1, part] = step_i
                after = spread(bi, at + u + 6) * step_i
                step_j = shift_next(here) - here
                if by_j is not None:
                    by_j[at + u - 2, part] = step_j
                along = spread(bj, at + u + 6) * step_j
                out = after - before + along - shift_back(along)
                if bases is not None:
                    out = out + bases(u, part)
                outs[at + u - 1, part] = out
                here, before = after_row, after

    group = GROUP

    def lap_rows(i, carry):
        r = i * group

        def own_y(u, part):
            return ty[r + u, part]

        lap(sp, r + 2, own_y, sy, ip, jp, group)
        lap(sv, r + 2, None, sz, iv, jv, group)
        return carry

    lax.fori_loop(0, rows // group, lap_rows, 0)
    none = jnp.zeros((layers, n), F32)
    sy[rows + 1], sz[rows + 1], ip[rows], iv[rows] = none, none, none, none

    def between(k):
        total = None
        for h in range(halves):
            part = slice(8 * h, 8 * h + 8)
            term = iv[k, part] * (sy[k + 1, part] - sy[k, part])
            term += ip[k, part] * (sz[k + 1, part] - sz[k, part])
            total = term if total is None else total + term
        return total

    def along_row(r):
        total = None
        for h in range(halves):
            part = slice(8 * h, 8 * h + 8)
            y, z = sy[r + 1, part], sz[r + 1, part]
            term = jv[r, part] * (shift_next(y) - y) + jp[r, part] * (shift_next(z) - z)
            total = term if total is None else total + term
        total = jnp.where(lane_iota(total.shape) == n - 1, 0.0, total)
        return total + shift_back(total)

    def products(i, before):
        r = i * group
        for u in range(group):
            after = between(r + u + 1)
            acc[r + u] = before + after + along_row(r + u)
            before = after
        return before

    lax.fori_loop(0, rows // group, products, jnp.zeros((8, n), F32))

    x = acc[...].reshape(8 * rows, n)
    at_row = lax.broadcasted_iota(jnp.int32, (rows, 8 * rows), 0)
    ones = (lax.broadcasted_iota(jnp.int32, (rows, 8 * rows), 1) // 8 == at_row).astype(F32).astype(jnp.bfloat16)
    hi = x.astype(jnp.bfloat16)
    rest = x - hi.astype(F32)
    lo = rest.astype(jnp.bfloat16)
    total = jnp.dot(ones, hi, preferred_element_type=F32) + jnp.dot(ones, lo, preferred_element_type=F32)
    g_ref[0] = (-0.5 * STEP_FACTOR * STEP_FACTOR * scale) * total


def main(scale, s, w, pat, matrix, index, depth):
    layers, panels, rows, n = s.shape
    npat, size = pat.shape[0], 8 * layers
    part = lambda count: pl.BlockSpec((count, 1, rows, n), lambda p: (0, p, 0, 0))
    full = lambda *shape: pl.BlockSpec(shape, lambda p: (0, 0))
    plane = pl.BlockSpec((1, rows, n), lambda p: (p, 0, 0))
    small = [(layers, 3 * layers), (layers, 3 * layers), (layers, 8)]
    field = lambda count: pltpu.VMEM((count, layers, n), F32)
    return pl.pallas_call(
        functools.partial(main_kernel, scale),
        grid=(panels,),
        in_specs=[part(layers), part(layers), part(npat), full(layers, layers), full(1, layers), plane],
        out_specs=[plane] + [full(*x) for x in small],
        out_shape=[jax.ShapeDtypeStruct((panels, rows, n), F32)]
        + [jax.ShapeDtypeStruct(x, jnp.bfloat16) for x in small],
        scratch_shapes=[
            pltpu.VMEM((3 * size, 2 * size), jnp.bfloat16),
            pltpu.VMEM((2 * size, 2 * size), jnp.bfloat16),
            pltpu.VMEM((size, 64), jnp.bfloat16),
            pltpu.VMEM((8, rows, n), F32),
            field(rows),
            field(rows + 4), field(rows + 4),
            field(rows + 2), field(rows + 2),
            field(rows + 1), field(rows + 1),
            field(rows), field(rows),
            pltpu.VMEM((rows + 24, n), F32),
            pltpu.VMEM((n // LANES, rows + 16, LANES), F32),
            pltpu.VMEM((n // LANES, rows + 16, LANES), F32),
            pltpu.VMEM((rows, 8, n), F32),
        ],
        compiler_params=pltpu.CompilerParams(vmem_limit_bytes=VMEM),
        cost_estimate=pl.CostEstimate(
            flops=panels * rows * layers * n * 120, bytes_accessed=panels * rows * layers * n * 10, transcendentals=0
        ),
        name="main",
    )(s, w, pat, matrix, index, depth)


def finish_kernel(scale, *refs):
    *ins, out_ref = refs
    half = len(ins) // 2
    panels, rows, n = out_ref.shape
    ln, row = lane_iota((rows, LANES)), lax.broadcasted_iota(jnp.int32, (rows, LANES), 0)
    for p in range(panels):
        fix = (-0.5 * STEP_FACTOR * STEP_FACTOR * scale) * sum(x[p] for x in ins[half:])
        out_ref[p] = sum(x[p] for x in ins[:half])
        edges = lane_gather(jnp.broadcast_to(fix[4:5, 0:LANES], (rows, LANES)), (ln + 4 * row + 2) % LANES)
        out_ref[p, :, 0:LANES] += jnp.where(ln < 2, edges, 0.0)
        out_ref[p, :, n - LANES : n] += jnp.where(ln >= LANES - 2, edges, 0.0)
        out_ref[p, 0:2, :] += fix[0:2]
        out_ref[p, rows - 2 : rows, :] += fix[2:4]


def finish(scale, totals, fixes):
    return pl.pallas_call(
        functools.partial(finish_kernel, scale),
        out_shape=jax.ShapeDtypeStruct(totals[0].shape, F32),
        name="finish",
    )(*totals, *fixes)


def body(bathymetry, initial_state, patterns, pattern_index, coupling, final_weights):
    tiles, samples = lax.axis_size("tile"), lax.axis_size("samp")
    layers, _, rows, _ = initial_state.shape
    weights = final_weights[0]
    em, low, high, mm, aa = pack(tiles, initial_state, weights, patterns, bathymetry)
    ring = [(i, (i + 1) % tiles) for i in range(tiles)]
    west = lax.ppermute(high, "tile", ring)
    east = lax.ppermute(low, "tile", [(j, i) for i, j in ring])
    mirrored = lax.ppermute(mm, "tile", [(i, tiles - 1 - i) for i in range(tiles)])
    windows = lax.all_to_all(aa, "tile", 0, 0, tiled=True)
    total, fwd, bwd, sel = main(1.0 / samples, initial_state, weights, patterns, coupling, pattern_index, bathymetry)
    fix = halos(tiles, layers, rows, west, east, low, high, em, mirrored, windows, fwd, bwd, sel)
    if samples == 2:
        swap = [(0, 1), (1, 0)]
        totals = (total, lax.ppermute(total, "samp", swap))
        fixes = (fix, lax.ppermute(fix, "samp", swap))
    else:
        totals, fixes = (lax.psum(total, "samp"),), (lax.psum(fix, "samp"),)
    return finish(1.0 / samples, totals, fixes)


def solution(mesh):
    in_specs = (
        P(None, "tile", None),
        P(None, None, "tile", None),
        P(None, None, "tile", None),
        P("samp", None),
        P(),
        P("samp", None, None, "tile", None),
    )
    return jax.shard_map(body, mesh=mesh, in_specs=in_specs, out_specs=P(None, "tile", None), check_vma=False)
```
